128 devices in a mesh: chan: 8 (over y_hi, z), frame: 16 (over x, y_lo, core).
Axes of the slice: x: 4, y: 4 (y_hi: 2, y_lo: 2; y = y_hi * 2 + y_lo), z: 4, core: 2. Of those that a mesh axis runs over, the one named last changes fastest.
Arguments:
- rf_data: bfloat16 [2, 8, 256, 1024], P(None, None, 'frame', 'chan'), may hold values from -6 to 6
- elem_pos: int32 [3, 1024], replicated, may hold values from -16 to 15, as said below
- vox_pos: int32 [3, 16384], P(None, 'chan'), may hold values from -32 to 62, as said below
- subbands: int32 [8], replicated, may hold values from 0 to 63, as said below
Outputs:
- filtered: bfloat16 [256, 2, 8, 16384], P('frame', None, None, 'chan')
The draws below stay inside these ranges and needn't reach their ends.
Inputs may be any that keep to these rules, and one draw needn't show every extreme that they name: `elem_pos`: the element positions are the 32 x 32 grid with x and y from -16, each point once in a drawn order; z is 0, 1 or 2. `vox_pos`: distinct voxels of a box: x and y from -32 to 31, z from 48 to 62 in steps of 2. `subbands`: 8 distinct bin numbers.
All inputs are finite; a program needn't handle non-finite values.
Results may differ from the reference program's by a relative error of at most 0.0075.
Values may be sent and summed in bfloat16 or wider, within the bound.
No kernel may reach another device: no remote copies, remote signals or barrier semaphores. Data moves between devices by JAX's collectives and lax.ppermute only.
A program may use at most 128 MiB of HBM per device.

```python
import math
import jax
import jax.numpy as jnp
from jax import lax

SIDE = 32
C = 1024
F = 256
B = 8
V = 16384


def draw_elem_pos(key, part):
    order = jax.random.permutation(jax.random.fold_in(key, 11), SIDE * SIDE).astype(jnp.int32)
    pos_x = order % SIDE - SIDE // 2
    pos_y = order // SIDE - SIDE // 2
    pos_z = jax.random.randint(jax.random.fold_in(key, 12), (SIDE * SIDE,), 0, 3).astype(jnp.int32)
    return jnp.stack([pos_x, pos_y, pos_z], axis=0).astype(jnp.int32)


def draw_vox_pos(key, part):
    middle = (jax.random.permutation(jax.random.fold_in(key, 21), 32766)[:V - 2] + 1).astype(jnp.int32)
    ends = jnp.array([0, 32767], dtype=jnp.int32)
    joined = jnp.concatenate([ends, middle]).astype(jnp.int32)
    chosen = jax.random.permutation(jax.random.fold_in(key, 22), joined).astype(jnp.int32)
    pos_x = chosen % 64 - 32
    pos_y = chosen // 64 % 64 - 32
    pos_z = 48 + 2 * (chosen // 4096)
    return jnp.stack([pos_x, pos_y, pos_z], axis=0).astype(jnp.int32)


def draw_subbands(key, part):
    middle = (jax.random.permutation(jax.random.fold_in(key, 31), 62)[:B - 2] + 1).astype(jnp.int32)
    ends = jnp.array([0, 63], dtype=jnp.int32)
    joined = jnp.concatenate([ends, middle]).astype(jnp.int32)
    return jax.random.permutation(jax.random.fold_in(key, 32), joined).astype(jnp.int32)


def block_scale(rng, dims, pieces, low, largest):
    level = 1.0
    for position, shards_of in pieces:
        draws = jax.random.uniform(jax.random.fold_in(jax.random.fold_in(rng, 6), position), (shards_of,), jnp.float32, low / len(pieces), largest / len(pieces))
        level = level * jnp.repeat(jnp.exp(draws), dims[position] // shards_of).reshape((-1,) + (1,) * (len(dims) - 1 - position))
    return level


def scatter_about(key, dims, width, bound, split=(), held_as=jnp.bfloat16):
    entries = jax.random.normal(key, dims, jnp.float32) * width
    if len(split) > 0:
        entries = block_scale(key, dims, split, -0.22, 0.18) * entries
    return jnp.clip(entries, min=-bound, max=bound).astype(held_as)


def setup_inputs(seed: int = 0) -> dict:
    splits = jax.random.split(jax.random.key(seed), 5)
    rf_data = scatter_about(splits[0], (2, B, F, C), 1.0, 6.0, ((2, 16), (3, 8)))
    elem_pos = draw_elem_pos(jax.random.fold_in(splits[4], 71), 0)
    vox_pos = draw_vox_pos(jax.random.fold_in(splits[4], 71), 0)
    subbands = draw_subbands(jax.random.fold_in(splits[4], 71), 0)
    return dict(rf_data=rf_data, elem_pos=elem_pos, vox_pos=vox_pos, subbands=subbands)


TWO_PI = 2.0 * math.pi
EPSILON = 1e-06

def geometry(elem_pos, vox_pos):
    elem = elem_pos.astype(jnp.float32)
    voxel = vox_pos.astype(jnp.float32)
    delta_x = voxel[0][:, None] - elem[0][None, :]
    delta_y = voxel[1][:, None] - elem[1][None, :]
    delta_z = voxel[2][:, None] - elem[2][None, :]
    distance = jnp.sqrt(delta_x * delta_x + delta_y * delta_y + delta_z * delta_z)
    inverse = 1.0 / math.sqrt(elem_pos.shape[1])
    weight = delta_z / distance * inverse
    travel = voxel[2][:, None] + distance
    return (weight, travel)

def data_matrix(rf_data):
    data_re = jnp.swapaxes(rf_data[0], 1, 2)
    data_im = jnp.swapaxes(rf_data[1], 1, 2)
    upper_rows = jnp.concatenate([data_re, data_im], axis=2)
    lower_rows = jnp.concatenate([-data_im, data_re], axis=2)
    return jnp.concatenate([upper_rows, lower_rows], axis=1)

def complex_product(left_pair, right_pair):
    first_re, first_im = left_pair
    second_re, second_im = right_pair
    high = lax.Precision.HIGHEST
    real_part = jnp.einsum('bij,bjk->bik', first_re, second_re, precision=high) - jnp.einsum('bij,bjk->bik', first_im, second_im, precision=high)
    imag_part = jnp.einsum('bij,bjk->bik', first_re, second_im, precision=high) + jnp.einsum('bij,bjk->bik', first_im, second_re, precision=high)
    return (real_part, imag_part)

def filter_matrix(gram):
    gram_re = gram[:, 0]
    gram_im = gram[:, 1]
    frames = gram.shape[2]
    squares = lax.optimization_barrier(jnp.sum(gram_re * gram_re + gram_im * gram_im, axis=(1, 2)))
    factor = 4.0 / jnp.sqrt(squares + EPSILON)
    mat_re = gram_re * factor[:, None, None]
    mat_im = gram_im * factor[:, None, None]
    second = complex_product((mat_re, mat_im), (mat_re, mat_im))
    third = complex_product(second, (mat_re, mat_im))
    identity = jnp.eye(frames, dtype=jnp.float32)[None]
    filter_re = identity - mat_re + 0.3 * second[0] - 0.03 * third[0]
    filter_im = -mat_im + 0.3 * second[1] - 0.03 * third[1]
    return jnp.stack([filter_re, filter_im], axis=1).astype(jnp.bfloat16)

def block_filter(filter_bf):
    filter_re = filter_bf[:, 0]
    filter_im = filter_bf[:, 1]
    upper_rows = jnp.concatenate([filter_re, filter_im], axis=2)
    lower_rows = jnp.concatenate([-filter_im, filter_re], axis=2)
    return jnp.concatenate([upper_rows, lower_rows], axis=1)

def reference(rf_data, elem_pos, vox_pos, subbands):
    weight, travel = geometry(elem_pos, vox_pos)
    wavenum = (32.0 + subbands.astype(jnp.float32)) / 64.0
    matrix = data_matrix(rf_data)

    def one_bin(index):
        phase_angle = TWO_PI * wavenum[index] * travel
        operator = jnp.concatenate([weight * jnp.cos(phase_angle), -(weight * jnp.sin(phase_angle))], axis=1).astype(jnp.bfloat16)
        return jnp.dot(operator, matrix[index], preferred_element_type=jnp.float32).astype(jnp.bfloat16)
    volumes = lax.map(one_bin, jnp.arange(B, dtype=jnp.int32))
    stacked = jnp.swapaxes(volumes, 0, 1).astype(jnp.float32)
    products = jnp.einsum('vbi,vbj->bij', stacked, stacked, precision=lax.Precision.HIGHEST)
    gram_re = products[:, :F, :F] + products[:, F:, F:]
    gram_im = products[:, :F, F:] - products[:, F:, :F]
    gram = jnp.stack([gram_re, gram_im], axis=1)
    filter_bf = filter_matrix(gram)
    blocks = block_filter(filter_bf).astype(jnp.float32)
    applied = jnp.einsum('vbi,bij->vbj', stacked, blocks, precision=lax.Precision.HIGHEST).astype(jnp.bfloat16)
    applied = applied.reshape(applied.shape[0], B, 2, F)
    return jnp.transpose(applied, (3, 2, 1, 0))
```

```python
import math

import jax
import jax.numpy as jnp
from jax import lax
from jax.experimental import pallas as pl
from jax.experimental.pallas import tpu as pltpu
from jax.sharding import Mesh, PartitionSpec as P

EPSILON = 1e-06
BINS = 8
CORES = 2
F32 = jnp.float32
BF16 = jnp.bfloat16
SIN = (3.1415925800446924, -5.167706878924515, 2.5500313772531213, -0.5980451739748806, 0.0772201286897368)
COS = (0.9999999534666272, -4.934792858670076, 4.058411914063177, -1.331880160583308, 0.21969679727234584)
ROWS = 32
LANES = 256
WIDE = pltpu.CompilerParams(vmem_limit_bytes=48 * 1024 * 1024)


def horner(coefficients, z):
    total = jnp.full_like(z, coefficients[-1])
    for value in coefficients[-2::-1]:
        total = total * z + value
    return total


def operator_tile(columns, voxel, wavenumber, scale):
    delta_x = voxel[0] - columns[0]
    delta_y = voxel[1] - columns[1]
    delta_z = voxel[2] - columns[2]
    squared = delta_x * delta_x + delta_y * delta_y + delta_z * delta_z
    inverse = lax.rsqrt(squared)
    turns = (voxel[2] + squared * inverse) * wavenumber
    part = turns - jnp.round(turns)
    z = part * part
    sine = part * horner(SIN, z)
    cosine = horner(COS, z)
    double = delta_z * inverse * (2.0 * scale)
    lean = double * sine
    return 0.5 * double - lean * sine, lean * cosine


def beam_kernel(elem, vox, subbands, own, other, y_ref, keep_ref, send_ref, data, cosines, sines, places, gram):
    core = lax.axis_index("core")
    channels = elem.shape[1]
    frames = y_ref.shape[0] // 2
    half = frames // CORES
    voxels = y_ref.shape[1]
    here = pl.multiple_of(core * half, half)
    there = pl.multiple_of((1 - core) * half, half)
    blocks = own.shape[0]
    width = own.shape[-1]
    for k in range(blocks):
        for part in range(2):
            lanes = slice(k * width, (k + 1) * width)
            data[pl.ds(part * frames + here, half), lanes] = own[k, :, part].reshape(half, width)
            data[pl.ds(part * frames + there, half), lanes] = other[k, :, part].reshape(half, width)
    wavenumber = (32.0 + subbands[lax.axis_index("bin")].astype(F32)) / 64.0
    scale = 1.0 / math.sqrt(channels)
    stacked = elem[...].astype(F32)
    padded = jnp.concatenate([stacked, jnp.zeros((5, channels), F32)], axis=0)
    places[...] = jnp.transpose(padded)
    for block in range(voxels // LANES):
        lanes = slice(block * LANES, (block + 1) * LANES)
        at = pl.multiple_of(core * voxels + block * LANES, LANES)
        voxel = [vox[d : d + 1, pl.ds(at, LANES)].astype(F32) for d in range(3)]

        def tile(index, carry, voxel=voxel, lanes=lanes):
            rows = pl.ds(pl.multiple_of(index * ROWS, ROWS), ROWS)
            columns = [places[rows, d : d + 1] for d in range(3)]
            real, imag = operator_tile(columns, voxel, wavenumber, scale)
            cosines[rows, lanes] = real.astype(BF16)
            sines[rows, lanes] = imag.astype(BF16)
            return carry

        lax.fori_loop(0, channels // ROWS, tile, 0)
        first = jnp.dot(data[...], cosines[:, lanes], preferred_element_type=F32)
        second = jnp.dot(data[...], sines[:, lanes], preferred_element_type=F32)
        y_ref[:frames, lanes] = (first[:frames] + second[frames:]).astype(BF16)
        y_ref[frames:, lanes] = (first[frames:] - second[:frames]).astype(BF16)
    y = y_ref[...]
    products = lax.dot_general(y, y, (((1,), (1,)), ((), ())), preferred_element_type=F32)
    gram[...] = (products[:frames, :frames] + products[frames:, frames:]) + (
        products[:frames, frames:] - products[frames:, :frames]
    )
    keep_ref[...] = gram[pl.ds(here, half), :]
    send_ref[...] = gram[pl.ds(there, half), :]


def complex_product(left, right):
    def dot(a, b):
        return jnp.dot(a, b, preferred_element_type=F32, precision=lax.Precision.HIGHEST)

    return (
        dot(left[0], right[0]) - dot(left[1], right[1]),
        dot(left[0], right[1]) + dot(left[1], right[0]),
    )


def filter_kernel(own, other, y_ref, out_ref, gram):
    core = lax.axis_index("core")
    half, frames = own.shape
    gram[pl.ds(pl.multiple_of(core * half, half), half), :] = own[...]
    gram[pl.ds(pl.multiple_of((1 - core) * half, half), half), :] = other[...]
    both = gram[...]
    flipped = jnp.transpose(both)
    gram_re = 0.5 * (both + flipped)
    gram_im = 0.5 * (both - flipped)
    squares = jnp.sum(gram_re * gram_re + gram_im * gram_im)
    factor = 4.0 / jnp.sqrt(jnp.full((1, 1), squares + EPSILON, F32))
    mat = (gram_re * factor, gram_im * factor)
    second = complex_product(mat, mat)
    third = complex_product(second, mat)
    rows = lax.broadcasted_iota(jnp.int32, (frames, frames), 0)
    cols = lax.broadcasted_iota(jnp.int32, (frames, frames), 1)
    identity = jnp.where(rows == cols, 1.0, 0.0).astype(F32)
    real = (identity - mat[0] + 0.3 * second[0] - 0.03 * third[0]).astype(BF16)
    imag = (-mat[1] + 0.3 * second[1] - 0.03 * third[1]).astype(BF16)
    matrix = jnp.concatenate(
        [jnp.concatenate([real, imag], axis=1), jnp.concatenate([-imag, real], axis=1)], axis=0
    )
    applied = jnp.dot(matrix, y_ref[...], preferred_element_type=F32).astype(BF16)
    group = out_ref.shape[2]
    bins = out_ref.shape[0] // CORES
    for part in range(2):
        for c in range(CORES):
            for j in range(bins):
                row = part * frames + c * half + j * group
                out_ref[j * CORES + c, part] = applied[row : row + group]


def place_kernel(got, out_ref):
    group, _, bins, _ = out_ref.shape
    voxels = got.shape[-1]
    size = group * bins
    rows = lax.broadcasted_iota(jnp.int32, (size, size), 0)
    cols = lax.broadcasted_iota(jnp.int32, (size, size), 1)
    turn = jnp.where(cols == (rows % bins) * group + rows // bins, 1.0, 0.0).astype(BF16)
    for c in range(CORES):
        for part in range(2):
            block = got[:, c, part].reshape(size, voxels)
            moved = jnp.dot(turn, block, preferred_element_type=F32).astype(BF16)
            out_ref[:, part, :, c * voxels : (c + 1) * voxels] = moved.reshape(group, bins, voxels)


def shards(rf_data, elem_pos, vox_pos, subbands):
    parts, bins, group, width = rf_data.shape
    chans = elem_pos.shape[1] // width
    voxels = vox_pos.shape[1] // CORES
    frames = group * bins * CORES
    half = frames // CORES
    swap = [(0, 1), (1, 0)]
    vmem = pl.BlockSpec(memory_space=pltpu.VMEM)
    smem = pl.BlockSpec(memory_space=pltpu.SMEM)

    by_bin = jnp.broadcast_to(jnp.swapaxes(rf_data, 0, 1)[None], (chans, bins, parts, group, width))
    by_bin = by_bin.reshape(chans * bins, parts, group, width)
    own = lax.all_to_all(by_bin, ("chan", "bin"), split_axis=0, concat_axis=0, tiled=True)
    other = lax.ppermute(own, "core", swap)
    own = own.reshape(chans, bins, parts, group, width)
    other = other.reshape(chans, bins, parts, group, width)

    y, keep, send = pl.pallas_call(
        beam_kernel,
        name="beam",
        out_shape=(
            jax.ShapeDtypeStruct((2 * frames, voxels), BF16),
            jax.ShapeDtypeStruct((half, frames), F32),
            jax.ShapeDtypeStruct((half, frames), F32),
        ),
        in_specs=[vmem, vmem, smem, vmem, vmem],
        out_specs=(vmem, vmem, vmem),
        scratch_shapes=[
            pltpu.VMEM((2 * frames, chans * width), BF16),
            pltpu.VMEM((chans * width, voxels), BF16),
            pltpu.VMEM((chans * width, voxels), BF16),
            pltpu.VMEM((chans * width, 8), F32),
            pltpu.VMEM((frames, frames), F32),
        ],
        compiler_params=WIDE,
    )(elem_pos, vox_pos, subbands, own, other)

    total = keep + lax.ppermute(send, "core", swap)
    step = 1
    while step < chans:
        total = total + lax.ppermute(total, "chan", [(a, a ^ step) for a in range(chans)])
        step *= 2
    rest = lax.ppermute(total, "core", swap)

    applied = pl.pallas_call(
        filter_kernel,
        name="filter",
        out_shape=jax.ShapeDtypeStruct((bins * CORES, parts, group, voxels), BF16),
        in_specs=[vmem, vmem, vmem],
        out_specs=vmem,
        scratch_shapes=[pltpu.VMEM((frames, frames), F32)],
        compiler_params=WIDE,
    )(total, rest, y)

    got = lax.all_to_all(applied, ("bin", "core"), split_axis=0, concat_axis=0, tiled=True)
    got = got.reshape(bins, CORES, parts, group, voxels)
    return pl.pallas_call(
        place_kernel,
        name="place",
        out_shape=jax.ShapeDtypeStruct((group, parts, bins, CORES * voxels), BF16),
        in_specs=[vmem],
        out_specs=vmem,
        compiler_params=WIDE,
    )(got)


def solution(mesh):
    chans = mesh.shape["chan"]
    fine = Mesh(mesh.devices.reshape(chans, BINS, CORES), ("chan", "bin", "core"))
    return jax.shard_map(
        shards,
        mesh=fine,
        in_specs=(P(None, None, ("bin", "core"), "chan"), P(), P(None, "chan"), P()),
        out_specs=P(("bin", "core"), None, None, "chan"),
        check_vma=False,
    )
```

```python
import math

import jax
import jax.numpy as jnp
from jax import lax
from jax.experimental import pallas as pl
from jax.experimental.pallas import tpu as pltpu
from jax.sharding import Mesh, PartitionSpec as P

EPSILON = 1e-06
BINS = 8
CORES = 2
F32 = jnp.float32
BF16 = jnp.bfloat16
SIN = (3.1415925800446924, -5.167706878924515, 2.5500313772531213, -0.5980451739748806, 0.0772201286897368)
COS = (0.9999999534666272, -4.934792858670076, 4.058411914063177, -1.331880160583308, 0.21969679727234584)
ROWS = 32
LANES = 256
WIDE = pltpu.CompilerParams(vmem_limit_bytes=48 * 1024 * 1024)


def horner(coefficients, z):
    total = jnp.full_like(z, coefficients[-1])
    for value in coefficients[-2::-1]:
        total = total * z + value
    return total


def operator_tile(columns, voxel, wavenumber, scale):
    delta_x = voxel[0] - columns[0]
    delta_y = voxel[1] - columns[1]
    delta_z = voxel[2] - columns[2]
    squared = delta_x * delta_x + delta_y * delta_y + delta_z * delta_z
    inverse = lax.rsqrt(squared)
    turns = (voxel[2] + squared * inverse) * wavenumber
    part = turns - jnp.round(turns)
    z = part * part
    sine = part * horner(SIN, z)
    cosine = horner(COS, z)
    double = delta_z * inverse * (2.0 * scale)
    lean = double * sine
    return 0.5 * double - lean * sine, lean * cosine


def operator_kernel(elem, vox, subbands, cosines, sines, places):
    core = lax.axis_index("core")
    channels, voxels = cosines.shape
    wavenumber = (32.0 + subbands[lax.axis_index("bin")].astype(F32)) / 64.0
    scale = 1.0 / math.sqrt(channels)
    stacked = elem[...].astype(F32)
    padded = jnp.concatenate([stacked, jnp.zeros((5, channels), F32)], axis=0)
    places[...] = jnp.transpose(padded)
    for block in range(voxels // LANES):
        lanes = slice(block * LANES, (block + 1) * LANES)
        at = pl.multiple_of(core * voxels + block * LANES, LANES)
        voxel = [vox[d : d + 1, pl.ds(at, LANES)].astype(F32) for d in range(3)]

        def tile(index, carry, voxel=voxel, lanes=lanes):
            rows = pl.ds(pl.multiple_of(index * ROWS, ROWS), ROWS)
            columns = [places[rows, d : d + 1] for d in range(3)]
            real, imag = operator_tile(columns, voxel, wavenumber, scale)
            cosines[rows, lanes] = real.astype(BF16)
            sines[rows, lanes] = imag.astype(BF16)
            return carry

        lax.fori_loop(0, channels // ROWS, tile, 0)


def beam_kernel(cosines, sines, own, other, y_ref, keep_ref, send_ref, data, gram):
    core = lax.axis_index("core")
    frames = y_ref.shape[0] // 2
    half = frames // CORES
    voxels = y_ref.shape[1]
    here = pl.multiple_of(core * half, half)
    there = pl.multiple_of((1 - core) * half, half)
    blocks = own.shape[0]
    width = own.shape[-1]
    for k in range(blocks):
        for part in range(2):
            lanes = slice(k * width, (k + 1) * width)
            data[pl.ds(part * frames + here, half), lanes] = own[k, :, part].reshape(half, width)
            data[pl.ds(part * frames + there, half), lanes] = other[k, :, part].reshape(half, width)
    for block in range(voxels // LANES):
        lanes = slice(block * LANES, (block + 1) * LANES)
        first = jnp.dot(data[...], cosines[:, lanes], preferred_element_type=F32)
        second = jnp.dot(data[...], sines[:, lanes], preferred_element_type=F32)
        y_ref[:frames, lanes] = (first[:frames] + second[frames:]).astype(BF16)
        y_ref[frames:, lanes] = (first[frames:] - second[:frames]).astype(BF16)
    y = y_ref[...]
    products = lax.dot_general(y, y, (((1,), (1,)), ((), ())), preferred_element_type=F32)
    gram[...] = (products[:frames, :frames] + products[frames:, frames:]) + (
        products[:frames, frames:] - products[frames:, :frames]
    )
    keep_ref[...] = gram[pl.ds(here, half), :]
    send_ref[...] = gram[pl.ds(there, half), :]


def complex_product(left, right):
    def dot(a, b):
        return jnp.dot(a, b, preferred_element_type=F32, precision=lax.Precision.HIGHEST)

    return (
        dot(left[0], right[0]) - dot(left[1], right[1]),
        dot(left[0], right[1]) + dot(left[1], right[0]),
    )


def filter_kernel(own, other, y_ref, out_ref, gram):
    core = lax.axis_index("core")
    half, frames = own.shape
    gram[pl.ds(pl.multiple_of(core * half, half), half), :] = own[...]
    gram[pl.ds(pl.multiple_of((1 - core) * half, half), half), :] = other[...]
    both = gram[...]
    flipped = jnp.transpose(both)
    gram_re = 0.5 * (both + flipped)
    gram_im = 0.5 * (both - flipped)
    squares = jnp.sum(gram_re * gram_re + gram_im * gram_im)
    factor = 4.0 / jnp.sqrt(jnp.full((1, 1), squares + EPSILON, F32))
    mat = (gram_re * factor, gram_im * factor)
    second = complex_product(mat, mat)
    third = complex_product(second, mat)
    rows = lax.broadcasted_iota(jnp.int32, (frames, frames), 0)
    cols = lax.broadcasted_iota(jnp.int32, (frames, frames), 1)
    identity = jnp.where(rows == cols, 1.0, 0.0).astype(F32)
    real = (identity - mat[0] + 0.3 * second[0] - 0.03 * third[0]).astype(BF16)
    imag = (-mat[1] + 0.3 * second[1] - 0.03 * third[1]).astype(BF16)
    matrix = jnp.concatenate(
        [jnp.concatenate([real, imag], axis=1), jnp.concatenate([-imag, real], axis=1)], axis=0
    )
    applied = jnp.dot(matrix, y_ref[...], preferred_element_type=F32).astype(BF16)
    group = out_ref.shape[2]
    bins = out_ref.shape[0] // CORES
    for part in range(2):
        for c in range(CORES):
            for j in range(bins):
                row = part * frames + c * half + j * group
                out_ref[j * CORES + c, part] = applied[row : row + group]


def place_kernel(got, out_ref):
    group, _, bins, _ = out_ref.shape
    voxels = got.shape[-1]
    size = group * bins
    rows = lax.broadcasted_iota(jnp.int32, (size, size), 0)
    cols = lax.broadcasted_iota(jnp.int32, (size, size), 1)
    turn = jnp.where(cols == (rows % bins) * group + rows // bins, 1.0, 0.0).astype(BF16)
    for c in range(CORES):
        for part in range(2):
            block = got[:, c, part].reshape(size, voxels)
            moved = jnp.dot(turn, block, preferred_element_type=F32).astype(BF16)
            out_ref[:, part, :, c * voxels : (c + 1) * voxels] = moved.reshape(group, bins, voxels)


def shards(rf_data, elem_pos, vox_pos, subbands):
    parts, bins, group, width = rf_data.shape
    chans = elem_pos.shape[1] // width
    voxels = vox_pos.shape[1] // CORES
    frames = group * bins * CORES
    half = frames // CORES
    swap = [(0, 1), (1, 0)]
    vmem = pl.BlockSpec(memory_space=pltpu.VMEM)
    smem = pl.BlockSpec(memory_space=pltpu.SMEM)

    by_bin = jnp.broadcast_to(jnp.swapaxes(rf_data, 0, 1)[None], (chans, bins, parts, group, width))
    by_bin = by_bin.reshape(chans * bins, parts, group, width)
    own = lax.all_to_all(by_bin, ("chan", "bin"), split_axis=0, concat_axis=0, tiled=True)
    cosines, sines = pl.pallas_call(
        operator_kernel,
        name="operator",
        out_shape=(jax.ShapeDtypeStruct((chans * width, voxels), BF16),) * 2,
        in_specs=[vmem, vmem, smem],
        out_specs=(vmem, vmem),
        scratch_shapes=[pltpu.VMEM((chans * width, 8), F32)],
        compiler_params=WIDE,
        cost_estimate=pl.CostEstimate(
            flops=60 * chans * width * voxels,
            transcendentals=chans * width * voxels,
            bytes_accessed=4 * chans * width * voxels,
        ),
    )(elem_pos, vox_pos, subbands)

    own, cosines, sines = lax.optimization_barrier((own, cosines, sines))
    other = lax.ppermute(own, "core", swap)
    own = own.reshape(chans, bins, parts, group, width)
    other = other.reshape(chans, bins, parts, group, width)

    y, keep, send = pl.pallas_call(
        beam_kernel,
        name="beam",
        out_shape=(
            jax.ShapeDtypeStruct((2 * frames, voxels), BF16),
            jax.ShapeDtypeStruct((half, frames), F32),
            jax.ShapeDtypeStruct((half, frames), F32),
        ),
        in_specs=[vmem, vmem, vmem, vmem],
        out_specs=(vmem, vmem, vmem),
        scratch_shapes=[
            pltpu.VMEM((2 * frames, chans * width), BF16),
            pltpu.VMEM((frames, frames), F32),
        ],
        compiler_params=WIDE,
    )(cosines, sines, own, other)

    total = keep + lax.ppermute(send, "core", swap)
    step = 1
    while step < chans:
        total = total + lax.ppermute(total, "chan", [(a, a ^ step) for a in range(chans)])
        step *= 2
    rest = lax.ppermute(total, "core", swap)

    applied = pl.pallas_call(
        filter_kernel,
        name="filter",
        out_shape=jax.ShapeDtypeStruct((bins * CORES, parts, group, voxels), BF16),
        in_specs=[vmem, vmem, vmem],
        out_specs=vmem,
        scratch_shapes=[pltpu.VMEM((frames, frames), F32)],
        compiler_params=WIDE,
    )(total, rest, y)

    got = lax.all_to_all(applied, ("bin", "core"), split_axis=0, concat_axis=0, tiled=True)
    got = got.reshape(bins, CORES, parts, group, voxels)
    return pl.pallas_call(
        place_kernel,
        name="place",
        out_shape=jax.ShapeDtypeStruct((group, parts, bins, CORES * voxels), BF16),
        in_specs=[vmem],
        out_specs=vmem,
        compiler_params=WIDE,
    )(got)


def solution(mesh):
    chans = mesh.shape["chan"]
    fine = Mesh(mesh.devices.reshape(chans, BINS, CORES), ("chan", "bin", "core"))
    return jax.shard_map(
        shards,
        mesh=fine,
        in_specs=(P(None, None, ("bin", "core"), "chan"), P(), P(None, "chan"), P()),
        out_specs=P(("bin", "core"), None, None, "chan"),
        check_vma=False,
    )
```

```python
import math

import jax
import jax.numpy as jnp
from jax import lax
from jax.experimental import pallas as pl
from jax.experimental.pallas import tpu as pltpu
from jax.sharding import Mesh, PartitionSpec as P

EPSILON = 1e-06
BINS = 8
CORES = 2
F32 = jnp.float32
BF16 = jnp.bfloat16
SIN = (3.1415925800446924, -5.167706878924515, 2.5500313772531213, -0.5980451739748806, 0.0772201286897368)
COS = (0.9999999534666272, -4.934792858670076, 4.058411914063177, -1.331880160583308, 0.21969679727234584)
ROUNDER = 12582912.0
ROWS = 256
LANES = 256
WIDE = pltpu.CompilerParams(vmem_limit_bytes=16 * 1024 * 1024)
VMEM = pl.BlockSpec(memory_space=pltpu.VMEM)
HBM = pl.BlockSpec(memory_space=pltpu.HBM)


def horner(coefficients, z):
    total = coefficients[-1] * z + coefficients[-2]
    for value in coefficients[-3::-1]:
        total = total * z + value
    return total


def digits(value, unit):
    high = jnp.floor(value * (1.0 / unit))
    return high, value - unit * high


def spread_kernel(rf_ref, out_ref, held, sem):
    copy = pltpu.make_async_copy(rf_ref, held, sem)
    copy.start()
    copy.wait()
    for part in range(held.shape[0]):
        block = held[part]
        for k in range(out_ref.shape[0]):
            out_ref[k, :, part] = block


def operator_kernel(elem_ref, vox_ref, bins_ref, out_ref, done_ref, elem, vox, bins, lhs_ref, sems):
    core = lax.axis_index("core")
    _, channels, voxels = out_ref.shape
    copies = [
        pltpu.make_async_copy(source, target, sems.at[n])
        for n, (source, target) in enumerate(((elem_ref, elem), (vox_ref, vox), (bins_ref, bins)))
    ]
    for copy in copies:
        copy.start()
    for copy in copies:
        copy.wait()
    wavenumber = (32.0 + bins[lax.axis_index("bin")].astype(F32)) / 64.0
    scale = 2.0 / math.sqrt(channels)

    place = elem[...].astype(F32)
    high, low = digits(jnp.sum(place * place, axis=0, keepdims=True), 16.0)
    one = jnp.ones((1, channels), F32)
    lhs = jnp.concatenate([place, high, low, one, one, 0.0 * one], axis=0)
    lhs_ref[...] = jnp.transpose(lhs).astype(BF16)
    voxel = vox[:, pl.ds(pl.multiple_of(core * voxels, voxels), voxels)].astype(F32)
    high, low = digits(jnp.sum(voxel * voxel, axis=0, keepdims=True), 64.0)
    one = jnp.ones((1, voxels), F32)
    zero = 0.0 * one
    level = voxel[2:3]
    squares = jnp.concatenate([-2.0 * voxel, 16.0 * one, one, 64.0 * high, low, zero], axis=0).astype(BF16)
    depths = jnp.concatenate([zero, zero, -1.0 * one, zero, zero, level, zero, zero], axis=0).astype(BF16)

    def tile(index, carry):
        rows = pl.ds(pl.multiple_of(index * ROWS, ROWS), ROWS)
        left = lhs_ref[rows]
        squared = jnp.dot(left, squares, preferred_element_type=F32)
        depth = jnp.dot(left, depths, preferred_element_type=F32)
        inverse = lax.rsqrt(squared)
        turns = (level + squared * inverse) * wavenumber
        part = turns - ((turns + ROUNDER) - ROUNDER)
        z = part * part
        sine = part * horner(SIN, z)
        cosine = horner(COS, z)
        double = depth * inverse * scale
        lean = double * sine
        out_ref[0, rows] = (0.5 * double - lean * sine).astype(BF16)
        out_ref[1, rows] = (lean * cosine).astype(BF16)
        return carry

    lax.fori_loop(0, channels // ROWS, tile, 0)
    done_ref[...] = jnp.zeros_like(done_ref)


def beamform(samples, operator, data):
    blocks, bins, _, group, width = samples.shape
    half = bins * group
    for k in range(blocks):
        for part in range(2):
            data[part * half : (part + 1) * half, k * width : (k + 1) * width] = samples[k, :, part].reshape(half, width)
    for block in range(operator.shape[2] // LANES):
        lanes = slice(block * LANES, (block + 1) * LANES)
        first = jnp.dot(data[...], operator[0, :, lanes], preferred_element_type=F32)
        second = jnp.dot(data[...], operator[1, :, lanes], preferred_element_type=F32)
        yield lanes, (first[:half] + second[half:]).astype(BF16), (first[half:] - second[:half]).astype(BF16)


def own_kernel(operator, samples, out_ref, data):
    half = out_ref.shape[0] // 2
    for lanes, real, imag in beamform(samples, operator, data):
        out_ref[:half, lanes] = real
        out_ref[half:, lanes] = imag


def other_kernel(operator, samples, own, y_ref, keep_ref, send_ref, data, gram):
    core = lax.axis_index("core")
    frames = y_ref.shape[0] // 2
    half = frames // CORES
    here = pl.multiple_of(core * half, half)
    there = pl.multiple_of((1 - core) * half, half)
    y_ref[pl.ds(here, half)] = own[:half]
    y_ref[pl.ds(frames + here, half)] = own[half:]
    for lanes, real, imag in beamform(samples, operator, data):
        y_ref[pl.ds(there, half), lanes] = real
        y_ref[pl.ds(frames + there, half), lanes] = imag
    y = y_ref[...]
    products = lax.dot_general(y, y, (((1,), (1,)), ((), ())), preferred_element_type=F32)
    gram[...] = (products[:frames, :frames] + products[frames:, frames:]) + (
        products[:frames, frames:] - products[frames:, :frames]
    )
    keep_ref[...] = gram[pl.ds(here, half), :]
    send_ref[...] = gram[pl.ds(there, half), :]


def halves(x):
    high = x.astype(BF16)
    return high, (x - high.astype(F32)).astype(BF16)


def product(left, right):
    left_high, left_low = halves(left)
    right_high, right_low = halves(right)
    return jnp.dot(
        jnp.concatenate([left_high, left_high, left_low], axis=1),
        jnp.concatenate([right_high, right_low, right_high], axis=0),
        preferred_element_type=F32,
    )


def unpack(packed):
    flipped = jnp.transpose(packed)
    return 0.5 * (packed + flipped), 0.5 * (packed - flipped), flipped


def filter_kernel(own, other, y_ref, out_ref, gram):
    core = lax.axis_index("core")
    half, frames = own.shape
    gram[pl.ds(pl.multiple_of(core * half, half), half), :] = own[...]
    gram[pl.ds(pl.multiple_of((1 - core) * half, half), half), :] = other[...]
    packed = gram[...]
    squares = jnp.sum(packed * packed)
    factor = 4.0 / jnp.sqrt(jnp.full((1, 1), squares + EPSILON, F32))
    mat = packed * factor
    real, imag, flipped = unpack(mat)
    left = jnp.concatenate([real, imag], axis=1)
    second = product(left, jnp.concatenate([mat, flipped], axis=0))
    third = product(left, jnp.concatenate([second, jnp.transpose(second)], axis=0))
    rows = lax.broadcasted_iota(jnp.int32, (frames, frames), 0)
    cols = lax.broadcasted_iota(jnp.int32, (frames, frames), 1)
    identity = jnp.where(rows == cols, 1.0, 0.0).astype(F32)
    real, imag, _ = unpack(identity - mat + 0.3 * second - 0.03 * third)
    real, imag = real.astype(BF16), imag.astype(BF16)
    matrix = jnp.concatenate(
        [jnp.concatenate([real, imag], axis=1), jnp.concatenate([-imag, real], axis=1)], axis=0
    )
    applied = jnp.dot(matrix, y_ref[...], preferred_element_type=F32).astype(BF16)
    group = out_ref.shape[2]
    bins = out_ref.shape[0] // CORES
    for part in range(2):
        for c in range(CORES):
            for j in range(bins):
                row = part * frames + c * half + j * group
                out_ref[j * CORES + c, part] = applied[row : row + group]


def place_kernel(got, out_ref):
    group, _, bins, _ = out_ref.shape
    voxels = got.shape[-1]
    size = group * bins
    rows = lax.broadcasted_iota(jnp.int32, (size, size), 0)
    cols = lax.broadcasted_iota(jnp.int32, (size, size), 1)
    turn = jnp.where(cols == (rows % bins) * group + rows // bins, 1.0, 0.0).astype(BF16)
    for c in range(CORES):
        for part in range(2):
            block = got[:, c, part].reshape(size, voxels)
            moved = jnp.dot(turn, block, preferred_element_type=F32).astype(BF16)
            out_ref[:, part, :, c * voxels : (c + 1) * voxels] = moved.reshape(group, bins, voxels)


def shards(rf_data, elem_pos, vox_pos, subbands):
    parts, bins, group, width = rf_data.shape
    channels = elem_pos.shape[1]
    chans = channels // width
    voxels = vox_pos.shape[1] // CORES
    frames = group * bins * CORES
    half = frames // CORES

    def shape(*dims, dtype=BF16):
        return jax.ShapeDtypeStruct(dims, dtype)

    def swap(x):
        return lax.ppermute(x, "core", [(0, 1), (1, 0)])

    def across(x, bits):
        return lax.ppermute(x, "chan", [(a, a ^ bits) for a in range(chans)])

    by_bin = pl.pallas_call(
        spread_kernel,
        name="spread",
        out_shape=shape(chans, bins, parts, group, width),
        in_specs=[HBM],
        out_specs=VMEM,
        scratch_shapes=[pltpu.VMEM(rf_data.shape, BF16), pltpu.SemaphoreType.DMA],
        compiler_params=WIDE,
    )(pltpu.with_memory_space_constraint(rf_data, pltpu.HBM))
    by_bin = by_bin.reshape(chans * bins, parts, group, width)
    own = lax.all_to_all(by_bin, ("chan", "bin"), split_axis=0, concat_axis=0, tiled=True)

    operator, done = pl.pallas_call(
        operator_kernel,
        name="operator",
        out_shape=(shape(2, channels, voxels), shape(8, 128, dtype=F32)),
        in_specs=[HBM, HBM, HBM],
        out_specs=(VMEM, VMEM),
        scratch_shapes=[
            pltpu.VMEM(elem_pos.shape, jnp.int32),
            pltpu.VMEM(vox_pos.shape, jnp.int32),
            pltpu.SMEM(subbands.shape, jnp.int32),
            pltpu.VMEM((channels, 8), BF16),
            pltpu.SemaphoreType.DMA((3,)),
        ],
        compiler_params=WIDE,
        cost_estimate=pl.CostEstimate(
            flops=60 * channels * voxels,
            transcendentals=channels * voxels,
            bytes_accessed=4 * channels * voxels,
        ),
    )(*(pltpu.with_memory_space_constraint(x, pltpu.HBM) for x in (elem_pos, vox_pos, subbands)))

    own, _ = lax.optimization_barrier((own, done))
    other = swap(own)
    own = own.reshape(chans, bins, parts, group, width)
    other = other.reshape(chans, bins, parts, group, width)

    beam_cost = pl.CostEstimate(
        flops=8 * half * channels * voxels * 2, transcendentals=0, bytes_accessed=4 * channels * voxels
    )
    mine = pl.pallas_call(
        own_kernel,
        name="beam_own",
        out_shape=shape(frames, voxels),
        in_specs=[VMEM, VMEM],
        out_specs=VMEM,
        scratch_shapes=[pltpu.VMEM((frames, channels), BF16)],
        compiler_params=WIDE,
        cost_estimate=beam_cost,
    )(operator, own)
    y, keep, send = pl.pallas_call(
        other_kernel,
        name="beam_other",
        out_shape=(shape(2 * frames, voxels), shape(half, frames, dtype=F32), shape(half, frames, dtype=F32)),
        in_specs=[VMEM, VMEM, VMEM],
        out_specs=(VMEM, VMEM, VMEM),
        scratch_shapes=[pltpu.VMEM((frames, channels), BF16), pltpu.VMEM((frames, frames), F32)],
        compiler_params=WIDE,
        cost_estimate=beam_cost,
    )(operator, other, mine)

    total = keep + swap(send)
    near, far, next_to = across(total, 1), across(total, 3), across(total, 2)
    total = total + near + far + next_to
    total = total + across(total, 4)
    rest = swap(total)

    applied = pl.pallas_call(
        filter_kernel,
        name="filter",
        out_shape=shape(bins * CORES, parts, group, voxels),
        in_specs=[VMEM, VMEM, VMEM],
        out_specs=VMEM,
        scratch_shapes=[pltpu.VMEM((frames, frames), F32)],
        compiler_params=WIDE,
    )(total, rest, y)

    got = lax.all_to_all(applied, ("bin", "core"), split_axis=0, concat_axis=0, tiled=True)
    got = got.reshape(bins, CORES, parts, group, voxels)
    return pl.pallas_call(
        place_kernel,
        name="place",
        out_shape=shape(group, parts, bins, CORES * voxels),
        in_specs=[VMEM],
        out_specs=VMEM,
        compiler_params=WIDE,
    )(got)


def solution(mesh):
    chans = mesh.shape["chan"]
    fine = Mesh(mesh.devices.reshape(chans, BINS, CORES), ("chan", "bin", "core"))
    return jax.shard_map(
        shards,
        mesh=fine,
        in_specs=(P(None, None, ("bin", "core"), "chan"), P(), P(None, "chan"), P()),
        out_specs=P(("bin", "core"), None, None, "chan"),
        check_vma=False,
    )
```

```python
import functools
import math

import jax
import jax.numpy as jnp
from jax import lax
from jax.experimental import pallas as pl
from jax.experimental.pallas import tpu as pltpu
from jax.sharding import Mesh, PartitionSpec as P

EPSILON = 1e-06
BINS = 8
CORES = 2
F32 = jnp.float32
BF16 = jnp.bfloat16
SIN = (3.1415925800446924, -5.167706878924515, 2.5500313772531213, -0.5980451739748806, 0.0772201286897368)
COS = (0.9999999534666272, -4.934792858670076, 4.058411914063177, -1.331880160583308, 0.21969679727234584)
ROUNDER = 12582912.0
ROWS = 256
LANES = 256
WIDE = pltpu.CompilerParams(vmem_limit_bytes=16 * 1024 * 1024)
VMEM = pl.BlockSpec(memory_space=pltpu.VMEM)
HBM = pl.BlockSpec(memory_space=pltpu.HBM)


def horner(coefficients, z):
    total = coefficients[-1] * z + coefficients[-2]
    for value in coefficients[-3::-1]:
        total = total * z + value
    return total


def digits(value, unit):
    high = jnp.floor(value * (1.0 / unit))
    return high, value - unit * high


def spread_kernel(rf_ref, out_ref, held, sem):
    copy = pltpu.make_async_copy(rf_ref, held, sem)
    copy.start()
    copy.wait()
    for part in range(held.shape[0]):
        block = held[part]
        for k in range(out_ref.shape[0]):
            out_ref[k, :, part] = block


def operator_kernel(start, elem_ref, vox_ref, bins_ref, out_ref, elem, vox, bins, lhs_ref, sems):
    core = lax.axis_index("core")
    _, share, voxels = out_ref.shape
    channels = elem.shape[1]
    copies = [
        pltpu.make_async_copy(source, target, sems.at[n])
        for n, (source, target) in enumerate(((elem_ref, elem), (vox_ref, vox), (bins_ref, bins)))
    ]
    for copy in copies:
        copy.start()
    for copy in copies:
        copy.wait()
    wavenumber = (32.0 + bins[lax.axis_index("bin")].astype(F32)) / 64.0
    scale = 2.0 / math.sqrt(channels)

    place = elem[...].astype(F32)
    high, low = digits(jnp.sum(place * place, axis=0, keepdims=True), 16.0)
    one = jnp.ones((1, channels), F32)
    lhs = jnp.concatenate([place, high, low, one, one, 0.0 * one], axis=0)
    lhs_ref[...] = jnp.transpose(lhs).astype(BF16)
    voxel = vox[:, pl.ds(pl.multiple_of(core * voxels, voxels), voxels)].astype(F32)
    high, low = digits(jnp.sum(voxel * voxel, axis=0, keepdims=True), 64.0)
    one = jnp.ones((1, voxels), F32)
    zero = 0.0 * one
    level = voxel[2:3]
    squares = jnp.concatenate([-2.0 * voxel, 16.0 * one, one, 64.0 * high, low, zero], axis=0).astype(BF16)
    depths = jnp.concatenate([zero, zero, -1.0 * one, zero, zero, level, zero, zero], axis=0).astype(BF16)

    def tile(index, carry):
        rows = pl.ds(pl.multiple_of(index * ROWS, ROWS), ROWS)
        left = lhs_ref[pl.ds(pl.multiple_of(start + index * ROWS, ROWS), ROWS)]
        squared = jnp.dot(left, squares, preferred_element_type=F32)
        depth = jnp.dot(left, depths, preferred_element_type=F32)
        inverse = lax.rsqrt(squared)
        turns = (level + squared * inverse) * wavenumber
        part = turns - ((turns + ROUNDER) - ROUNDER)
        z = part * part
        sine = part * horner(SIN, z)
        cosine = horner(COS, z)
        double = depth * inverse * scale
        lean = double * sine
        out_ref[0, rows] = (0.5 * double - lean * sine).astype(BF16)
        out_ref[1, rows] = (lean * cosine).astype(BF16)
        return carry

    lax.fori_loop(0, share // ROWS, tile, 0)


def beamform(samples, upper, lower, data):
    blocks, bins, _, group, width = samples.shape
    half = bins * group
    for k in range(blocks):
        for part in range(2):
            data[part * half : (part + 1) * half, k * width : (k + 1) * width] = samples[k, :, part].reshape(half, width)
    share = upper.shape[1]

    def applied(which, lanes):
        left = jnp.dot(data[:, :share], upper[which, :, lanes], preferred_element_type=F32)
        return left + jnp.dot(data[:, share:], lower[which, :, lanes], preferred_element_type=F32)

    for block in range(upper.shape[2] // LANES):
        lanes = slice(block * LANES, (block + 1) * LANES)
        first, second = applied(0, lanes), applied(1, lanes)
        yield lanes, (first[:half] + second[half:]).astype(BF16), (first[half:] - second[:half]).astype(BF16)


def own_kernel(upper, lower, samples, out_ref, data):
    half = out_ref.shape[0] // 2
    for lanes, real, imag in beamform(samples, upper, lower, data):
        out_ref[:half, lanes] = real
        out_ref[half:, lanes] = imag


def other_kernel(upper, lower, samples, own, y_ref, keep_ref, send_ref, data, gram):
    core = lax.axis_index("core")
    frames = y_ref.shape[0] // 2
    half = frames // CORES
    here = pl.multiple_of(core * half, half)
    there = pl.multiple_of((1 - core) * half, half)
    y_ref[pl.ds(here, half)] = own[:half]
    y_ref[pl.ds(frames + here, half)] = own[half:]
    for lanes, real, imag in beamform(samples, upper, lower, data):
        y_ref[pl.ds(there, half), lanes] = real
        y_ref[pl.ds(frames + there, half), lanes] = imag
    y = y_ref[...]
    products = lax.dot_general(y, y, (((1,), (1,)), ((), ())), preferred_element_type=F32)
    gram[...] = (products[:frames, :frames] + products[frames:, frames:]) + (
        products[:frames, frames:] - products[frames:, :frames]
    )
    keep_ref[...] = gram[pl.ds(here, half), :]
    send_ref[...] = gram[pl.ds(there, half), :]


def halves(x):
    high = x.astype(BF16)
    return high, (x - high.astype(F32)).astype(BF16)


def product(left, right):
    left_high, left_low = halves(left)
    right_high, right_low = halves(right)
    return jnp.dot(
        jnp.concatenate([left_high, left_high, left_low], axis=1),
        jnp.concatenate([right_high, right_low, right_high], axis=0),
        preferred_element_type=F32,
    )


def unpack(packed):
    flipped = jnp.transpose(packed)
    return 0.5 * (packed + flipped), 0.5 * (packed - flipped), flipped


def filter_kernel(own, other, y_ref, out_ref, gram):
    core = lax.axis_index("core")
    half, frames = own.shape
    gram[pl.ds(pl.multiple_of(core * half, half), half), :] = own[...]
    gram[pl.ds(pl.multiple_of((1 - core) * half, half), half), :] = other[...]
    packed = gram[...]
    squares = jnp.sum(packed * packed)
    factor = 4.0 / jnp.sqrt(jnp.full((1, 1), squares + EPSILON, F32))
    mat = packed * factor
    real, imag, flipped = unpack(mat)
    left = jnp.concatenate([real, imag], axis=1)
    second = product(left, jnp.concatenate([mat, flipped], axis=0))
    third = product(left, jnp.concatenate([second, jnp.transpose(second)], axis=0))
    rows = lax.broadcasted_iota(jnp.int32, (frames, frames), 0)
    cols = lax.broadcasted_iota(jnp.int32, (frames, frames), 1)
    identity = jnp.where(rows == cols, 1.0, 0.0).astype(F32)
    real, imag, _ = unpack(identity - mat + 0.3 * second - 0.03 * third)
    real, imag = real.astype(BF16), imag.astype(BF16)
    matrix = jnp.concatenate(
        [jnp.concatenate([real, imag], axis=1), jnp.concatenate([-imag, real], axis=1)], axis=0
    )
    applied = jnp.dot(matrix, y_ref[...], preferred_element_type=F32).astype(BF16)
    group = out_ref.shape[2]
    bins = out_ref.shape[0] // CORES
    for part in range(2):
        for c in range(CORES):
            for j in range(bins):
                row = part * frames + c * half + j * group
                out_ref[j * CORES + c, part] = applied[row : row + group]


def place_kernel(got, out_ref):
    group, _, bins, _ = out_ref.shape
    voxels = got.shape[-1]
    size = group * bins
    rows = lax.broadcasted_iota(jnp.int32, (size, size), 0)
    cols = lax.broadcasted_iota(jnp.int32, (size, size), 1)
    turn = jnp.where(cols == (rows % bins) * group + rows // bins, 1.0, 0.0).astype(BF16)
    for c in range(CORES):
        for part in range(2):
            block = got[:, c, part].reshape(size, voxels)
            moved = jnp.dot(turn, block, preferred_element_type=F32).astype(BF16)
            out_ref[:, part, :, c * voxels : (c + 1) * voxels] = moved.reshape(group, bins, voxels)


def shards(rf_data, elem_pos, vox_pos, subbands):
    parts, bins, group, width = rf_data.shape
    channels = elem_pos.shape[1]
    chans = channels // width
    voxels = vox_pos.shape[1] // CORES
    frames = group * bins * CORES
    half = frames // CORES

    def shape(*dims, dtype=BF16):
        return jax.ShapeDtypeStruct(dims, dtype)

    def swap(x):
        return lax.ppermute(x, "core", [(0, 1), (1, 0)])

    def across(x, bits):
        return lax.ppermute(x, "chan", [(a, a ^ bits) for a in range(chans)])

    by_bin = pl.pallas_call(
        spread_kernel,
        name="spread",
        out_shape=shape(chans, bins, parts, group, width),
        in_specs=[HBM],
        out_specs=VMEM,
        scratch_shapes=[pltpu.VMEM(rf_data.shape, BF16), pltpu.SemaphoreType.DMA],
        compiler_params=WIDE,
    )(pltpu.with_memory_space_constraint(rf_data, pltpu.HBM))
    by_bin = by_bin.reshape(chans * bins, parts, group, width)
    own = lax.all_to_all(by_bin, ("chan", "bin"), split_axis=0, concat_axis=0, tiled=True)

    def operator(start, share, elem_pos):
        return pl.pallas_call(
            functools.partial(operator_kernel, start),
            name="operator",
            out_shape=shape(2, share, voxels),
            in_specs=[HBM, HBM, HBM],
            out_specs=VMEM,
            scratch_shapes=[
                pltpu.VMEM(elem_pos.shape, jnp.int32),
                pltpu.VMEM(vox_pos.shape, jnp.int32),
                pltpu.SMEM(subbands.shape, jnp.int32),
                pltpu.VMEM((channels, 8), BF16),
                pltpu.SemaphoreType.DMA((3,)),
            ],
            compiler_params=WIDE,
            cost_estimate=pl.CostEstimate(
                flops=60 * share * voxels, transcendentals=share * voxels, bytes_accessed=4 * share * voxels
            ),
        )(*(pltpu.with_memory_space_constraint(x, pltpu.HBM) for x in (elem_pos, vox_pos, subbands)))

    first = 3 * channels // 4
    upper = operator(0, first, elem_pos)
    own, upper, elem_pos = lax.optimization_barrier((own, upper, elem_pos))
    other = swap(own)
    lower = operator(first, channels - first, elem_pos)
    own = own.reshape(chans, bins, parts, group, width)
    other = other.reshape(chans, bins, parts, group, width)

    beam_cost = pl.CostEstimate(
        flops=8 * half * channels * voxels * 2, transcendentals=0, bytes_accessed=4 * channels * voxels
    )
    mine = pl.pallas_call(
        own_kernel,
        name="beam_own",
        out_shape=shape(frames, voxels),
        in_specs=[VMEM, VMEM, VMEM],
        out_specs=VMEM,
        scratch_shapes=[pltpu.VMEM((frames, channels), BF16)],
        compiler_params=WIDE,
        cost_estimate=beam_cost,
    )(upper, lower, own)
    y, keep, send = pl.pallas_call(
        other_kernel,
        name="beam_other",
        out_shape=(shape(2 * frames, voxels), shape(half, frames, dtype=F32), shape(half, frames, dtype=F32)),
        in_specs=[VMEM, VMEM, VMEM, VMEM],
        out_specs=(VMEM, VMEM, VMEM),
        scratch_shapes=[pltpu.VMEM((frames, channels), BF16), pltpu.VMEM((frames, frames), F32)],
        compiler_params=WIDE,
        cost_estimate=beam_cost,
    )(upper, lower, other, mine)

    total = keep + swap(send)
    near, far, next_to = across(total, 1), across(total, 3), across(total, 2)
    total = total + near + far + next_to
    total = total + across(total, 4)
    rest = swap(total)

    applied = pl.pallas_call(
        filter_kernel,
        name="filter",
        out_shape=shape(bins * CORES, parts, group, voxels),
        in_specs=[VMEM, VMEM, VMEM],
        out_specs=VMEM,
        scratch_shapes=[pltpu.VMEM((frames, frames), F32)],
        compiler_params=WIDE,
    )(total, rest, y)

    got = lax.all_to_all(applied, ("bin", "core"), split_axis=0, concat_axis=0, tiled=True)
    got = got.reshape(bins, CORES, parts, group, voxels)
    return pl.pallas_call(
        place_kernel,
        name="place",
        out_shape=shape(group, parts, bins, CORES * voxels),
        in_specs=[VMEM],
        out_specs=VMEM,
        compiler_params=WIDE,
    )(got)


def solution(mesh):
    chans = mesh.shape["chan"]
    fine = Mesh(mesh.devices.reshape(chans, BINS, CORES), ("chan", "bin", "core"))
    return jax.shard_map(
        shards,
        mesh=fine,
        in_specs=(P(None, None, ("bin", "core"), "chan"), P(), P(None, "chan"), P()),
        out_specs=P(("bin", "core"), None, None, "chan"),
        check_vma=False,
    )
```

```python
import functools
import math

import jax
import jax.numpy as jnp
from jax import lax
from jax.experimental import pallas as pl
from jax.experimental.pallas import tpu as pltpu
from jax.sharding import Mesh, PartitionSpec as P

EPSILON = 1e-06
BINS = 8
CORES = 2
F32 = jnp.float32
BF16 = jnp.bfloat16
SIN = (3.1415925800446924, -5.167706878924515, 2.5500313772531213, -0.5980451739748806, 0.0772201286897368)
COS = (0.9999999534666272, -4.934792858670076, 4.058411914063177, -1.331880160583308, 0.21969679727234584)
ROUNDER = 12582912.0
UPPER_ROWS = 192
LOWER_ROWS = 224
LANES = 256
WIDE = pltpu.CompilerParams(vmem_limit_bytes=16 * 1024 * 1024)
VMEM = pl.BlockSpec(memory_space=pltpu.VMEM)
HBM = pl.BlockSpec(memory_space=pltpu.HBM)


def horner(coefficients, z):
    total = coefficients[-1] * z + coefficients[-2]
    for value in coefficients[-3::-1]:
        total = total * z + value
    return total


def digits(value, unit):
    high = jnp.floor(value * (1.0 / unit))
    return high, value - unit * high


def spread_kernel(rf_ref, out_ref, sems):
    parts = rf_ref.shape[0]
    copies = [
        pltpu.make_async_copy(rf_ref.at[part], out_ref.at[k, :, part], sems.at[k * parts + part])
        for k in range(out_ref.shape[0])
        for part in range(parts)
    ]
    for copy in copies:
        copy.start()
    for copy in copies:
        copy.wait()


def operator_kernel(elem_ref, vox_ref, bins_ref, upper, lower, elem, vox, bins, lhs_ref, sems):
    core = lax.axis_index("core")
    voxels = upper.shape[2]
    channels = elem.shape[1]
    copies = [
        pltpu.make_async_copy(source, target, sems.at[n])
        for n, (source, target) in enumerate(((elem_ref, elem), (vox_ref, vox), (bins_ref, bins)))
    ]
    for copy in copies:
        copy.start()
    for copy in copies:
        copy.wait()
    wavenumber = (32.0 + bins[lax.axis_index("bin")].astype(F32)) / 64.0
    scale = 2.0 / math.sqrt(channels)

    place = elem[...].astype(F32)
    high, low = digits(jnp.sum(place * place, axis=0, keepdims=True), 16.0)
    one = jnp.ones((1, channels), F32)
    lhs = jnp.concatenate([place, high, low, one, one, 0.0 * one], axis=0)
    lhs_ref[...] = jnp.transpose(lhs).astype(BF16)
    voxel = vox[:, pl.ds(pl.multiple_of(core * voxels, voxels), voxels)].astype(F32)
    high, low = digits(jnp.sum(voxel * voxel, axis=0, keepdims=True), 64.0)
    one = jnp.ones((1, voxels), F32)
    zero = 0.0 * one
    level = voxel[2:3]
    squares = jnp.concatenate([-2.0 * voxel, 16.0 * one, one, 64.0 * high, low, zero], axis=0).astype(BF16)
    depths = jnp.concatenate([zero, zero, -1.0 * one, zero, zero, level, zero, zero], axis=0).astype(BF16)

    def tile(index, carry, out_ref, start, size):
        rows = pl.ds(pl.multiple_of(index * size, size), size)
        left = lhs_ref[pl.ds(pl.multiple_of(start + index * size, 16), size)]
        squared = jnp.dot(left, squares, preferred_element_type=F32)
        depth = jnp.dot(left, depths, preferred_element_type=F32)
        inverse = lax.rsqrt(squared)
        turns = (level + squared * inverse) * wavenumber
        part = turns - ((turns + ROUNDER) - ROUNDER)
        z = part * part
        sine = part * horner(SIN, z)
        cosine = horner(COS, z)
        double = depth * inverse * scale
        lean = double * sine
        out_ref[0, rows] = (0.5 * double - lean * sine).astype(BF16)
        out_ref[1, rows] = (lean * cosine).astype(BF16)
        return carry

    start = 0
    for out_ref, size in ((upper, UPPER_ROWS), (lower, LOWER_ROWS)):
        lax.fori_loop(0, out_ref.shape[1] // size, functools.partial(tile, out_ref=out_ref, start=start, size=size), 0)
        start += out_ref.shape[1]


def beamform(samples, upper, lower, data):
    blocks, bins, _, group, width = samples.shape
    half = bins * group
    for k in range(blocks):
        for part in range(2):
            data[part * half : (part + 1) * half, k * width : (k + 1) * width] = samples[k, :, part].reshape(half, width)
    share = upper.shape[1]

    def applied(which, lanes):
        left = jnp.dot(data[:, :share], upper[which, :, lanes], preferred_element_type=F32)
        return left + jnp.dot(data[:, share:], lower[which, :, lanes], preferred_element_type=F32)

    for block in range(upper.shape[2] // LANES):
        lanes = slice(block * LANES, (block + 1) * LANES)
        first, second = applied(0, lanes), applied(1, lanes)
        yield lanes, (first[:half] + second[half:]).astype(BF16), (first[half:] - second[:half]).astype(BF16)


def own_kernel(upper, lower, samples, out_ref, data):
    half = out_ref.shape[0] // 2
    for lanes, real, imag in beamform(samples, upper, lower, data):
        out_ref[:half, lanes] = real
        out_ref[half:, lanes] = imag


def other_kernel(upper, lower, samples, own, y_ref, keep_ref, send_ref, data, gram):
    core = lax.axis_index("core")
    frames = y_ref.shape[0] // 2
    half = frames // CORES
    here = pl.multiple_of(core * half, half)
    there = pl.multiple_of((1 - core) * half, half)
    y_ref[pl.ds(here, half)] = own[:half]
    y_ref[pl.ds(frames + here, half)] = own[half:]
    for lanes, real, imag in beamform(samples, upper, lower, data):
        y_ref[pl.ds(there, half), lanes] = real
        y_ref[pl.ds(frames + there, half), lanes] = imag
    y = y_ref[...]
    products = lax.dot_general(y, y, (((1,), (1,)), ((), ())), preferred_element_type=F32)
    gram[...] = (products[:frames, :frames] + products[frames:, frames:]) + (
        products[:frames, frames:] - products[frames:, :frames]
    )
    keep_ref[...] = gram[pl.ds(here, half), :]
    send_ref[...] = gram[pl.ds(there, half), :]


def halves(x):
    high = x.astype(BF16)
    return high, (x - high.astype(F32)).astype(BF16)


def product(left, right):
    left_high, left_low = halves(left)
    right_high, right_low = halves(right)
    return jnp.dot(
        jnp.concatenate([left_high, left_high, left_low], axis=1),
        jnp.concatenate([right_high, right_low, right_high], axis=0),
        preferred_element_type=F32,
    )


def unpack(packed):
    flipped = jnp.transpose(packed)
    return 0.5 * (packed + flipped), 0.5 * (packed - flipped), flipped


def filter_kernel(own, other, y_ref, out_ref, gram):
    core = lax.axis_index("core")
    half, frames = own.shape
    gram[pl.ds(pl.multiple_of(core * half, half), half), :] = own[...]
    gram[pl.ds(pl.multiple_of((1 - core) * half, half), half), :] = other[...]
    packed = gram[...]
    squares = jnp.sum(packed * packed)
    factor = 4.0 / jnp.sqrt(jnp.full((1, 1), squares + EPSILON, F32))
    mat = packed * factor
    real, imag, flipped = unpack(mat)
    left = jnp.concatenate([real, imag], axis=1)
    second = product(left, jnp.concatenate([mat, flipped], axis=0))
    third = product(left, jnp.concatenate([second, jnp.transpose(second)], axis=0))
    rows = lax.broadcasted_iota(jnp.int32, (frames, frames), 0)
    cols = lax.broadcasted_iota(jnp.int32, (frames, frames), 1)
    identity = jnp.where(rows == cols, 1.0, 0.0).astype(F32)
    real, imag, _ = unpack(identity - mat + 0.3 * second - 0.03 * third)
    real, imag = real.astype(BF16), imag.astype(BF16)
    matrix = jnp.concatenate(
        [jnp.concatenate([real, imag], axis=1), jnp.concatenate([-imag, real], axis=1)], axis=0
    )
    applied = jnp.dot(matrix, y_ref[...], preferred_element_type=F32).astype(BF16)
    group = out_ref.shape[2]
    bins = out_ref.shape[0] // CORES
    for part in range(2):
        for c in range(CORES):
            for j in range(bins):
                row = part * frames + c * half + j * group
                out_ref[j * CORES + c, part] = applied[row : row + group]


def place_kernel(got, out_ref):
    group, _, bins, _ = out_ref.shape
    voxels = got.shape[-1]
    size = group * bins
    rows = lax.broadcasted_iota(jnp.int32, (size, size), 0)
    cols = lax.broadcasted_iota(jnp.int32, (size, size), 1)
    turn = jnp.where(cols == (rows % bins) * group + rows // bins, 1.0, 0.0).astype(BF16)
    for c in range(CORES):
        for part in range(2):
            block = got[:, c, part].reshape(size, voxels)
            moved = jnp.dot(turn, block, preferred_element_type=F32).astype(BF16)
            out_ref[:, part, :, c * voxels : (c + 1) * voxels] = moved.reshape(group, bins, voxels)


def shards(rf_data, elem_pos, vox_pos, subbands):
    parts, bins, group, width = rf_data.shape
    channels = elem_pos.shape[1]
    chans = channels // width
    voxels = vox_pos.shape[1] // CORES
    frames = group * bins * CORES
    half = frames // CORES

    def shape(*dims, dtype=BF16):
        return jax.ShapeDtypeStruct(dims, dtype)

    def swap(x):
        return lax.ppermute(x, "core", [(0, 1), (1, 0)])

    def across(x, bits):
        return lax.ppermute(x, "chan", [(a, a ^ bits) for a in range(chans)])

    by_bin = pl.pallas_call(
        spread_kernel,
        name="spread",
        out_shape=shape(chans, bins, parts, group, width),
        in_specs=[HBM],
        out_specs=HBM,
        scratch_shapes=[pltpu.SemaphoreType.DMA((chans * parts,))],
        compiler_params=WIDE,
    )(pltpu.with_memory_space_constraint(rf_data, pltpu.HBM))
    by_bin = by_bin.reshape(chans * bins, parts, group, width)
    own = lax.all_to_all(by_bin, ("chan", "bin"), split_axis=0, concat_axis=0, tiled=True)

    share = 3 * UPPER_ROWS
    upper, lower = pl.pallas_call(
        operator_kernel,
        name="operator",
        out_shape=(shape(2, share, voxels), shape(2, channels - share, voxels)),
        in_specs=[HBM, HBM, HBM],
        out_specs=(VMEM, VMEM),
        scratch_shapes=[
            pltpu.VMEM(elem_pos.shape, jnp.int32),
            pltpu.VMEM(vox_pos.shape, jnp.int32),
            pltpu.SMEM(subbands.shape, jnp.int32),
            pltpu.VMEM((channels, 8), BF16),
            pltpu.SemaphoreType.DMA((3,)),
        ],
        compiler_params=WIDE,
        cost_estimate=pl.CostEstimate(
            flops=60 * channels * voxels,
            transcendentals=channels * voxels,
            bytes_accessed=4 * channels * voxels,
        ),
    )(*(pltpu.with_memory_space_constraint(x, pltpu.HBM) for x in (elem_pos, vox_pos, subbands)))

    own, upper, lower = lax.optimization_barrier((own, upper, lower))
    other = swap(own)
    own = own.reshape(chans, bins, parts, group, width)
    other = other.reshape(chans, bins, parts, group, width)

    beam_cost = pl.CostEstimate(
        flops=8 * half * channels * voxels * 2, transcendentals=0, bytes_accessed=4 * channels * voxels
    )
    mine = pl.pallas_call(
        own_kernel,
        name="beam_own",
        out_shape=shape(frames, voxels),
        in_specs=[VMEM, VMEM, VMEM],
        out_specs=VMEM,
        scratch_shapes=[pltpu.VMEM((frames, channels), BF16)],
        compiler_params=WIDE,
        cost_estimate=beam_cost,
    )(upper, lower, own)
    y, keep, send = pl.pallas_call(
        other_kernel,
        name="beam_other",
        out_shape=(shape(2 * frames, voxels), shape(half, frames, dtype=F32), shape(half, frames, dtype=F32)),
        in_specs=[VMEM, VMEM, VMEM, VMEM],
        out_specs=(VMEM, VMEM, VMEM),
        scratch_shapes=[pltpu.VMEM((frames, channels), BF16), pltpu.VMEM((frames, frames), F32)],
        compiler_params=WIDE,
        cost_estimate=beam_cost,
    )(upper, lower, other, mine)

    total = keep + swap(send)
    near, far, next_to = across(total, 1), across(total, 3), across(total, 2)
    total = total + near + far + next_to
    total = total + across(total, 4)
    rest = swap(total)

    applied = pl.pallas_call(
        filter_kernel,
        name="filter",
        out_shape=shape(bins * CORES, parts, group, voxels),
        in_specs=[VMEM, VMEM, VMEM],
        out_specs=VMEM,
        scratch_shapes=[pltpu.VMEM((frames, frames), F32)],
        compiler_params=WIDE,
    )(total, rest, y)

    got = lax.all_to_all(applied, ("bin", "core"), split_axis=0, concat_axis=0, tiled=True)
    got = got.reshape(bins, CORES, parts, group, voxels)
    return pl.pallas_call(
        place_kernel,
        name="place",
        out_shape=shape(group, parts, bins, CORES * voxels),
        in_specs=[VMEM],
        out_specs=VMEM,
        compiler_params=WIDE,
    )(got)


def solution(mesh):
    chans = mesh.shape["chan"]
    fine = Mesh(mesh.devices.reshape(chans, BINS, CORES), ("chan", "bin", "core"))
    return jax.shard_map(
        shards,
        mesh=fine,
        in_specs=(P(None, None, ("bin", "core"), "chan"), P(), P(None, "chan"), P()),
        out_specs=P(("bin", "core"), None, None, "chan"),
        check_vma=False,
    )
```

```python
import functools
import math

import jax
import jax.numpy as jnp
from jax import lax
from jax.experimental import pallas as pl
from jax.experimental.pallas import tpu as pltpu
from jax.sharding import Mesh, PartitionSpec as P

EPSILON = 1e-06
BINS = 8
CORES = 2
F32 = jnp.float32
BF16 = jnp.bfloat16
SIN = (3.1415925800446924, -5.167706878924515, 2.5500313772531213, -0.5980451739748806, 0.0772201286897368)
COS = (0.9999999534666272, -4.934792858670076, 4.058411914063177, -1.331880160583308, 0.21969679727234584)
ROUNDER = 12582912.0
ROWS = 256
LANES = 256
WIDE = pltpu.CompilerParams(vmem_limit_bytes=16 * 1024 * 1024)
VMEM = pl.BlockSpec(memory_space=pltpu.VMEM)
HBM = pl.BlockSpec(memory_space=pltpu.HBM)


def horner(coefficients, z):
    total = coefficients[-1] * z + coefficients[-2]
    for value in coefficients[-3::-1]:
        total = total * z + value
    return total


def digits(value, unit):
    high = jnp.floor(value * (1.0 / unit))
    return high, value - unit * high


def spread_kernel(rf_ref, out_ref, held, sem):
    copy = pltpu.make_async_copy(rf_ref, held, sem)
    copy.start()
    copy.wait()
    for part in range(held.shape[0]):
        block = held[part]
        for k in range(out_ref.shape[0]):
            out_ref[k, :, part] = block


def operator_kernel(elem_ref, vox_ref, bins_ref, upper, lower_ref, elem, vox, bins, lhs_ref, lower, sems):
    core = lax.axis_index("core")
    voxels = upper.shape[2]
    channels = elem.shape[1]
    copies = [
        pltpu.make_async_copy(source, target, sems.at[n])
        for n, (source, target) in enumerate(((elem_ref, elem), (vox_ref, vox), (bins_ref, bins)))
    ]
    for copy in copies:
        copy.start()
    for copy in copies:
        copy.wait()
    wavenumber = (32.0 + bins[lax.axis_index("bin")].astype(F32)) / 64.0
    scale = 2.0 / math.sqrt(channels)

    place = elem[...].astype(F32)
    high, low = digits(jnp.sum(place * place, axis=0, keepdims=True), 16.0)
    one = jnp.ones((1, channels), F32)
    lhs = jnp.concatenate([place, high, low, one, one, 0.0 * one], axis=0)
    lhs_ref[...] = jnp.transpose(lhs).astype(BF16)
    voxel = vox[:, pl.ds(pl.multiple_of(core * voxels, voxels), voxels)].astype(F32)
    high, low = digits(jnp.sum(voxel * voxel, axis=0, keepdims=True), 64.0)
    one = jnp.ones((1, voxels), F32)
    zero = 0.0 * one
    level = voxel[2:3]
    squares = jnp.concatenate([-2.0 * voxel, 16.0 * one, one, 64.0 * high, low, zero], axis=0).astype(BF16)
    depths = jnp.concatenate([zero, zero, -1.0 * one, zero, zero, level, zero, zero], axis=0).astype(BF16)

    def tile(index, carry, out_ref, start):
        rows = pl.ds(pl.multiple_of(index * ROWS, ROWS), ROWS)
        left = lhs_ref[pl.ds(pl.multiple_of(start + index * ROWS, ROWS), ROWS)]
        squared = jnp.dot(left, squares, preferred_element_type=F32)
        depth = jnp.dot(left, depths, preferred_element_type=F32)
        inverse = lax.rsqrt(squared)
        turns = (level + squared * inverse) * wavenumber
        part = turns - ((turns + ROUNDER) - ROUNDER)
        z = part * part
        sine = part * horner(SIN, z)
        cosine = horner(COS, z)
        double = depth * inverse * scale
        lean = double * sine
        out_ref[0, rows] = (0.5 * double - lean * sine).astype(BF16)
        out_ref[1, rows] = (lean * cosine).astype(BF16)
        return carry

    share = upper.shape[1]
    lax.fori_loop(0, (channels - share) // ROWS, functools.partial(tile, out_ref=lower, start=share), 0)
    copy = pltpu.make_async_copy(lower, lower_ref, sems.at[3])
    copy.start()
    lax.fori_loop(0, share // ROWS, functools.partial(tile, out_ref=upper, start=0), 0)
    copy.wait()


def arrange(samples, data):
    blocks, bins, _, group, width = samples.shape
    half = bins * group
    for k in range(blocks):
        for part in range(2):
            data[part * half : (part + 1) * half, k * width : (k + 1) * width] = samples[k, :, part].reshape(half, width)


def applied(data, operator, lanes):
    return [jnp.dot(data, operator[which, :, lanes], preferred_element_type=F32) for which in range(2)]


def joined(first, second):
    half = first.shape[0] // 2
    return (first[:half] + second[half:]).astype(BF16), (first[half:] - second[:half]).astype(BF16)


def own_kernel(upper, lower_ref, samples, out_ref, lower, data, partial, sem):
    copy = pltpu.make_async_copy(lower_ref, lower, sem)
    copy.start()
    arrange(samples, data)
    half = out_ref.shape[0] // 2
    share = upper.shape[1]
    blocks = [slice(n, n + LANES) for n in range(0, upper.shape[2], LANES)]
    for lanes in blocks:
        first, second = applied(data[:, :share], upper, lanes)
        partial[0, :, lanes] = first
        partial[1, :, lanes] = second
    copy.wait()
    for lanes in blocks:
        first, second = applied(data[:, share:], lower, lanes)
        out_ref[:half, lanes], out_ref[half:, lanes] = joined(
            partial[0, :, lanes] + first, partial[1, :, lanes] + second
        )


def other_kernel(upper, lower, samples, own, y_ref, keep_ref, send_ref, data, gram):
    core = lax.axis_index("core")
    frames = y_ref.shape[0] // 2
    half = frames // CORES
    here = pl.multiple_of(core * half, half)
    there = pl.multiple_of((1 - core) * half, half)
    y_ref[pl.ds(here, half)] = own[:half]
    y_ref[pl.ds(frames + here, half)] = own[half:]
    arrange(samples, data)
    share = upper.shape[1]
    for n in range(0, upper.shape[2], LANES):
        lanes = slice(n, n + LANES)
        first, second = applied(data[:, :share], upper, lanes)
        more, further = applied(data[:, share:], lower, lanes)
        y_ref[pl.ds(there, half), lanes], y_ref[pl.ds(frames + there, half), lanes] = joined(
            first + more, second + further
        )
    y = y_ref[...]
    products = lax.dot_general(y, y, (((1,), (1,)), ((), ())), preferred_element_type=F32)
    gram[...] = (products[:frames, :frames] + products[frames:, frames:]) + (
        products[:frames, frames:] - products[frames:, :frames]
    )
    keep_ref[...] = gram[pl.ds(here, half), :]
    send_ref[...] = gram[pl.ds(there, half), :]


def halves(x):
    high = x.astype(BF16)
    return high, (x - high.astype(F32)).astype(BF16)


def product(left, right):
    left_high, left_low = halves(left)
    right_high, right_low = halves(right)
    return jnp.dot(
        jnp.concatenate([left_high, left_high, left_low], axis=1),
        jnp.concatenate([right_high, right_low, right_high], axis=0),
        preferred_element_type=F32,
    )


def unpack(packed):
    flipped = jnp.transpose(packed)
    return 0.5 * (packed + flipped), 0.5 * (packed - flipped), flipped


def filter_kernel(own, other, y_ref, out_ref, gram):
    core = lax.axis_index("core")
    half, frames = own.shape
    gram[pl.ds(pl.multiple_of(core * half, half), half), :] = own[...]
    gram[pl.ds(pl.multiple_of((1 - core) * half, half), half), :] = other[...]
    packed = gram[...]
    squares = jnp.sum(packed * packed)
    factor = 4.0 / jnp.sqrt(jnp.full((1, 1), squares + EPSILON, F32))
    mat = packed * factor
    real, imag, flipped = unpack(mat)
    left = jnp.concatenate([real, imag], axis=1)
    second = product(left, jnp.concatenate([mat, flipped], axis=0))
    third = product(left, jnp.concatenate([second, jnp.transpose(second)], axis=0))
    rows = lax.broadcasted_iota(jnp.int32, (frames, frames), 0)
    cols = lax.broadcasted_iota(jnp.int32, (frames, frames), 1)
    identity = jnp.where(rows == cols, 1.0, 0.0).astype(F32)
    real, imag, _ = unpack(identity - mat + 0.3 * second - 0.03 * third)
    real, imag = real.astype(BF16), imag.astype(BF16)
    matrix = jnp.concatenate(
        [jnp.concatenate([real, imag], axis=1), jnp.concatenate([-imag, real], axis=1)], axis=0
    )
    applied = jnp.dot(matrix, y_ref[...], preferred_element_type=F32).astype(BF16)
    group = out_ref.shape[2]
    bins = out_ref.shape[0] // CORES
    for part in range(2):
        for c in range(CORES):
            for j in range(bins):
                row = part * frames + c * half + j * group
                out_ref[j * CORES + c, part] = applied[row : row + group]


def place_kernel(got, out_ref):
    group, _, bins, _ = out_ref.shape
    voxels = got.shape[-1]
    size = group * bins
    rows = lax.broadcasted_iota(jnp.int32, (size, size), 0)
    cols = lax.broadcasted_iota(jnp.int32, (size, size), 1)
    turn = jnp.where(cols == (rows % bins) * group + rows // bins, 1.0, 0.0).astype(BF16)
    for c in range(CORES):
        for part in range(2):
            block = got[:, c, part].reshape(size, voxels)
            moved = jnp.dot(turn, block, preferred_element_type=F32).astype(BF16)
            out_ref[:, part, :, c * voxels : (c + 1) * voxels] = moved.reshape(group, bins, voxels)


def shards(rf_data, elem_pos, vox_pos, subbands):
    parts, bins, group, width = rf_data.shape
    channels = elem_pos.shape[1]
    chans = channels // width
    voxels = vox_pos.shape[1] // CORES
    frames = group * bins * CORES
    half = frames // CORES

    def shape(*dims, dtype=BF16):
        return jax.ShapeDtypeStruct(dims, dtype)

    def swap(x):
        return lax.ppermute(x, "core", [(0, 1), (1, 0)])

    def across(x, bits):
        return lax.ppermute(x, "chan", [(a, a ^ bits) for a in range(chans)])

    by_bin = pl.pallas_call(
        spread_kernel,
        name="spread",
        out_shape=shape(chans, bins, parts, group, width),
        in_specs=[HBM],
        out_specs=VMEM,
        scratch_shapes=[pltpu.VMEM(rf_data.shape, BF16), pltpu.SemaphoreType.DMA],
        compiler_params=WIDE,
    )(pltpu.with_memory_space_constraint(rf_data, pltpu.HBM))
    by_bin = by_bin.reshape(chans * bins, parts, group, width)
    own = lax.all_to_all(by_bin, ("chan", "bin"), split_axis=0, concat_axis=0, tiled=True)

    share = channels // 2
    upper, lower = pl.pallas_call(
        operator_kernel,
        name="operator",
        out_shape=(shape(2, share, voxels), pltpu.HBM((2, channels - share, voxels), BF16)),
        in_specs=[HBM, HBM, HBM],
        out_specs=(VMEM, HBM),
        scratch_shapes=[
            pltpu.VMEM(elem_pos.shape, jnp.int32),
            pltpu.VMEM(vox_pos.shape, jnp.int32),
            pltpu.SMEM(subbands.shape, jnp.int32),
            pltpu.VMEM((channels, 8), BF16),
            pltpu.VMEM((2, channels - share, voxels), BF16),
            pltpu.SemaphoreType.DMA((4,)),
        ],
        compiler_params=WIDE,
        cost_estimate=pl.CostEstimate(
            flops=60 * channels * voxels,
            transcendentals=channels * voxels,
            bytes_accessed=4 * channels * voxels,
        ),
    )(*(pltpu.with_memory_space_constraint(x, pltpu.HBM) for x in (elem_pos, vox_pos, subbands)))

    own, upper, lower = lax.optimization_barrier((own, upper, lower))
    other = swap(own)
    own = own.reshape(chans, bins, parts, group, width)
    other = other.reshape(chans, bins, parts, group, width)

    beam_cost = pl.CostEstimate(
        flops=8 * half * channels * voxels * 2, transcendentals=0, bytes_accessed=4 * channels * voxels
    )
    mine, lower = pl.pallas_call(
        own_kernel,
        name="beam_own",
        out_shape=(shape(frames, voxels), shape(2, channels - share, voxels)),
        in_specs=[VMEM, HBM, VMEM],
        out_specs=(VMEM, VMEM),
        scratch_shapes=[
            pltpu.VMEM((frames, channels), BF16),
            pltpu.VMEM((2, frames, voxels), F32),
            pltpu.SemaphoreType.DMA,
        ],
        compiler_params=WIDE,
        cost_estimate=beam_cost,
    )(upper, pltpu.with_memory_space_constraint(lower, pltpu.HBM), own)
    y, keep, send = pl.pallas_call(
        other_kernel,
        name="beam_other",
        out_shape=(shape(2 * frames, voxels), shape(half, frames, dtype=F32), shape(half, frames, dtype=F32)),
        in_specs=[VMEM, VMEM, VMEM, VMEM],
        out_specs=(VMEM, VMEM, VMEM),
        scratch_shapes=[pltpu.VMEM((frames, channels), BF16), pltpu.VMEM((frames, frames), F32)],
        compiler_params=WIDE,
        cost_estimate=beam_cost,
    )(upper, lower, other, mine)

    total = keep + swap(send)
    near, far, next_to = across(total, 1), across(total, 3), across(total, 2)
    total = total + near + far + next_to
    total = total + across(total, 4)
    rest = swap(total)

    applied = pl.pallas_call(
        filter_kernel,
        name="filter",
        out_shape=shape(bins * CORES, parts, group, voxels),
        in_specs=[VMEM, VMEM, VMEM],
        out_specs=VMEM,
        scratch_shapes=[pltpu.VMEM((frames, frames), F32)],
        compiler_params=WIDE,
    )(total, rest, y)

    got = lax.all_to_all(applied, ("bin", "core"), split_axis=0, concat_axis=0, tiled=True)
    got = got.reshape(bins, CORES, parts, group, voxels)
    return pl.pallas_call(
        place_kernel,
        name="place",
        out_shape=shape(group, parts, bins, CORES * voxels),
        in_specs=[VMEM],
        out_specs=VMEM,
        compiler_params=WIDE,
    )(got)


def solution(mesh):
    chans = mesh.shape["chan"]
    fine = Mesh(mesh.devices.reshape(chans, BINS, CORES), ("chan", "bin", "core"))
    return jax.shard_map(
        shards,
        mesh=fine,
        in_specs=(P(None, None, ("bin", "core"), "chan"), P(), P(None, "chan"), P()),
        out_specs=P(("bin", "core"), None, None, "chan"),
        check_vma=False,
    )
```

```python
import functools
import math

import jax
import jax.numpy as jnp
from jax import lax
from jax.experimental import pallas as pl
from jax.experimental.pallas import tpu as pltpu
from jax.sharding import Mesh, PartitionSpec as P

EPSILON = 1e-06
BINS = 8
CORES = 2
F32 = jnp.float32
BF16 = jnp.bfloat16
SIN = (3.1415925800446924, -5.167706878924515, 2.5500313772531213, -0.5980451739748806, 0.0772201286897368)
COS = (0.9999999534666272, -4.934792858670076, 4.058411914063177, -1.331880160583308, 0.21969679727234584)
ROUNDER = 12582912.0
ROWS = 256
LANES = 256
WIDE = pltpu.CompilerParams(vmem_limit_bytes=16 * 1024 * 1024)
VMEM = pl.BlockSpec(memory_space=pltpu.VMEM)
HBM = pl.BlockSpec(memory_space=pltpu.HBM)


def horner(coefficients, z):
    total = coefficients[-1] * z + coefficients[-2]
    for value in coefficients[-3::-1]:
        total = total * z + value
    return total


def digits(value, unit):
    high = jnp.floor(value * (1.0 / unit))
    return high, value - unit * high


def spread_kernel(rf_ref, out_ref, held, sems):
    parts, bins = held.shape[:2]
    chans = out_ref.shape[0] // bins
    copy = pltpu.make_async_copy(rf_ref, held, sems.at[chans * parts])
    copy.start()
    copy.wait()
    copies = [
        pltpu.make_async_copy(held.at[part], out_ref.at[k * bins : (k + 1) * bins, part], sems.at[k * parts + part])
        for k in range(chans)
        for part in range(parts)
    ]
    for copy in copies:
        copy.start()
    for copy in copies:
        copy.wait()


def operator_kernel(elem_ref, vox_ref, bins_ref, upper, lower_ref, elem, vox, bins, lhs_ref, lower, sems):
    core = lax.axis_index("core")
    voxels = upper.shape[2]
    channels = elem.shape[1]
    copies = [
        pltpu.make_async_copy(source, target, sems.at[n])
        for n, (source, target) in enumerate(((elem_ref, elem), (vox_ref, vox), (bins_ref, bins)))
    ]
    for copy in copies:
        copy.start()
    for copy in copies:
        copy.wait()
    wavenumber = (32.0 + bins[lax.axis_index("bin")].astype(F32)) / 64.0
    scale = 2.0 / math.sqrt(channels)

    place = elem[...].astype(F32)
    high, low = digits(jnp.sum(place * place, axis=0, keepdims=True), 16.0)
    one = jnp.ones((1, channels), F32)
    lhs = jnp.concatenate([place, high, low, one, one, 0.0 * one], axis=0)
    lhs_ref[...] = jnp.transpose(lhs).astype(BF16)
    voxel = vox[:, pl.ds(pl.multiple_of(core * voxels, voxels), voxels)].astype(F32)
    high, low = digits(jnp.sum(voxel * voxel, axis=0, keepdims=True), 64.0)
    one = jnp.ones((1, voxels), F32)
    zero = 0.0 * one
    level = voxel[2:3]
    squares = jnp.concatenate([-2.0 * voxel, 16.0 * one, one, 64.0 * high, low, zero], axis=0).astype(BF16)
    depths = jnp.concatenate([zero, zero, -1.0 * one, zero, zero, level, zero, zero], axis=0).astype(BF16)

    def tile(index, carry, out_ref, start):
        rows = pl.ds(pl.multiple_of(index * ROWS, ROWS), ROWS)
        left = lhs_ref[pl.ds(pl.multiple_of(start + index * ROWS, ROWS), ROWS)]
        squared = jnp.dot(left, squares, preferred_element_type=F32)
        depth = jnp.dot(left, depths, preferred_element_type=F32)
        inverse = lax.rsqrt(squared)
        turns = (level + squared * inverse) * wavenumber
        part = turns - ((turns + ROUNDER) - ROUNDER)
        z = part * part
        sine = part * horner(SIN, z)
        cosine = horner(COS, z)
        double = depth * inverse * scale
        lean = double * sine
        out_ref[0, rows] = (0.5 * double - lean * sine).astype(BF16)
        out_ref[1, rows] = (lean * cosine).astype(BF16)
        return carry

    share = upper.shape[1]
    lax.fori_loop(0, (channels - share) // ROWS, functools.partial(tile, out_ref=lower, start=share), 0)
    copy = pltpu.make_async_copy(lower, lower_ref, sems.at[3])
    copy.start()
    lax.fori_loop(0, share // ROWS, functools.partial(tile, out_ref=upper, start=0), 0)
    copy.wait()


def arrange(samples, data):
    blocks, bins, _, group, width = samples.shape
    half = bins * group
    for k in range(blocks):
        for part in range(2):
            data[part * half : (part + 1) * half, k * width : (k + 1) * width] = samples[k, :, part].reshape(half, width)


def applied(data, operator, lanes):
    return [jnp.dot(data, operator[which, :, lanes], preferred_element_type=F32) for which in range(2)]


def joined(first, second):
    half = first.shape[0] // 2
    return (first[:half] + second[half:]).astype(BF16), (first[half:] - second[:half]).astype(BF16)


def own_kernel(upper, lower_ref, samples, out_ref, lower, data, partial, sem):
    copy = pltpu.make_async_copy(lower_ref, lower, sem)
    copy.start()
    arrange(samples, data)
    half = out_ref.shape[0] // 2
    share = upper.shape[1]
    blocks = [slice(n, n + LANES) for n in range(0, upper.shape[2], LANES)]
    for lanes in blocks:
        first, second = applied(data[:, :share], upper, lanes)
        partial[0, :, lanes] = first
        partial[1, :, lanes] = second
    copy.wait()
    for lanes in blocks:
        first, second = applied(data[:, share:], lower, lanes)
        out_ref[:half, lanes], out_ref[half:, lanes] = joined(
            partial[0, :, lanes] + first, partial[1, :, lanes] + second
        )


def other_kernel(upper, lower, samples, own, y_ref, keep_ref, send_ref, data, gram):
    core = lax.axis_index("core")
    frames = y_ref.shape[0] // 2
    half = frames // CORES
    here = pl.multiple_of(core * half, half)
    there = pl.multiple_of((1 - core) * half, half)
    y_ref[pl.ds(here, half)] = own[:half]
    y_ref[pl.ds(frames + here, half)] = own[half:]
    arrange(samples, data)
    share = upper.shape[1]
    for n in range(0, upper.shape[2], LANES):
        lanes = slice(n, n + LANES)
        first, second = applied(data[:, :share], upper, lanes)
        more, further = applied(data[:, share:], lower, lanes)
        y_ref[pl.ds(there, half), lanes], y_ref[pl.ds(frames + there, half), lanes] = joined(
            first + more, second + further
        )
    y = y_ref[...]
    products = lax.dot_general(y, y, (((1,), (1,)), ((), ())), preferred_element_type=F32)
    gram[...] = (products[:frames, :frames] + products[frames:, frames:]) + (
        products[:frames, frames:] - products[frames:, :frames]
    )
    keep_ref[...] = gram[pl.ds(here, half), :]
    send_ref[...] = gram[pl.ds(there, half), :]


def halves(x):
    high = x.astype(BF16)
    return high, (x - high.astype(F32)).astype(BF16)


def product(left, right):
    left_high, left_low = halves(left)
    right_high, right_low = halves(right)
    return jnp.dot(
        jnp.concatenate([left_high, left_high, left_low], axis=1),
        jnp.concatenate([right_high, right_low, right_high], axis=0),
        preferred_element_type=F32,
    )


def unpack(packed):
    flipped = jnp.transpose(packed)
    return 0.5 * (packed + flipped), 0.5 * (packed - flipped), flipped


def filter_kernel(own, other, y_ref, out_ref, gram):
    core = lax.axis_index("core")
    half, frames = own.shape
    gram[pl.ds(pl.multiple_of(core * half, half), half), :] = own[...]
    gram[pl.ds(pl.multiple_of((1 - core) * half, half), half), :] = other[...]
    packed = gram[...]
    squares = jnp.sum(packed * packed)
    factor = 4.0 / jnp.sqrt(jnp.full((1, 1), squares + EPSILON, F32))
    mat = packed * factor
    real, imag, flipped = unpack(mat)
    left = jnp.concatenate([real, imag], axis=1)
    second = product(left, jnp.concatenate([mat, flipped], axis=0))
    third = product(left, jnp.concatenate([second, jnp.transpose(second)], axis=0))
    rows = lax.broadcasted_iota(jnp.int32, (frames, frames), 0)
    cols = lax.broadcasted_iota(jnp.int32, (frames, frames), 1)
    identity = jnp.where(rows == cols, 1.0, 0.0).astype(F32)
    real, imag, _ = unpack(identity - mat + 0.3 * second - 0.03 * third)
    real, imag = real.astype(BF16), imag.astype(BF16)
    matrix = jnp.concatenate(
        [jnp.concatenate([real, imag], axis=1), jnp.concatenate([-imag, real], axis=1)], axis=0
    )
    applied = jnp.dot(matrix, y_ref[...], preferred_element_type=F32).astype(BF16)
    group = out_ref.shape[2]
    bins = out_ref.shape[0] // CORES
    for part in range(2):
        for c in range(CORES):
            for j in range(bins):
                row = part * frames + c * half + j * group
                out_ref[j * CORES + c, part] = applied[row : row + group]


def place_kernel(got, out_ref):
    group, _, bins, _ = out_ref.shape
    voxels = got.shape[-1]
    size = group * bins
    rows = lax.broadcasted_iota(jnp.int32, (size, size), 0)
    cols = lax.broadcasted_iota(jnp.int32, (size, size), 1)
    turn = jnp.where(cols == (rows % bins) * group + rows // bins, 1.0, 0.0).astype(BF16)
    for c in range(CORES):
        for part in range(2):
            block = got[:, c, part].reshape(size, voxels)
            moved = jnp.dot(turn, block, preferred_element_type=F32).astype(BF16)
            out_ref[:, part, :, c * voxels : (c + 1) * voxels] = moved.reshape(group, bins, voxels)


def shards(rf_data, elem_pos, vox_pos, subbands):
    parts, bins, group, width = rf_data.shape
    channels = elem_pos.shape[1]
    chans = channels // width
    voxels = vox_pos.shape[1] // CORES
    frames = group * bins * CORES
    half = frames // CORES

    def shape(*dims, dtype=BF16):
        return jax.ShapeDtypeStruct(dims, dtype)

    def swap(x):
        return lax.ppermute(x, "core", [(0, 1), (1, 0)])

    def across(x, bits):
        return lax.ppermute(x, "chan", [(a, a ^ bits) for a in range(chans)])

    by_bin = pl.pallas_call(
        spread_kernel,
        name="spread",
        out_shape=shape(chans * bins, parts, group, width),
        in_specs=[HBM],
        out_specs=HBM,
        scratch_shapes=[pltpu.VMEM(rf_data.shape, BF16), pltpu.SemaphoreType.DMA((chans * parts + 1,))],
        compiler_params=WIDE,
    )(pltpu.with_memory_space_constraint(rf_data, pltpu.HBM))
    own = lax.all_to_all(by_bin, ("chan", "bin"), split_axis=0, concat_axis=0, tiled=True)

    share = channels // 2
    upper, lower = pl.pallas_call(
        operator_kernel,
        name="operator",
        out_shape=(shape(2, share, voxels), pltpu.HBM((2, channels - share, voxels), BF16)),
        in_specs=[HBM, HBM, HBM],
        out_specs=(VMEM, HBM),
        scratch_shapes=[
            pltpu.VMEM(elem_pos.shape, jnp.int32),
            pltpu.VMEM(vox_pos.shape, jnp.int32),
            pltpu.SMEM(subbands.shape, jnp.int32),
            pltpu.VMEM((channels, 8), BF16),
            pltpu.VMEM((2, channels - share, voxels), BF16),
            pltpu.SemaphoreType.DMA((4,)),
        ],
        compiler_params=WIDE,
        cost_estimate=pl.CostEstimate(
            flops=60 * channels * voxels,
            transcendentals=channels * voxels,
            bytes_accessed=4 * channels * voxels,
        ),
    )(*(pltpu.with_memory_space_constraint(x, pltpu.HBM) for x in (elem_pos, vox_pos, subbands)))

    own, upper, lower = lax.optimization_barrier((own, upper, lower))
    other = swap(own)
    own = own.reshape(chans, bins, parts, group, width)
    other = other.reshape(chans, bins, parts, group, width)

    beam_cost = pl.CostEstimate(
        flops=8 * half * channels * voxels * 2, transcendentals=0, bytes_accessed=4 * channels * voxels
    )
    mine, lower = pl.pallas_call(
        own_kernel,
        name="beam_own",
        out_shape=(shape(frames, voxels), shape(2, channels - share, voxels)),
        in_specs=[VMEM, HBM, VMEM],
        out_specs=(VMEM, VMEM),
        scratch_shapes=[
            pltpu.VMEM((frames, channels), BF16),
            pltpu.VMEM((2, frames, voxels), F32),
            pltpu.SemaphoreType.DMA,
        ],
        compiler_params=WIDE,
        cost_estimate=beam_cost,
    )(upper, pltpu.with_memory_space_constraint(lower, pltpu.HBM), own)
    y, keep, send = pl.pallas_call(
        other_kernel,
        name="beam_other",
        out_shape=(shape(2 * frames, voxels), shape(half, frames, dtype=F32), shape(half, frames, dtype=F32)),
        in_specs=[VMEM, VMEM, VMEM, VMEM],
        out_specs=(VMEM, VMEM, VMEM),
        scratch_shapes=[pltpu.VMEM((frames, channels), BF16), pltpu.VMEM((frames, frames), F32)],
        compiler_params=WIDE,
        cost_estimate=beam_cost,
    )(upper, lower, other, mine)

    total = keep + swap(send)
    narrow = total.astype(BF16)
    total = total + sum(across(narrow, bits).astype(F32) for bits in (1, 3, 2))
    total = total + across(total.astype(BF16), 4).astype(F32)
    rest = swap(total)

    applied = pl.pallas_call(
        filter_kernel,
        name="filter",
        out_shape=shape(bins * CORES, parts, group, voxels),
        in_specs=[VMEM, VMEM, VMEM],
        out_specs=VMEM,
        scratch_shapes=[pltpu.VMEM((frames, frames), F32)],
        compiler_params=WIDE,
    )(total, rest, y)

    got = lax.all_to_all(applied, ("bin", "core"), split_axis=0, concat_axis=0, tiled=True)
    got = got.reshape(bins, CORES, parts, group, voxels)
    return pl.pallas_call(
        place_kernel,
        name="place",
        out_shape=shape(group, parts, bins, CORES * voxels),
        in_specs=[VMEM],
        out_specs=VMEM,
        compiler_params=WIDE,
    )(got)


def solution(mesh):
    chans = mesh.shape["chan"]
    fine = Mesh(mesh.devices.reshape(chans, BINS, CORES), ("chan", "bin", "core"))
    return jax.shard_map(
        shards,
        mesh=fine,
        in_specs=(P(None, None, ("bin", "core"), "chan"), P(), P(None, "chan"), P()),
        out_specs=P(("bin", "core"), None, None, "chan"),
        check_vma=False,
    )
```

```python
import functools
import math

import jax
import jax.numpy as jnp
from jax import lax
from jax.experimental import pallas as pl
from jax.experimental.pallas import tpu as pltpu
from jax.sharding import Mesh, PartitionSpec as P

EPSILON = 1e-06
BINS = 8
CORES = 2
F32 = jnp.float32
BF16 = jnp.bfloat16
SIN = (3.1415925800446924, -5.167706878924515, 2.5500313772531213, -0.5980451739748806, 0.0772201286897368)
COS = (0.9999999534666272, -4.934792858670076, 4.058411914063177, -1.331880160583308, 0.21969679727234584)
ROUNDER = 12582912.0
ROWS = 512
LANES = 256
WIDE = pltpu.CompilerParams(vmem_limit_bytes=16 * 1024 * 1024)
VMEM = pl.BlockSpec(memory_space=pltpu.VMEM)
HBM = pl.BlockSpec(memory_space=pltpu.HBM)


def horner(coefficients, z):
    total = coefficients[-1] * z + coefficients[-2]
    for value in coefficients[-3::-1]:
        total = total * z + value
    return total


def digits(value, unit):
    high = jnp.floor(value * (1.0 / unit))
    return high, value - unit * high


def spread_kernel(rf_ref, out_ref, held, sems):
    parts, bins = held.shape[:2]
    chans = out_ref.shape[0] // bins
    copy = pltpu.make_async_copy(rf_ref, held, sems.at[chans * parts])
    copy.start()
    copy.wait()
    copies = [
        pltpu.make_async_copy(held.at[part], out_ref.at[k * bins : (k + 1) * bins, part], sems.at[k * parts + part])
        for k in range(chans)
        for part in range(parts)
    ]
    for copy in copies:
        copy.start()
    for copy in copies:
        copy.wait()


def operator_kernel(elem_ref, vox_ref, bins_ref, upper, lower_ref, elem, vox, bins, lhs_ref, lower, sems):
    core = lax.axis_index("core")
    channels = elem.shape[1]
    share = upper.shape[2]
    voxels = share + lower.shape[2]
    copies = [
        pltpu.make_async_copy(source, target, sems.at[n])
        for n, (source, target) in enumerate(((elem_ref, elem), (vox_ref, vox), (bins_ref, bins)))
    ]
    for copy in copies:
        copy.start()
    for copy in copies:
        copy.wait()
    wavenumber = (32.0 + bins[lax.axis_index("bin")].astype(F32)) / 64.0
    scale = 2.0 / math.sqrt(channels)

    place = elem[...].astype(F32)
    high, low = digits(jnp.sum(place * place, axis=0, keepdims=True), 16.0)
    one = jnp.ones((1, channels), F32)
    lhs = jnp.concatenate([place, high, low, one, one, 0.0 * one], axis=0)
    lhs_ref[...] = jnp.transpose(lhs).astype(BF16)
    voxel = vox[:, pl.ds(pl.multiple_of(core * voxels, voxels), voxels)].astype(F32)
    high, low = digits(jnp.sum(voxel * voxel, axis=0, keepdims=True), 64.0)
    one = jnp.ones((1, voxels), F32)
    zero = 0.0 * one
    level = voxel[2:3]
    squares = jnp.concatenate([-2.0 * voxel, 16.0 * one, one, 64.0 * high, low, zero], axis=0).astype(BF16)
    depths = jnp.concatenate([zero, zero, -1.0 * one, zero, zero, level, zero, zero], axis=0).astype(BF16)

    def tile(index, carry, out_ref, lanes):
        rows = pl.ds(pl.multiple_of(index * ROWS, ROWS), ROWS)
        left = lhs_ref[rows]
        squared = jnp.dot(left, squares[:, lanes], preferred_element_type=F32)
        depth = jnp.dot(left, depths[:, lanes], preferred_element_type=F32)
        inverse = lax.rsqrt(squared)
        turns = (level[:, lanes] + squared * inverse) * wavenumber
        part = turns - ((turns + ROUNDER) - ROUNDER)
        z = part * part
        sine = part * horner(SIN, z)
        cosine = horner(COS, z)
        double = depth * inverse * scale
        lean = double * sine
        out_ref[0, rows] = (0.5 * double - lean * sine).astype(BF16)
        out_ref[1, rows] = (lean * cosine).astype(BF16)
        return carry

    lax.fori_loop(0, channels // ROWS, functools.partial(tile, out_ref=lower, lanes=slice(share, voxels)), 0)
    copy = pltpu.make_async_copy(lower, lower_ref, sems.at[3])
    copy.start()
    lax.fori_loop(0, channels // ROWS, functools.partial(tile, out_ref=upper, lanes=slice(0, share)), 0)
    copy.wait()


def arrange(samples, data):
    blocks, bins, _, group, width = samples.shape
    half = bins * group
    for k in range(blocks):
        for part in range(2):
            data[part * half : (part + 1) * half, k * width : (k + 1) * width] = samples[k, :, part].reshape(half, width)


def beamform(data, operator, start):
    half = data.shape[0] // 2
    for n in range(0, operator.shape[2], LANES):
        first, second = (
            jnp.dot(data[...], operator[which, :, n : n + LANES], preferred_element_type=F32) for which in range(2)
        )
        real = (first[:half] + second[half:]).astype(BF16)
        imag = (first[half:] - second[:half]).astype(BF16)
        yield slice(start + n, start + n + LANES), real, imag


def own_kernel(upper, lower_ref, samples, out_ref, lower, data, sem):
    copy = pltpu.make_async_copy(lower_ref, lower, sem)
    copy.start()
    arrange(samples, data)
    half = out_ref.shape[0] // 2
    for lanes, real, imag in beamform(data, upper, 0):
        out_ref[:half, lanes], out_ref[half:, lanes] = real, imag
    copy.wait()
    for lanes, real, imag in beamform(data, lower, upper.shape[2]):
        out_ref[:half, lanes], out_ref[half:, lanes] = real, imag


def other_kernel(upper, lower, samples, own, y_ref, keep_ref, send_ref, data, gram):
    core = lax.axis_index("core")
    frames = y_ref.shape[0] // 2
    half = frames // CORES
    here = pl.multiple_of(core * half, half)
    there = pl.multiple_of((1 - core) * half, half)
    y_ref[pl.ds(here, half)] = own[:half]
    y_ref[pl.ds(frames + here, half)] = own[half:]
    arrange(samples, data)
    for operator, start in ((upper, 0), (lower, upper.shape[2])):
        for lanes, real, imag in beamform(data, operator, start):
            y_ref[pl.ds(there, half), lanes], y_ref[pl.ds(frames + there, half), lanes] = real, imag
    y = y_ref[...]
    products = lax.dot_general(y, y, (((1,), (1,)), ((), ())), preferred_element_type=F32)
    gram[...] = (products[:frames, :frames] + products[frames:, frames:]) + (
        products[:frames, frames:] - products[frames:, :frames]
    )
    keep_ref[...] = gram[pl.ds(here, half), :]
    send_ref[...] = gram[pl.ds(there, half), :]


def halves(x):
    high = x.astype(BF16)
    return high, (x - high.astype(F32)).astype(BF16)


def product(left, right):
    left_high, left_low = halves(left)
    right_high, right_low = halves(right)
    return jnp.dot(
        jnp.concatenate([left_high, left_high, left_low], axis=1),
        jnp.concatenate([right_high, right_low, right_high], axis=0),
        preferred_element_type=F32,
    )


def unpack(packed):
    flipped = jnp.transpose(packed)
    return 0.5 * (packed + flipped), 0.5 * (packed - flipped), flipped


def filter_kernel(own, other, y_ref, peer_ref, out_ref, gram, kept):
    core = lax.axis_index("core")
    half, frames = own.shape
    gram[pl.ds(pl.multiple_of(core * half, half), half), :] = own[...]
    gram[pl.ds(pl.multiple_of((1 - core) * half, half), half), :] = other[...]
    packed = gram[...]
    squares = jnp.sum(packed * packed)
    factor = 4.0 / jnp.sqrt(jnp.full((1, 1), squares + EPSILON, F32))
    mat = packed * factor
    real, imag, flipped = unpack(mat)
    left = jnp.concatenate([real, imag], axis=1)
    second = product(left, jnp.concatenate([mat, flipped], axis=0))
    third = product(left, jnp.concatenate([second, jnp.transpose(second)], axis=0))
    rows = lax.broadcasted_iota(jnp.int32, (frames, frames), 0)
    cols = lax.broadcasted_iota(jnp.int32, (frames, frames), 1)
    identity = jnp.where(rows == cols, 1.0, 0.0).astype(F32)
    real, imag, _ = unpack(identity - mat + 0.3 * second - 0.03 * third)
    kept[0] = real.astype(BF16)
    kept[1] = imag.astype(BF16)
    real, imag = (kept[part, pl.ds(pl.multiple_of(core * half, half), half)] for part in range(2))
    matrix = jnp.concatenate(
        [jnp.concatenate([real, imag], axis=1), jnp.concatenate([-imag, real], axis=1)], axis=0
    )
    bins, parts, group, _ = out_ref.shape
    voxels = y_ref.shape[1]
    for source, place in ((y_ref, core), (peer_ref, 1 - core)):
        lanes = pl.ds(pl.multiple_of(place * voxels, voxels), voxels)
        applied = jnp.dot(matrix, source[...], preferred_element_type=F32).astype(BF16)
        for part in range(parts):
            for j in range(bins):
                row = part * half + j * group
                out_ref[j, part, :, lanes] = applied[row : row + group]


def place_kernel(got, out_ref):
    bins, parts, group, voxels = got.shape
    size = group * bins
    rows = lax.broadcasted_iota(jnp.int32, (size, size), 0)
    cols = lax.broadcasted_iota(jnp.int32, (size, size), 1)
    turn = jnp.where(cols == (rows % bins) * group + rows // bins, 1.0, 0.0).astype(BF16)
    for part in range(parts):
        moved = jnp.dot(turn, got[:, part].reshape(size, voxels), preferred_element_type=F32).astype(BF16)
        out_ref[:, part] = moved.reshape(group, bins, voxels)


def shards(rf_data, elem_pos, vox_pos, subbands):
    parts, bins, group, width = rf_data.shape
    channels = elem_pos.shape[1]
    chans = channels // width
    voxels = vox_pos.shape[1] // CORES
    frames = group * bins * CORES
    half = frames // CORES

    def shape(*dims, dtype=BF16):
        return jax.ShapeDtypeStruct(dims, dtype)

    def swap(x):
        return lax.ppermute(x, "core", [(0, 1), (1, 0)])

    def across(x, bits):
        return lax.ppermute(x, "chan", [(a, a ^ bits) for a in range(chans)])

    by_bin = pl.pallas_call(
        spread_kernel,
        name="spread",
        out_shape=shape(chans * bins, parts, group, width),
        in_specs=[HBM],
        out_specs=HBM,
        scratch_shapes=[pltpu.VMEM(rf_data.shape, BF16), pltpu.SemaphoreType.DMA((chans * parts + 1,))],
        compiler_params=WIDE,
    )(pltpu.with_memory_space_constraint(rf_data, pltpu.HBM))
    own = lax.all_to_all(by_bin, ("chan", "bin"), split_axis=0, concat_axis=0, tiled=True)

    share = voxels // 2
    upper, lower = pl.pallas_call(
        operator_kernel,
        name="operator",
        out_shape=(shape(2, channels, share), pltpu.HBM((2, channels, voxels - share), BF16)),
        in_specs=[HBM, HBM, HBM],
        out_specs=(VMEM, HBM),
        scratch_shapes=[
            pltpu.VMEM(elem_pos.shape, jnp.int32),
            pltpu.VMEM(vox_pos.shape, jnp.int32),
            pltpu.SMEM(subbands.shape, jnp.int32),
            pltpu.VMEM((channels, 8), BF16),
            pltpu.VMEM((2, channels, voxels - share), BF16),
            pltpu.SemaphoreType.DMA((4,)),
        ],
        compiler_params=WIDE,
        cost_estimate=pl.CostEstimate(
            flops=60 * channels * voxels,
            transcendentals=channels * voxels,
            bytes_accessed=4 * channels * voxels,
        ),
    )(*(pltpu.with_memory_space_constraint(x, pltpu.HBM) for x in (elem_pos, vox_pos, subbands)))

    own, upper, lower = lax.optimization_barrier((own, upper, lower))
    other = swap(own)
    own = own.reshape(chans, bins, parts, group, width)
    other = other.reshape(chans, bins, parts, group, width)

    beam_cost = pl.CostEstimate(
        flops=8 * half * channels * voxels * 2, transcendentals=0, bytes_accessed=4 * channels * voxels
    )
    mine, lower = pl.pallas_call(
        own_kernel,
        name="beam_own",
        out_shape=(shape(frames, voxels), shape(2, channels, voxels - share)),
        in_specs=[VMEM, HBM, VMEM],
        out_specs=(VMEM, VMEM),
        scratch_shapes=[
            pltpu.VMEM((frames, channels), BF16),
            pltpu.SemaphoreType.DMA,
        ],
        compiler_params=WIDE,
        cost_estimate=beam_cost,
    )(upper, pltpu.with_memory_space_constraint(lower, pltpu.HBM), own)
    y, keep, send = pl.pallas_call(
        other_kernel,
        name="beam_other",
        out_shape=(shape(2 * frames, voxels), shape(half, frames, dtype=F32), shape(half, frames, dtype=F32)),
        in_specs=[VMEM, VMEM, VMEM, VMEM],
        out_specs=(VMEM, VMEM, VMEM),
        scratch_shapes=[pltpu.VMEM((frames, channels), BF16), pltpu.VMEM((frames, frames), F32)],
        compiler_params=WIDE,
        cost_estimate=beam_cost,
    )(upper, lower, other, mine)

    total = keep + swap(send)
    total, y = lax.optimization_barrier((total, y))
    peer = swap(y)
    narrow = total.astype(BF16)
    total = total + sum(across(narrow, bits).astype(F32) for bits in (1, 3, 2))
    total = total + across(total.astype(BF16), 4).astype(F32)
    rest = swap(total)

    applied = pl.pallas_call(
        filter_kernel,
        name="filter",
        out_shape=shape(bins, parts, group, CORES * voxels),
        in_specs=[VMEM] * 4,
        out_specs=VMEM,
        scratch_shapes=[pltpu.VMEM((frames, frames), F32), pltpu.VMEM((2, frames, frames), BF16)],
        compiler_params=WIDE,
    )(total, rest, y, peer)

    got = lax.all_to_all(applied, "bin", split_axis=0, concat_axis=0, tiled=True)
    return pl.pallas_call(
        place_kernel,
        name="place",
        out_shape=shape(group, parts, bins, CORES * voxels),
        in_specs=[VMEM],
        out_specs=VMEM,
        compiler_params=WIDE,
    )(got)


def solution(mesh):
    chans = mesh.shape["chan"]
    fine = Mesh(mesh.devices.reshape(chans, BINS, CORES), ("chan", "bin", "core"))
    return jax.shard_map(
        shards,
        mesh=fine,
        in_specs=(P(None, None, ("bin", "core"), "chan"), P(), P(None, "chan"), P()),
        out_specs=P(("bin", "core"), None, None, "chan"),
        check_vma=False,
    )
```

```python
import functools
import math

import jax
import jax.numpy as jnp
from jax import lax
from jax.experimental import pallas as pl
from jax.experimental.pallas import tpu as pltpu
from jax.sharding import Mesh, PartitionSpec as P

EPSILON = 1e-06
BINS = 8
CORES = 2
F32 = jnp.float32
BF16 = jnp.bfloat16
SIN = (3.1415925800446924, -5.167706878924515, 2.5500313772531213, -0.5980451739748806, 0.0772201286897368)
COS = (0.9999999534666272, -4.934792858670076, 4.058411914063177, -1.331880160583308, 0.21969679727234584)
ROUNDER = 12582912.0
ROWS = 512
LANES = 256
PLACED = 512
WIDE = pltpu.CompilerParams(vmem_limit_bytes=16 * 1024 * 1024)
VMEM = pl.BlockSpec(memory_space=pltpu.VMEM)
HBM = pl.BlockSpec(memory_space=pltpu.HBM)


def horner(coefficients, z):
    total = coefficients[-1] * z + coefficients[-2]
    for value in coefficients[-3::-1]:
        total = total * z + value
    return total


def digits(value, unit):
    high = jnp.floor(value * (1.0 / unit))
    return high, value - unit * high


def spread_kernel(rf_ref, out_ref, held, sems):
    parts, bins = held.shape[:2]
    chans = out_ref.shape[0] // bins
    copy = pltpu.make_async_copy(rf_ref, held, sems.at[chans * parts])
    copy.start()
    copy.wait()
    copies = [
        pltpu.make_async_copy(held.at[part], out_ref.at[k * bins : (k + 1) * bins, part], sems.at[k * parts + part])
        for k in range(chans)
        for part in range(parts)
    ]
    for copy in copies:
        copy.start()
    for copy in copies:
        copy.wait()


def operator_kernel(elem_ref, vox_ref, bins_ref, upper, lower_ref, elem, vox, bins, lhs_ref, lower, sems):
    core = lax.axis_index("core")
    channels = elem.shape[1]
    share = upper.shape[2]
    voxels = share + lower.shape[2]
    copies = [
        pltpu.make_async_copy(source, target, sems.at[n])
        for n, (source, target) in enumerate(((elem_ref, elem), (vox_ref, vox), (bins_ref, bins)))
    ]
    for copy in copies:
        copy.start()
    for copy in copies:
        copy.wait()
    wavenumber = (32.0 + bins[lax.axis_index("bin")].astype(F32)) / 64.0
    scale = 2.0 / math.sqrt(channels)

    place = elem[...].astype(F32)
    high, low = digits(jnp.sum(place * place, axis=0, keepdims=True), 16.0)
    one = jnp.ones((1, channels), F32)
    lhs = jnp.concatenate([place, high, low, one, one, 0.0 * one], axis=0)
    lhs_ref[...] = jnp.transpose(lhs).astype(BF16)
    voxel = vox[:, pl.ds(pl.multiple_of(core * voxels, voxels), voxels)].astype(F32)
    high, low = digits(jnp.sum(voxel * voxel, axis=0, keepdims=True), 64.0)
    one = jnp.ones((1, voxels), F32)
    zero = 0.0 * one
    level = voxel[2:3]
    squares = jnp.concatenate([-2.0 * voxel, 16.0 * one, one, 64.0 * high, low, zero], axis=0).astype(BF16)
    depths = jnp.concatenate([zero, zero, -1.0 * one, zero, zero, level, zero, zero], axis=0).astype(BF16)

    def tile(index, carry, out_ref, lanes):
        rows = pl.ds(pl.multiple_of(index * ROWS, ROWS), ROWS)
        left = lhs_ref[rows]
        squared = jnp.dot(left, squares[:, lanes], preferred_element_type=F32)
        depth = jnp.dot(left, depths[:, lanes], preferred_element_type=F32)
        inverse = lax.rsqrt(squared)
        turns = (level[:, lanes] + squared * inverse) * wavenumber
        part = turns - ((turns + ROUNDER) - ROUNDER)
        z = part * part
        sine = part * horner(SIN, z)
        cosine = horner(COS, z)
        double = depth * inverse * scale
        lean = double * sine
        out_ref[0, rows] = (0.5 * double - lean * sine).astype(BF16)
        out_ref[1, rows] = (lean * cosine).astype(BF16)
        return carry

    lax.fori_loop(0, channels // ROWS, functools.partial(tile, out_ref=lower, lanes=slice(share, voxels)), 0)
    copy = pltpu.make_async_copy(lower, lower_ref, sems.at[3])
    copy.start()
    lax.fori_loop(0, channels // ROWS, functools.partial(tile, out_ref=upper, lanes=slice(0, share)), 0)
    copy.wait()


def arrange(samples, data):
    blocks, bins, _, group, width = samples.shape
    half = bins * group
    for k in range(blocks):
        for part in range(2):
            data[part * half : (part + 1) * half, k * width : (k + 1) * width] = samples[k, :, part].reshape(half, width)


def beamform(data, operator, start):
    half = data.shape[0] // 2
    for n in range(0, operator.shape[2], LANES):
        first, second = (
            jnp.dot(data[...], operator[which, :, n : n + LANES], preferred_element_type=F32) for which in range(2)
        )
        real = (first[:half] + second[half:]).astype(BF16)
        imag = (first[half:] - second[:half]).astype(BF16)
        yield slice(start + n, start + n + LANES), real, imag


def own_kernel(upper, lower_ref, samples, out_ref, lower, data, sem):
    copy = pltpu.make_async_copy(lower_ref, lower, sem)
    copy.start()
    arrange(samples, data)
    half = out_ref.shape[0] // 2
    for lanes, real, imag in beamform(data, upper, 0):
        out_ref[:half, lanes], out_ref[half:, lanes] = real, imag
    copy.wait()
    for lanes, real, imag in beamform(data, lower, upper.shape[2]):
        out_ref[:half, lanes], out_ref[half:, lanes] = real, imag


def other_kernel(upper, lower, samples, own, y_ref, keep_ref, send_ref, data, gram):
    core = lax.axis_index("core")
    frames = y_ref.shape[0] // 2
    half = frames // CORES
    here = pl.multiple_of(core * half, half)
    there = pl.multiple_of((1 - core) * half, half)
    y_ref[pl.ds(here, half)] = own[:half]
    y_ref[pl.ds(frames + here, half)] = own[half:]
    arrange(samples, data)
    for operator, start in ((upper, 0), (lower, upper.shape[2])):
        for lanes, real, imag in beamform(data, operator, start):
            y_ref[pl.ds(there, half), lanes], y_ref[pl.ds(frames + there, half), lanes] = real, imag
    y = y_ref[...]
    products = lax.dot_general(y, y, (((1,), (1,)), ((), ())), preferred_element_type=F32)
    gram[...] = (products[:frames, :frames] + products[frames:, frames:]) + (
        products[:frames, frames:] - products[frames:, :frames]
    )
    keep_ref[...] = gram[pl.ds(here, half), :]
    send_ref[...] = gram[pl.ds(there, half), :]


def halves(x):
    high = x.astype(BF16)
    return high, (x - high.astype(F32)).astype(BF16)


def product(left, right):
    left_high, left_low = halves(left)
    right_high, right_low = halves(right)
    return jnp.dot(
        jnp.concatenate([left_high, left_high, left_low], axis=1),
        jnp.concatenate([right_high, right_low, right_high], axis=0),
        preferred_element_type=F32,
    )


def unpack(packed):
    flipped = jnp.transpose(packed)
    return 0.5 * (packed + flipped), 0.5 * (packed - flipped), flipped


def filter_kernel(mine, far, twin, far_twin, y_ref, peer_ref, out_ref, gram, kept):
    core = lax.axis_index("core")
    half, frames = mine.shape
    gram[pl.ds(pl.multiple_of(core * half, half), half), :] = mine[...] + far[...].astype(F32)
    gram[pl.ds(pl.multiple_of((1 - core) * half, half), half), :] = twin[...] + far_twin[...].astype(F32)
    packed = gram[...]
    squares = jnp.sum(packed * packed)
    factor = 4.0 / jnp.sqrt(jnp.full((1, 1), squares + EPSILON, F32))
    real, imag, flipped = unpack(packed)
    left = jnp.concatenate([real, imag], axis=1)
    second = product(left, jnp.concatenate([packed, flipped], axis=0)) * (factor * factor)
    third = product(left, jnp.concatenate([second, jnp.transpose(second)], axis=0)) * factor
    rows = lax.broadcasted_iota(jnp.int32, (frames, frames), 0)
    cols = lax.broadcasted_iota(jnp.int32, (frames, frames), 1)
    identity = jnp.where(rows == cols, 1.0, 0.0).astype(F32)
    real, imag, _ = unpack(identity - factor * packed + 0.3 * second - 0.03 * third)
    kept[0] = real.astype(BF16)
    kept[1] = imag.astype(BF16)
    real, imag = (kept[part, pl.ds(pl.multiple_of(core * half, half), half)] for part in range(2))
    matrix = jnp.concatenate(
        [jnp.concatenate([real, imag], axis=1), jnp.concatenate([-imag, real], axis=1)], axis=0
    )
    bins, parts, group, _ = out_ref.shape
    voxels = y_ref.shape[1]
    for source, place in ((y_ref, core), (peer_ref, 1 - core)):
        lanes = pl.ds(pl.multiple_of(place * voxels, voxels), voxels)
        applied = jnp.dot(matrix, source[...], preferred_element_type=F32).astype(BF16)
        for part in range(parts):
            for j in range(bins):
                row = part * half + j * group
                out_ref[j, part, :, lanes] = applied[row : row + group]


def place_kernel(got, out_ref):
    bins, parts, group, _ = got.shape
    width = out_ref.shape[3]
    size = group * bins
    rows = lax.broadcasted_iota(jnp.int32, (size, size), 0)
    cols = lax.broadcasted_iota(jnp.int32, (size, size), 1)
    turn = jnp.where(cols == (rows % bins) * group + rows // bins, 1.0, 0.0).astype(BF16)
    lanes = pl.ds(pl.multiple_of(pl.program_id(0) * width, width), width)
    for part in range(parts):
        block = got[:, part, :, lanes].reshape(size, width)
        moved = jnp.dot(turn, block, preferred_element_type=F32).astype(BF16)
        out_ref[:, part] = moved.reshape(group, bins, width)


def shards(rf_data, elem_pos, vox_pos, subbands):
    parts, bins, group, width = rf_data.shape
    channels = elem_pos.shape[1]
    chans = channels // width
    voxels = vox_pos.shape[1] // CORES
    frames = group * bins * CORES
    half = frames // CORES

    def shape(*dims, dtype=BF16):
        return jax.ShapeDtypeStruct(dims, dtype)

    def swap(x):
        return lax.ppermute(x, "core", [(0, 1), (1, 0)])

    def across(x, bits):
        return lax.ppermute(x, "chan", [(a, a ^ bits) for a in range(chans)])

    by_bin = pl.pallas_call(
        spread_kernel,
        name="spread",
        out_shape=shape(chans * bins, parts, group, width),
        in_specs=[HBM],
        out_specs=HBM,
        scratch_shapes=[pltpu.VMEM(rf_data.shape, BF16), pltpu.SemaphoreType.DMA((chans * parts + 1,))],
        compiler_params=WIDE,
    )(pltpu.with_memory_space_constraint(rf_data, pltpu.HBM))
    own = lax.all_to_all(by_bin, ("chan", "bin"), split_axis=0, concat_axis=0, tiled=True)

    share = voxels // 2
    upper, lower = pl.pallas_call(
        operator_kernel,
        name="operator",
        out_shape=(shape(2, channels, share), pltpu.HBM((2, channels, voxels - share), BF16)),
        in_specs=[HBM, HBM, HBM],
        out_specs=(VMEM, HBM),
        scratch_shapes=[
            pltpu.VMEM(elem_pos.shape, jnp.int32),
            pltpu.VMEM(vox_pos.shape, jnp.int32),
            pltpu.SMEM(subbands.shape, jnp.int32),
            pltpu.VMEM((channels, 8), BF16),
            pltpu.VMEM((2, channels, voxels - share), BF16),
            pltpu.SemaphoreType.DMA((4,)),
        ],
        compiler_params=WIDE,
        cost_estimate=pl.CostEstimate(
            flops=60 * channels * voxels,
            transcendentals=channels * voxels,
            bytes_accessed=4 * channels * voxels,
        ),
    )(*(pltpu.with_memory_space_constraint(x, pltpu.HBM) for x in (elem_pos, vox_pos, subbands)))

    own, upper, lower = lax.optimization_barrier((own, upper, lower))
    other = swap(own)
    own = own.reshape(chans, bins, parts, group, width)
    other = other.reshape(chans, bins, parts, group, width)

    beam_cost = pl.CostEstimate(
        flops=8 * half * channels * voxels * 2, transcendentals=0, bytes_accessed=4 * channels * voxels
    )
    mine, lower = pl.pallas_call(
        own_kernel,
        name="beam_own",
        out_shape=(shape(frames, voxels), shape(2, channels, voxels - share)),
        in_specs=[VMEM, HBM, VMEM],
        out_specs=(VMEM, VMEM),
        scratch_shapes=[
            pltpu.VMEM((frames, channels), BF16),
            pltpu.SemaphoreType.DMA,
        ],
        compiler_params=WIDE,
        cost_estimate=beam_cost,
    )(upper, pltpu.with_memory_space_constraint(lower, pltpu.HBM), own)
    y, keep, send = pl.pallas_call(
        other_kernel,
        name="beam_other",
        out_shape=(shape(2 * frames, voxels), shape(half, frames, dtype=F32), shape(half, frames, dtype=F32)),
        in_specs=[VMEM, VMEM, VMEM, VMEM],
        out_specs=(VMEM, VMEM, VMEM),
        scratch_shapes=[pltpu.VMEM((frames, channels), BF16), pltpu.VMEM((frames, frames), F32)],
        compiler_params=WIDE,
        cost_estimate=beam_cost,
    )(upper, lower, other, mine)

    total = keep + swap(send)
    total, y = lax.optimization_barrier((total, y))
    peer = swap(y)
    narrow = total.astype(BF16)
    total = total + sum(across(narrow, bits).astype(F32) for bits in (1, 3, 2))
    narrow = total.astype(BF16)
    far = across(narrow, 4)
    far_twin = lax.ppermute(
        narrow, ("chan", "core"), [(2 * a + c, 2 * (a ^ 4) + 1 - c) for a in range(chans) for c in range(CORES)]
    )
    twin = swap(total)

    applied = pl.pallas_call(
        filter_kernel,
        name="filter",
        out_shape=shape(bins, parts, group, CORES * voxels),
        in_specs=[VMEM] * 6,
        out_specs=VMEM,
        scratch_shapes=[pltpu.VMEM((frames, frames), F32), pltpu.VMEM((2, frames, frames), BF16)],
        compiler_params=WIDE,
    )(total, far, twin, far_twin, y, peer)

    got = lax.all_to_all(applied, "bin", split_axis=0, concat_axis=0, tiled=True)
    return pl.pallas_call(
        place_kernel,
        name="place",
        grid=(CORES * voxels // PLACED,),
        out_shape=shape(group, parts, bins, CORES * voxels),
        in_specs=[VMEM],
        out_specs=pl.BlockSpec((group, parts, bins, PLACED), lambda n: (0, 0, 0, n)),
        compiler_params=WIDE,
    )(got)


def solution(mesh):
    chans = mesh.shape["chan"]
    fine = Mesh(mesh.devices.reshape(chans, BINS, CORES), ("chan", "bin", "core"))
    return jax.shard_map(
        shards,
        mesh=fine,
        in_specs=(P(None, None, ("bin", "core"), "chan"), P(), P(None, "chan"), P()),
        out_specs=P(("bin", "core"), None, None, "chan"),
        check_vma=False,
    )
```

```python
import functools
import math

import jax
import jax.numpy as jnp
from jax import lax
from jax.experimental import pallas as pl
from jax.experimental.pallas import tpu as pltpu
from jax.sharding import Mesh, PartitionSpec as P

EPSILON = 1e-06
BINS = 8
CORES = 2
F32 = jnp.float32
BF16 = jnp.bfloat16
SIN = (3.1415925800446924, -5.167706878924515, 2.5500313772531213, -0.5980451739748806, 0.0772201286897368)
COS = (0.9999999534666272, -4.934792858670076, 4.058411914063177, -1.331880160583308, 0.21969679727234584)
ROUNDER = 12582912.0
ROWS = 512
LANES = 256
WIDE = pltpu.CompilerParams(vmem_limit_bytes=16 * 1024 * 1024)
VMEM = pl.BlockSpec(memory_space=pltpu.VMEM)
HBM = pl.BlockSpec(memory_space=pltpu.HBM)


def horner(coefficients, z):
    total = coefficients[-1] * z + coefficients[-2]
    for value in coefficients[-3::-1]:
        total = total * z + value
    return total


def digits(value, unit):
    high = jnp.floor(value * (1.0 / unit))
    return high, value - unit * high


def spread_kernel(rf_ref, out_ref, held, sems):
    parts, bins = held.shape[:2]
    chans = out_ref.shape[0] // bins
    copy = pltpu.make_async_copy(rf_ref, held, sems.at[chans * parts])
    copy.start()
    copy.wait()
    copies = [
        pltpu.make_async_copy(held.at[part], out_ref.at[k * bins : (k + 1) * bins, part], sems.at[k * parts + part])
        for k in range(chans)
        for part in range(parts)
    ]
    for copy in copies:
        copy.start()
    for copy in copies:
        copy.wait()


def operator_kernel(elem_ref, vox_ref, bins_ref, upper, lower_ref, elem, vox, bins, lhs_ref, lower, sems):
    core = lax.axis_index("core")
    channels = elem.shape[1]
    share = upper.shape[2]
    voxels = share + lower.shape[2]
    copies = [
        pltpu.make_async_copy(source, target, sems.at[n])
        for n, (source, target) in enumerate(((elem_ref, elem), (vox_ref, vox), (bins_ref, bins)))
    ]
    for copy in copies:
        copy.start()
    for copy in copies:
        copy.wait()
    wavenumber = (32.0 + bins[lax.axis_index("bin")].astype(F32)) / 64.0
    scale = 2.0 / math.sqrt(channels)

    place = elem[...].astype(F32)
    high, low = digits(jnp.sum(place * place, axis=0, keepdims=True), 16.0)
    one = jnp.ones((1, channels), F32)
    lhs = jnp.concatenate([place, high, low, one, one, 0.0 * one], axis=0)
    lhs_ref[...] = jnp.transpose(lhs).astype(BF16)
    voxel = vox[:, pl.ds(pl.multiple_of(core * voxels, voxels), voxels)].astype(F32)
    high, low = digits(jnp.sum(voxel * voxel, axis=0, keepdims=True), 64.0)
    one = jnp.ones((1, voxels), F32)
    zero = 0.0 * one
    level = voxel[2:3]
    squares = jnp.concatenate([-2.0 * voxel, 16.0 * one, one, 64.0 * high, low, zero], axis=0).astype(BF16)
    depths = jnp.concatenate([zero, zero, -1.0 * one, zero, zero, level, zero, zero], axis=0).astype(BF16)

    def tile(index, carry, out_ref, lanes):
        rows = pl.ds(pl.multiple_of(index * ROWS, ROWS), ROWS)
        left = lhs_ref[rows]
        squared = jnp.dot(left, squares[:, lanes], preferred_element_type=F32)
        depth = jnp.dot(left, depths[:, lanes], preferred_element_type=F32)
        inverse = lax.rsqrt(squared)
        turns = (level[:, lanes] + squared * inverse) * wavenumber
        part = turns - ((turns + ROUNDER) - ROUNDER)
        z = part * part
        sine = part * horner(SIN, z)
        cosine = horner(COS, z)
        double = depth * inverse * scale
        lean = double * sine
        out_ref[0, rows] = (0.5 * double - lean * sine).astype(BF16)
        out_ref[1, rows] = (lean * cosine).astype(BF16)
        return carry

    lax.fori_loop(0, channels // ROWS, functools.partial(tile, out_ref=lower, lanes=slice(share, voxels)), 0)
    copy = pltpu.make_async_copy(lower, lower_ref, sems.at[3])
    copy.start()
    lax.fori_loop(0, channels // ROWS, functools.partial(tile, out_ref=upper, lanes=slice(0, share)), 0)
    copy.wait()


def arrange(samples, data):
    blocks, bins, _, group, width = samples.shape
    half = bins * group
    for k in range(blocks):
        for part in range(2):
            data[part * half : (part + 1) * half, k * width : (k + 1) * width] = samples[k, :, part].reshape(half, width)


def beamform(data, operator, start):
    half = data.shape[0] // 2
    for n in range(0, operator.shape[2], LANES):
        first, second = (
            jnp.dot(data[...], operator[which, :, n : n + LANES], preferred_element_type=F32) for which in range(2)
        )
        real = (first[:half] + second[half:]).astype(BF16)
        imag = (first[half:] - second[:half]).astype(BF16)
        yield slice(start + n, start + n + LANES), real, imag


def own_kernel(upper, lower_ref, samples, out_ref, lower, data, sem):
    copy = pltpu.make_async_copy(lower_ref, lower, sem)
    copy.start()
    arrange(samples, data)
    half = out_ref.shape[0] // 2
    for lanes, real, imag in beamform(data, upper, 0):
        out_ref[:half, lanes], out_ref[half:, lanes] = real, imag
    copy.wait()
    for lanes, real, imag in beamform(data, lower, upper.shape[2]):
        out_ref[:half, lanes], out_ref[half:, lanes] = real, imag


def other_kernel(upper, lower, samples, own, y_ref, keep_ref, send_ref, data, gram):
    core = lax.axis_index("core")
    frames = y_ref.shape[0] // 2
    half = frames // CORES
    here = pl.multiple_of(core * half, half)
    there = pl.multiple_of((1 - core) * half, half)
    y_ref[pl.ds(here, half)] = own[:half]
    y_ref[pl.ds(frames + here, half)] = own[half:]
    arrange(samples, data)
    for operator, start in ((upper, 0), (lower, upper.shape[2])):
        for lanes, real, imag in beamform(data, operator, start):
            y_ref[pl.ds(there, half), lanes], y_ref[pl.ds(frames + there, half), lanes] = real, imag
    y = y_ref[...]
    products = lax.dot_general(y, y, (((1,), (1,)), ((), ())), preferred_element_type=F32)
    gram[...] = (products[:frames, :frames] + products[frames:, frames:]) + (
        products[:frames, frames:] - products[frames:, :frames]
    )
    keep_ref[...] = gram[pl.ds(here, half), :]
    send_ref[...] = gram[pl.ds(there, half), :]


def halves(x):
    high = x.astype(BF16)
    return high, (x - high.astype(F32)).astype(BF16)


def product(left, right):
    left_high, left_low = halves(left)
    right_high, right_low = halves(right)
    return jnp.dot(
        jnp.concatenate([left_high, left_high, left_low], axis=1),
        jnp.concatenate([right_high, right_low, right_high], axis=0),
        preferred_element_type=F32,
    )


def unpack(packed):
    flipped = jnp.transpose(packed)
    return 0.5 * (packed + flipped), 0.5 * (packed - flipped), flipped


def filter_kernel(mine, far, twin, far_twin, y_ref, peer_ref, out_ref, gram, kept):
    core = lax.axis_index("core")
    half, frames = mine.shape
    gram[pl.ds(pl.multiple_of(core * half, half), half), :] = mine[...] + far[...].astype(F32)
    gram[pl.ds(pl.multiple_of((1 - core) * half, half), half), :] = twin[...] + far_twin[...].astype(F32)
    packed = gram[...]
    squares = jnp.sum(packed * packed)
    factor = 4.0 / jnp.sqrt(jnp.full((1, 1), squares + EPSILON, F32))
    real, imag, flipped = unpack(packed)
    left = jnp.concatenate([real, imag], axis=1)
    second = product(left, jnp.concatenate([packed, flipped], axis=0)) * (factor * factor)
    third = product(left, jnp.concatenate([second, jnp.transpose(second)], axis=0)) * factor
    rows = lax.broadcasted_iota(jnp.int32, (frames, frames), 0)
    cols = lax.broadcasted_iota(jnp.int32, (frames, frames), 1)
    identity = jnp.where(rows == cols, 1.0, 0.0).astype(F32)
    real, imag, _ = unpack(identity - factor * packed + 0.3 * second - 0.03 * third)
    kept[0] = real.astype(BF16)
    kept[1] = imag.astype(BF16)
    real, imag = (kept[part, pl.ds(pl.multiple_of(core * half, half), half)] for part in range(2))
    matrix = jnp.concatenate(
        [jnp.concatenate([real, imag], axis=1), jnp.concatenate([-imag, real], axis=1)], axis=0
    )
    bins, parts, group, _ = out_ref.shape
    voxels = y_ref.shape[1]
    for source, place in ((y_ref, core), (peer_ref, 1 - core)):
        lanes = pl.ds(pl.multiple_of(place * voxels, voxels), voxels)
        applied = jnp.dot(matrix, source[...], preferred_element_type=F32).astype(BF16)
        for part in range(parts):
            for j in range(bins):
                row = part * half + j * group
                out_ref[j, part, :, lanes] = applied[row : row + group]


def place_kernel(got, out_ref, held, sems):
    bins, parts, group, voxels = got.shape
    size = group * bins
    rows = lax.broadcasted_iota(jnp.int32, (size, size), 0)
    cols = lax.broadcasted_iota(jnp.int32, (size, size), 1)
    turn = jnp.where(cols == (rows % bins) * group + rows // bins, 1.0, 0.0).astype(BF16)
    copies = [
        pltpu.make_async_copy(held.at[part], out_ref.at[:, part], sems.at[part]) for part in range(parts)
    ]
    for part in range(parts):
        moved = jnp.dot(turn, got[:, part].reshape(size, voxels), preferred_element_type=F32).astype(BF16)
        held[part] = moved.reshape(group, bins, voxels)
        copies[part].start()
    for copy in copies:
        copy.wait()


def shards(rf_data, elem_pos, vox_pos, subbands):
    parts, bins, group, width = rf_data.shape
    channels = elem_pos.shape[1]
    chans = channels // width
    voxels = vox_pos.shape[1] // CORES
    frames = group * bins * CORES
    half = frames // CORES

    def shape(*dims, dtype=BF16):
        return jax.ShapeDtypeStruct(dims, dtype)

    def swap(x):
        return lax.ppermute(x, "core", [(0, 1), (1, 0)])

    def across(x, bits):
        return lax.ppermute(x, "chan", [(a, a ^ bits) for a in range(chans)])

    by_bin = pl.pallas_call(
        spread_kernel,
        name="spread",
        out_shape=shape(chans * bins, parts, group, width),
        in_specs=[HBM],
        out_specs=HBM,
        scratch_shapes=[pltpu.VMEM(rf_data.shape, BF16), pltpu.SemaphoreType.DMA((chans * parts + 1,))],
        compiler_params=WIDE,
    )(pltpu.with_memory_space_constraint(rf_data, pltpu.HBM))
    own = lax.all_to_all(by_bin, ("chan", "bin"), split_axis=0, concat_axis=0, tiled=True)

    share = voxels // 2
    upper, lower = pl.pallas_call(
        operator_kernel,
        name="operator",
        out_shape=(shape(2, channels, share), pltpu.HBM((2, channels, voxels - share), BF16)),
        in_specs=[HBM, HBM, HBM],
        out_specs=(VMEM, HBM),
        scratch_shapes=[
            pltpu.VMEM(elem_pos.shape, jnp.int32),
            pltpu.VMEM(vox_pos.shape, jnp.int32),
            pltpu.SMEM(subbands.shape, jnp.int32),
            pltpu.VMEM((channels, 8), BF16),
            pltpu.VMEM((2, channels, voxels - share), BF16),
            pltpu.SemaphoreType.DMA((4,)),
        ],
        compiler_params=WIDE,
        cost_estimate=pl.CostEstimate(
            flops=60 * channels * voxels,
            transcendentals=channels * voxels,
            bytes_accessed=4 * channels * voxels,
        ),
    )(*(pltpu.with_memory_space_constraint(x, pltpu.HBM) for x in (elem_pos, vox_pos, subbands)))

    own, upper, lower = lax.optimization_barrier((own, upper, lower))
    other = swap(own)
    own = own.reshape(chans, bins, parts, group, width)
    other = other.reshape(chans, bins, parts, group, width)

    beam_cost = pl.CostEstimate(
        flops=8 * half * channels * voxels * 2, transcendentals=0, bytes_accessed=4 * channels * voxels
    )
    mine, lower = pl.pallas_call(
        own_kernel,
        name="beam_own",
        out_shape=(shape(frames, voxels), shape(2, channels, voxels - share)),
        in_specs=[VMEM, HBM, VMEM],
        out_specs=(VMEM, VMEM),
        scratch_shapes=[
            pltpu.VMEM((frames, channels), BF16),
            pltpu.SemaphoreType.DMA,
        ],
        compiler_params=WIDE,
        cost_estimate=beam_cost,
    )(upper, pltpu.with_memory_space_constraint(lower, pltpu.HBM), own)
    y, keep, send = pl.pallas_call(
        other_kernel,
        name="beam_other",
        out_shape=(shape(2 * frames, voxels), shape(half, frames, dtype=F32), shape(half, frames, dtype=F32)),
        in_specs=[VMEM, VMEM, VMEM, VMEM],
        out_specs=(VMEM, VMEM, VMEM),
        scratch_shapes=[pltpu.VMEM((frames, channels), BF16), pltpu.VMEM((frames, frames), F32)],
        compiler_params=WIDE,
        cost_estimate=beam_cost,
    )(upper, lower, other, mine)

    total = keep + swap(send)
    total, y = lax.optimization_barrier((total, y))
    peer = swap(y)
    narrow = total.astype(BF16)
    total = total + sum(across(narrow, bits).astype(F32) for bits in (1, 3, 2))
    narrow = total.astype(BF16)
    far = across(narrow, 4)
    far_twin = lax.ppermute(
        narrow, ("chan", "core"), [(2 * a + c, 2 * (a ^ 4) + 1 - c) for a in range(chans) for c in range(CORES)]
    )
    twin = swap(total)

    applied = pl.pallas_call(
        filter_kernel,
        name="filter",
        out_shape=shape(bins, parts, group, CORES * voxels),
        in_specs=[VMEM] * 6,
        out_specs=VMEM,
        scratch_shapes=[pltpu.VMEM((frames, frames), F32), pltpu.VMEM((2, frames, frames), BF16)],
        compiler_params=WIDE,
    )(total, far, twin, far_twin, y, peer)

    got = lax.all_to_all(applied, "bin", split_axis=0, concat_axis=0, tiled=True)
    return pl.pallas_call(
        place_kernel,
        name="place",
        out_shape=shape(group, parts, bins, CORES * voxels),
        in_specs=[VMEM],
        out_specs=HBM,
        scratch_shapes=[
            pltpu.VMEM((parts, group, bins, CORES * voxels), BF16),
            pltpu.SemaphoreType.DMA((parts,)),
        ],
        compiler_params=WIDE,
    )(got)


def solution(mesh):
    chans = mesh.shape["chan"]
    fine = Mesh(mesh.devices.reshape(chans, BINS, CORES), ("chan", "bin", "core"))
    return jax.shard_map(
        shards,
        mesh=fine,
        in_specs=(P(None, None, ("bin", "core"), "chan"), P(), P(None, "chan"), P()),
        out_specs=P(("bin", "core"), None, None, "chan"),
        check_vma=False,
    )
```

```python
import functools
import math

import jax
import jax.numpy as jnp
from jax import lax
from jax.experimental import pallas as pl
from jax.experimental.pallas import tpu as pltpu
from jax.sharding import Mesh, PartitionSpec as P

EPSILON = 1e-06
BINS = 8
CORES = 2
F32 = jnp.float32
BF16 = jnp.bfloat16
SIN = (3.1415925800446924, -5.167706878924515, 2.5500313772531213, -0.5980451739748806, 0.0772201286897368)
COS = (0.9999999534666272, -4.934792858670076, 4.058411914063177, -1.331880160583308, 0.21969679727234584)
ROUNDER = 12582912.0
ROWS = 512
LANES = 256
IN_FLIGHT = 5
WIDE = pltpu.CompilerParams(vmem_limit_bytes=16 * 1024 * 1024)
VMEM = pl.BlockSpec(memory_space=pltpu.VMEM)
HBM = pl.BlockSpec(memory_space=pltpu.HBM)


def horner(coefficients, z):
    total = coefficients[-1] * z + coefficients[-2]
    for value in coefficients[-3::-1]:
        total = total * z + value
    return total


def digits(value, unit):
    high = jnp.floor(value * (1.0 / unit))
    return high, value - unit * high


def spread_kernel(rf_ref, out_ref, held, sems):
    parts, bins = held.shape[:2]
    chans = out_ref.shape[0] // bins
    copy = pltpu.make_async_copy(rf_ref, held, sems.at[chans * parts])
    copy.start()
    copy.wait()
    copies = [
        pltpu.make_async_copy(held.at[part], out_ref.at[k * bins : (k + 1) * bins, part], sems.at[k * parts + part])
        for k in range(chans)
        for part in range(parts)
    ]
    for copy in copies:
        copy.start()
    for copy in copies:
        copy.wait()


def operator_kernel(elem_ref, vox_ref, bins_ref, upper, lower_ref, elem, vox, bins, lhs_ref, lower, sems):
    core = lax.axis_index("core")
    channels = elem.shape[1]
    share = upper.shape[2]
    voxels = share + lower.shape[2]
    copies = [
        pltpu.make_async_copy(source, target, sems.at[n])
        for n, (source, target) in enumerate(((elem_ref, elem), (vox_ref, vox), (bins_ref, bins)))
    ]
    for copy in copies:
        copy.start()
    for copy in copies:
        copy.wait()
    wavenumber = (32.0 + bins[lax.axis_index("bin")].astype(F32)) / 64.0
    scale = 2.0 / math.sqrt(channels)

    place = elem[...].astype(F32)
    high, low = digits(jnp.sum(place * place, axis=0, keepdims=True), 16.0)
    one = jnp.ones((1, channels), F32)
    lhs = jnp.concatenate([place, high, low, one, one, 0.0 * one], axis=0)
    lhs_ref[...] = jnp.transpose(lhs).astype(BF16)
    voxel = vox[:, pl.ds(pl.multiple_of(core * voxels, voxels), voxels)].astype(F32)
    high, low = digits(jnp.sum(voxel * voxel, axis=0, keepdims=True), 64.0)
    one = jnp.ones((1, voxels), F32)
    zero = 0.0 * one
    level = voxel[2:3]
    squares = jnp.concatenate([-2.0 * voxel, 16.0 * one, one, 64.0 * high, low, zero], axis=0).astype(BF16)
    depths = jnp.concatenate([zero, zero, -1.0 * one, zero, zero, level, zero, zero], axis=0).astype(BF16)

    def tile(index, carry, out_ref, lanes):
        rows = pl.ds(pl.multiple_of(index * ROWS, ROWS), ROWS)
        left = lhs_ref[rows]
        squared = jnp.dot(left, squares[:, lanes], preferred_element_type=F32)
        depth = jnp.dot(left, depths[:, lanes], preferred_element_type=F32)
        inverse = lax.rsqrt(squared)
        turns = (level[:, lanes] + squared * inverse) * wavenumber
        part = turns - ((turns + ROUNDER) - ROUNDER)
        z = part * part
        sine = part * horner(SIN, z)
        cosine = horner(COS, z)
        double = depth * inverse * scale
        lean = double * sine
        out_ref[0, rows] = (0.5 * double - lean * sine).astype(BF16)
        out_ref[1, rows] = (lean * cosine).astype(BF16)
        return carry

    lax.fori_loop(0, channels // ROWS, functools.partial(tile, out_ref=lower, lanes=slice(share, voxels)), 0)
    copy = pltpu.make_async_copy(lower, lower_ref, sems.at[3])
    copy.start()
    lax.fori_loop(0, channels // ROWS, functools.partial(tile, out_ref=upper, lanes=slice(0, share)), 0)
    copy.wait()


def arrange(samples, data):
    blocks, bins, _, group, width = samples.shape
    half = bins * group
    for k in range(blocks):
        for part in range(2):
            data[part * half : (part + 1) * half, k * width : (k + 1) * width] = samples[k, :, part].reshape(half, width)


def beamform(data, operator, start):
    half = data.shape[0] // 2
    for n in range(0, operator.shape[2], LANES):
        first, second = (
            jnp.dot(data[...], operator[which, :, n : n + LANES], preferred_element_type=F32) for which in range(2)
        )
        real = (first[:half] + second[half:]).astype(BF16)
        imag = (first[half:] - second[:half]).astype(BF16)
        yield slice(start + n, start + n + LANES), real, imag


def own_kernel(upper, lower_ref, samples, out_ref, lower, data, sem):
    copy = pltpu.make_async_copy(lower_ref, lower, sem)
    copy.start()
    arrange(samples, data)
    half = out_ref.shape[0] // 2
    for lanes, real, imag in beamform(data, upper, 0):
        out_ref[:half, lanes], out_ref[half:, lanes] = real, imag
    copy.wait()
    for lanes, real, imag in beamform(data, lower, upper.shape[2]):
        out_ref[:half, lanes], out_ref[half:, lanes] = real, imag


def other_kernel(upper, lower, samples, own, y_ref, keep_ref, send_ref, data, gram):
    core = lax.axis_index("core")
    frames = y_ref.shape[0] // 2
    half = frames // CORES
    here = pl.multiple_of(core * half, half)
    there = pl.multiple_of((1 - core) * half, half)
    y_ref[pl.ds(here, half)] = own[:half]
    y_ref[pl.ds(frames + here, half)] = own[half:]
    arrange(samples, data)
    for operator, start in ((upper, 0), (lower, upper.shape[2])):
        for lanes, real, imag in beamform(data, operator, start):
            y_ref[pl.ds(there, half), lanes], y_ref[pl.ds(frames + there, half), lanes] = real, imag
    y = y_ref[...]
    products = lax.dot_general(y, y, (((1,), (1,)), ((), ())), preferred_element_type=F32)
    gram[...] = (products[:frames, :frames] + products[frames:, frames:]) + (
        products[:frames, frames:] - products[frames:, :frames]
    )
    keep_ref[...] = gram[pl.ds(here, half), :]
    send_ref[...] = gram[pl.ds(there, half), :]


def halves(x):
    high = x.astype(BF16)
    return high, (x - high.astype(F32)).astype(BF16)


def product(left, right):
    left_high, left_low = halves(left)
    right_high, right_low = halves(right)
    return jnp.dot(
        jnp.concatenate([left_high, left_high, left_low], axis=1),
        jnp.concatenate([right_high, right_low, right_high], axis=0),
        preferred_element_type=F32,
    )


def unpack(packed):
    flipped = jnp.transpose(packed)
    return 0.5 * (packed + flipped), 0.5 * (packed - flipped), flipped


def filter_kernel(mine, far, twin, far_twin, y_ref, peer_ref, *refs):
    core = lax.axis_index("core")
    *out_refs, gram, kept = refs
    half, frames = mine.shape
    gram[pl.ds(pl.multiple_of(core * half, half), half), :] = mine[...] + far[...].astype(F32)
    gram[pl.ds(pl.multiple_of((1 - core) * half, half), half), :] = twin[...] + far_twin[...].astype(F32)
    packed = gram[...]
    squares = jnp.sum(packed * packed)
    factor = 4.0 / jnp.sqrt(jnp.full((1, 1), squares + EPSILON, F32))
    real, imag, flipped = unpack(packed)
    left = jnp.concatenate([real, imag], axis=1)
    second = product(left, jnp.concatenate([packed, flipped], axis=0)) * (factor * factor)
    third = product(left, jnp.concatenate([second, jnp.transpose(second)], axis=0)) * factor
    rows = lax.broadcasted_iota(jnp.int32, (frames, frames), 0)
    cols = lax.broadcasted_iota(jnp.int32, (frames, frames), 1)
    identity = jnp.where(rows == cols, 1.0, 0.0).astype(F32)
    real, imag, _ = unpack(identity - factor * packed + 0.3 * second - 0.03 * third)
    kept[0] = real.astype(BF16)
    kept[1] = imag.astype(BF16)
    parts, group, _ = out_refs[0].shape
    index = lax.axis_index("bin")
    starts = [pl.multiple_of(core * half + (index ^ m) * group, group) for m in range(len(out_refs))]
    real, imag = (
        jnp.concatenate([kept[part, pl.ds(start, group)] for start in starts], axis=0) for part in range(parts)
    )
    matrix = jnp.concatenate(
        [jnp.concatenate([real, imag], axis=1), jnp.concatenate([-imag, real], axis=1)], axis=0
    )
    voxels = y_ref.shape[1]
    for source, place in ((y_ref, core), (peer_ref, 1 - core)):
        lanes = pl.ds(pl.multiple_of(place * voxels, voxels), voxels)
        applied = jnp.dot(matrix, source[...], preferred_element_type=F32).astype(BF16)
        for part in range(parts):
            for m, out_ref in enumerate(out_refs):
                row = part * half + m * group
                out_ref[part, :, lanes] = applied[row : row + group]


def place_kernel(*refs):
    *got, out_ref, held, sems = refs
    bins = len(got)
    parts, group, voxels = got[0].shape
    size = group * bins
    rows = lax.broadcasted_iota(jnp.int32, (size, size), 0)
    cols = lax.broadcasted_iota(jnp.int32, (size, size), 1)
    slots = (rows % bins) ^ lax.axis_index("bin")
    turn = jnp.where(cols == slots * group + rows // bins, 1.0, 0.0).astype(BF16)
    copies = [
        pltpu.make_async_copy(held.at[part], out_ref.at[:, part], sems.at[part]) for part in range(parts)
    ]
    for part in range(parts):
        block = jnp.concatenate([piece[part] for piece in got], axis=0)
        moved = jnp.dot(turn, block, preferred_element_type=F32).astype(BF16)
        held[part] = moved.reshape(group, bins, voxels)
        copies[part].start()
    for copy in copies:
        copy.wait()


def shards(rf_data, elem_pos, vox_pos, subbands):
    parts, bins, group, width = rf_data.shape
    channels = elem_pos.shape[1]
    chans = channels // width
    voxels = vox_pos.shape[1] // CORES
    frames = group * bins * CORES
    half = frames // CORES

    def shape(*dims, dtype=BF16):
        return jax.ShapeDtypeStruct(dims, dtype)

    def swap(x):
        return lax.ppermute(x, "core", [(0, 1), (1, 0)])

    def across(x, bits):
        return lax.ppermute(x, "chan", [(a, a ^ bits) for a in range(chans)])

    by_bin = pl.pallas_call(
        spread_kernel,
        name="spread",
        out_shape=shape(chans * bins, parts, group, width),
        in_specs=[HBM],
        out_specs=HBM,
        scratch_shapes=[pltpu.VMEM(rf_data.shape, BF16), pltpu.SemaphoreType.DMA((chans * parts + 1,))],
        compiler_params=WIDE,
    )(pltpu.with_memory_space_constraint(rf_data, pltpu.HBM))
    own = lax.all_to_all(by_bin, ("chan", "bin"), split_axis=0, concat_axis=0, tiled=True)

    share = voxels // 2
    upper, lower = pl.pallas_call(
        operator_kernel,
        name="operator",
        out_shape=(shape(2, channels, share), pltpu.HBM((2, channels, voxels - share), BF16)),
        in_specs=[HBM, HBM, HBM],
        out_specs=(VMEM, HBM),
        scratch_shapes=[
            pltpu.VMEM(elem_pos.shape, jnp.int32),
            pltpu.VMEM(vox_pos.shape, jnp.int32),
            pltpu.SMEM(subbands.shape, jnp.int32),
            pltpu.VMEM((channels, 8), BF16),
            pltpu.VMEM((2, channels, voxels - share), BF16),
            pltpu.SemaphoreType.DMA((4,)),
        ],
        compiler_params=WIDE,
        cost_estimate=pl.CostEstimate(
            flops=60 * channels * voxels,
            transcendentals=channels * voxels,
            bytes_accessed=4 * channels * voxels,
        ),
    )(*(pltpu.with_memory_space_constraint(x, pltpu.HBM) for x in (elem_pos, vox_pos, subbands)))

    own, upper, lower = lax.optimization_barrier((own, upper, lower))
    other = swap(own)
    own = own.reshape(chans, bins, parts, group, width)
    other = other.reshape(chans, bins, parts, group, width)

    beam_cost = pl.CostEstimate(
        flops=8 * half * channels * voxels * 2, transcendentals=0, bytes_accessed=4 * channels * voxels
    )
    mine, lower = pl.pallas_call(
        own_kernel,
        name="beam_own",
        out_shape=(shape(frames, voxels), shape(2, channels, voxels - share)),
        in_specs=[VMEM, HBM, VMEM],
        out_specs=(VMEM, VMEM),
        scratch_shapes=[
            pltpu.VMEM((frames, channels), BF16),
            pltpu.SemaphoreType.DMA,
        ],
        compiler_params=WIDE,
        cost_estimate=beam_cost,
    )(upper, pltpu.with_memory_space_constraint(lower, pltpu.HBM), own)
    y, keep, send = pl.pallas_call(
        other_kernel,
        name="beam_other",
        out_shape=(shape(2 * frames, voxels), shape(half, frames, dtype=F32), shape(half, frames, dtype=F32)),
        in_specs=[VMEM, VMEM, VMEM, VMEM],
        out_specs=(VMEM, VMEM, VMEM),
        scratch_shapes=[pltpu.VMEM((frames, channels), BF16), pltpu.VMEM((frames, frames), F32)],
        compiler_params=WIDE,
        cost_estimate=beam_cost,
    )(upper, lower, other, mine)

    total = keep + swap(send)
    total, y = lax.optimization_barrier((total, y))
    peer = swap(y)
    narrow = total.astype(BF16)
    total = total + sum(across(narrow, bits).astype(F32) for bits in (1, 3, 2))
    narrow = total.astype(BF16)
    far = across(narrow, 4)
    far_twin = lax.ppermute(
        narrow, ("chan", "core"), [(2 * a + c, 2 * (a ^ 4) + 1 - c) for a in range(chans) for c in range(CORES)]
    )
    twin = swap(total)

    pieces = pl.pallas_call(
        filter_kernel,
        name="filter",
        out_shape=(shape(parts, group, CORES * voxels),) * bins,
        in_specs=[VMEM] * 6,
        out_specs=(VMEM,) * bins,
        scratch_shapes=[pltpu.VMEM((frames, frames), F32), pltpu.VMEM((2, frames, frames), BF16)],
        compiler_params=WIDE,
    )(total, far, twin, far_twin, y, peer)

    got = {0: pieces[0]}
    order = [5, 4, 7, 3, 6, 2, 1]
    for n, m in enumerate(order):
        piece = pieces[m]
        if n >= IN_FLIGHT:
            earlier = order[n - IN_FLIGHT]
            piece, got[earlier] = lax.optimization_barrier((piece, got[earlier]))
        got[m] = lax.ppermute(piece, "bin", [(a, a ^ m) for a in range(bins)])

    return pl.pallas_call(
        place_kernel,
        name="place",
        out_shape=shape(group, parts, bins, CORES * voxels),
        in_specs=[VMEM] * bins,
        out_specs=HBM,
        scratch_shapes=[
            pltpu.VMEM((parts, group, bins, CORES * voxels), BF16),
            pltpu.SemaphoreType.DMA((parts,)),
        ],
        compiler_params=WIDE,
    )(*(got[m] for m in range(bins)))


def solution(mesh):
    chans = mesh.shape["chan"]
    fine = Mesh(mesh.devices.reshape(chans, BINS, CORES), ("chan", "bin", "core"))
    return jax.shard_map(
        shards,
        mesh=fine,
        in_specs=(P(None, None, ("bin", "core"), "chan"), P(), P(None, "chan"), P()),
        out_specs=P(("bin", "core"), None, None, "chan"),
        check_vma=False,
    )
```

```python
import functools
import math

import jax
import jax.numpy as jnp
from jax import lax
from jax.experimental import pallas as pl
from jax.experimental.pallas import tpu as pltpu
from jax.sharding import Mesh, PartitionSpec as P

EPSILON = 1e-06
BINS = 8
CORES = 2
F32 = jnp.float32
BF16 = jnp.bfloat16
SIN = (3.1415925800446924, -5.167706878924515, 2.5500313772531213, -0.5980451739748806, 0.0772201286897368)
COS = (0.9999999534666272, -4.934792858670076, 4.058411914063177, -1.331880160583308, 0.21969679727234584)
ROUNDER = 12582912.0
ROWS = 512
LANES = 256
WIDE = pltpu.CompilerParams(vmem_limit_bytes=16 * 1024 * 1024)
VMEM = pl.BlockSpec(memory_space=pltpu.VMEM)
HBM = pl.BlockSpec(memory_space=pltpu.HBM)


def horner(coefficients, z):
    total = coefficients[-1] * z + coefficients[-2]
    for value in coefficients[-3::-1]:
        total = total * z + value
    return total


def digits(value, unit):
    high = jnp.floor(value * (1.0 / unit))
    return high, value - unit * high


def spread_kernel(rf_ref, out_ref, held, sems):
    parts, bins = held.shape[:2]
    chans = out_ref.shape[0] // bins
    copy = pltpu.make_async_copy(rf_ref, held, sems.at[chans * parts])
    copy.start()
    copy.wait()
    copies = [
        pltpu.make_async_copy(held.at[part], out_ref.at[k * bins : (k + 1) * bins, part], sems.at[k * parts + part])
        for k in range(chans)
        for part in range(parts)
    ]
    for copy in copies:
        copy.start()
    for copy in copies:
        copy.wait()


def operator_kernel(elem_ref, vox_ref, bins_ref, upper, lower_ref, elem, vox, bins, lhs_ref, lower, sems):
    core = lax.axis_index("core")
    channels = elem.shape[1]
    share = upper.shape[2]
    voxels = share + lower.shape[2]
    copies = [
        pltpu.make_async_copy(source, target, sems.at[n])
        for n, (source, target) in enumerate(((elem_ref, elem), (vox_ref, vox), (bins_ref, bins)))
    ]
    for copy in copies:
        copy.start()
    for copy in copies:
        copy.wait()
    wavenumber = (32.0 + bins[lax.axis_index("bin")].astype(F32)) / 64.0
    scale = 2.0 / math.sqrt(channels)

    place = elem[...].astype(F32)
    high, low = digits(jnp.sum(place * place, axis=0, keepdims=True), 16.0)
    one = jnp.ones((1, channels), F32)
    lhs = jnp.concatenate([place, high, low, one, one, 0.0 * one], axis=0)
    lhs_ref[...] = jnp.transpose(lhs).astype(BF16)
    voxel = vox[:, pl.ds(pl.multiple_of(core * voxels, voxels), voxels)].astype(F32)
    high, low = digits(jnp.sum(voxel * voxel, axis=0, keepdims=True), 64.0)
    one = jnp.ones((1, voxels), F32)
    zero = 0.0 * one
    level = voxel[2:3]
    squares = jnp.concatenate([-2.0 * voxel, 16.0 * one, one, 64.0 * high, low, zero], axis=0).astype(BF16)
    depths = jnp.concatenate([zero, zero, -1.0 * one, zero, zero, level, zero, zero], axis=0).astype(BF16)

    def tile(index, carry, out_ref, lanes):
        rows = pl.ds(pl.multiple_of(index * ROWS, ROWS), ROWS)
        left = lhs_ref[rows]
        squared = jnp.dot(left, squares[:, lanes], preferred_element_type=F32)
        depth = jnp.dot(left, depths[:, lanes], preferred_element_type=F32)
        inverse = lax.rsqrt(squared)
        turns = (level[:, lanes] + squared * inverse) * wavenumber
        part = turns - ((turns + ROUNDER) - ROUNDER)
        z = part * part
        sine = part * horner(SIN, z)
        cosine = horner(COS, z)
        double = depth * inverse * scale
        lean = double * sine
        out_ref[0, rows] = (0.5 * double - lean * sine).astype(BF16)
        out_ref[1, rows] = (lean * cosine).astype(BF16)
        return carry

    lax.fori_loop(0, channels // ROWS, functools.partial(tile, out_ref=lower, lanes=slice(share, voxels)), 0)
    copy = pltpu.make_async_copy(lower, lower_ref, sems.at[3])
    copy.start()
    lax.fori_loop(0, channels // ROWS, functools.partial(tile, out_ref=upper, lanes=slice(0, share)), 0)
    copy.wait()


def arrange(samples, data):
    blocks, bins, _, group, width = samples.shape
    half = bins * group
    for k in range(blocks):
        for part in range(2):
            data[part * half : (part + 1) * half, k * width : (k + 1) * width] = samples[k, :, part].reshape(half, width)


def beamform(data, operator, start):
    half = data.shape[0] // 2
    for n in range(0, operator.shape[2], LANES):
        first, second = (
            jnp.dot(data[...], operator[which, :, n : n + LANES], preferred_element_type=F32) for which in range(2)
        )
        real = (first[:half] + second[half:]).astype(BF16)
        imag = (first[half:] - second[:half]).astype(BF16)
        yield slice(start + n, start + n + LANES), real, imag


def own_kernel(upper, lower_ref, samples, out_ref, lower, data, sem):
    copy = pltpu.make_async_copy(lower_ref, lower, sem)
    copy.start()
    arrange(samples, data)
    half = out_ref.shape[0] // 2
    for lanes, real, imag in beamform(data, upper, 0):
        out_ref[:half, lanes], out_ref[half:, lanes] = real, imag
    copy.wait()
    for lanes, real, imag in beamform(data, lower, upper.shape[2]):
        out_ref[:half, lanes], out_ref[half:, lanes] = real, imag


def other_kernel(upper, lower, samples, own, y_ref, gram_ref, data):
    core = lax.axis_index("core")
    frames = y_ref.shape[0] // 2
    half = frames // CORES
    here = pl.multiple_of(core * half, half)
    there = pl.multiple_of((1 - core) * half, half)
    y_ref[pl.ds(here, half)] = own[:half]
    y_ref[pl.ds(frames + here, half)] = own[half:]
    arrange(samples, data)
    for operator, start in ((upper, 0), (lower, upper.shape[2])):
        for lanes, real, imag in beamform(data, operator, start):
            y_ref[pl.ds(there, half), lanes], y_ref[pl.ds(frames + there, half), lanes] = real, imag
    y = y_ref[...]
    products = lax.dot_general(y, y, (((1,), (1,)), ((), ())), preferred_element_type=F32)
    gram_ref[...] = (products[:frames, :frames] + products[frames:, frames:]) + (
        products[:frames, frames:] - products[frames:, :frames]
    )


def halves(x):
    high = x.astype(BF16)
    return high, (x - high.astype(F32)).astype(BF16)


def product(left, right):
    left_high, left_low = halves(left)
    right_high, right_low = halves(right)
    return jnp.dot(
        jnp.concatenate([left_high, left_high, left_low], axis=1),
        jnp.concatenate([right_high, right_low, right_high], axis=0),
        preferred_element_type=F32,
    )


def unpack(packed):
    flipped = jnp.transpose(packed)
    return 0.5 * (packed + flipped), 0.5 * (packed - flipped), flipped


def filter_kernel(near, far, y_ref, peer_ref, out_ref, kept):
    core = lax.axis_index("core")
    frames = near.shape[0]
    half = frames // CORES
    packed = near[...] + far[...].astype(F32)
    squares = jnp.sum(packed * packed)
    factor = 4.0 / jnp.sqrt(jnp.full((1, 1), squares + EPSILON, F32))
    real, imag, flipped = unpack(packed)
    left = jnp.concatenate([real, imag], axis=1)
    second = product(left, jnp.concatenate([packed, flipped], axis=0)) * (factor * factor)
    third = product(left, jnp.concatenate([second, jnp.transpose(second)], axis=0)) * factor
    rows = lax.broadcasted_iota(jnp.int32, (frames, frames), 0)
    cols = lax.broadcasted_iota(jnp.int32, (frames, frames), 1)
    identity = jnp.where(rows == cols, 1.0, 0.0).astype(F32)
    real, imag, _ = unpack(identity - factor * packed + 0.3 * second - 0.03 * third)
    kept[0] = real.astype(BF16)
    kept[1] = imag.astype(BF16)
    real, imag = (kept[part, pl.ds(pl.multiple_of(core * half, half), half)] for part in range(2))
    matrix = jnp.concatenate(
        [jnp.concatenate([real, imag], axis=1), jnp.concatenate([-imag, real], axis=1)], axis=0
    )
    bins, parts, group, _ = out_ref.shape
    voxels = y_ref.shape[1]
    for source, place in ((y_ref, core), (peer_ref, 1 - core)):
        lanes = pl.ds(pl.multiple_of(place * voxels, voxels), voxels)
        applied = jnp.dot(matrix, source[...], preferred_element_type=F32).astype(BF16)
        for part in range(parts):
            for j in range(bins):
                row = part * half + j * group
                out_ref[j, part, :, lanes] = applied[row : row + group]


def place_kernel(got, out_ref, held, sems):
    bins, parts, group, voxels = got.shape
    size = group * bins
    rows = lax.broadcasted_iota(jnp.int32, (size, size), 0)
    cols = lax.broadcasted_iota(jnp.int32, (size, size), 1)
    turn = jnp.where(cols == (rows % bins) * group + rows // bins, 1.0, 0.0).astype(BF16)
    copies = [
        pltpu.make_async_copy(held.at[part], out_ref.at[:, part], sems.at[part]) for part in range(parts)
    ]
    for part in range(parts):
        moved = jnp.dot(turn, got[:, part].reshape(size, voxels), preferred_element_type=F32).astype(BF16)
        held[part] = moved.reshape(group, bins, voxels)
        copies[part].start()
    for copy in copies:
        copy.wait()


def shards(rf_data, elem_pos, vox_pos, subbands):
    parts, bins, group, width = rf_data.shape
    channels = elem_pos.shape[1]
    chans = channels // width
    voxels = vox_pos.shape[1] // CORES
    frames = group * bins * CORES
    half = frames // CORES

    def shape(*dims, dtype=BF16):
        return jax.ShapeDtypeStruct(dims, dtype)

    def swap(x):
        return lax.ppermute(x, "core", [(0, 1), (1, 0)])

    by_bin = pl.pallas_call(
        spread_kernel,
        name="spread",
        out_shape=shape(chans * bins, parts, group, width),
        in_specs=[HBM],
        out_specs=HBM,
        scratch_shapes=[pltpu.VMEM(rf_data.shape, BF16), pltpu.SemaphoreType.DMA((chans * parts + 1,))],
        compiler_params=WIDE,
    )(pltpu.with_memory_space_constraint(rf_data, pltpu.HBM))
    own = lax.all_to_all(by_bin, ("chan", "bin"), split_axis=0, concat_axis=0, tiled=True)

    share = voxels // 2
    upper, lower = pl.pallas_call(
        operator_kernel,
        name="operator",
        out_shape=(shape(2, channels, share), pltpu.HBM((2, channels, voxels - share), BF16)),
        in_specs=[HBM, HBM, HBM],
        out_specs=(VMEM, HBM),
        scratch_shapes=[
            pltpu.VMEM(elem_pos.shape, jnp.int32),
            pltpu.VMEM(vox_pos.shape, jnp.int32),
            pltpu.SMEM(subbands.shape, jnp.int32),
            pltpu.VMEM((channels, 8), BF16),
            pltpu.VMEM((2, channels, voxels - share), BF16),
            pltpu.SemaphoreType.DMA((4,)),
        ],
        compiler_params=WIDE,
        cost_estimate=pl.CostEstimate(
            flops=60 * channels * voxels,
            transcendentals=channels * voxels,
            bytes_accessed=4 * channels * voxels,
        ),
    )(*(pltpu.with_memory_space_constraint(x, pltpu.HBM) for x in (elem_pos, vox_pos, subbands)))

    own, upper, lower = lax.optimization_barrier((own, upper, lower))
    other = swap(own)
    own = own.reshape(chans, bins, parts, group, width)
    other = other.reshape(chans, bins, parts, group, width)

    beam_cost = pl.CostEstimate(
        flops=8 * half * channels * voxels * 2, transcendentals=0, bytes_accessed=4 * channels * voxels
    )
    mine, lower = pl.pallas_call(
        own_kernel,
        name="beam_own",
        out_shape=(shape(frames, voxels), shape(2, channels, voxels - share)),
        in_specs=[VMEM, HBM, VMEM],
        out_specs=(VMEM, VMEM),
        scratch_shapes=[
            pltpu.VMEM((frames, channels), BF16),
            pltpu.SemaphoreType.DMA,
        ],
        compiler_params=WIDE,
        cost_estimate=beam_cost,
    )(upper, pltpu.with_memory_space_constraint(lower, pltpu.HBM), own)
    y, gram = pl.pallas_call(
        other_kernel,
        name="beam_other",
        out_shape=(shape(2 * frames, voxels), shape(frames, frames, dtype=F32)),
        in_specs=[VMEM, VMEM, VMEM, VMEM],
        out_specs=(VMEM, VMEM),
        scratch_shapes=[pltpu.VMEM((frames, channels), BF16)],
        compiler_params=WIDE,
        cost_estimate=beam_cost,
    )(upper, lower, other, mine)

    total = gram + swap(gram)
    total, y = lax.optimization_barrier((total, y))
    peer = swap(y)
    narrow = total.astype(BF16)
    beside = lax.ppermute(
        narrow, ("chan", "core"), [(2 * a + c, 2 * (a ^ (3 if c else 1)) + c) for a in range(chans) for c in range(CORES)]
    )
    across = lax.ppermute(narrow, "chan", [(a, a ^ 2) for a in range(chans)])
    total = total + (beside.astype(F32) + swap(beside).astype(F32)) + across.astype(F32)
    far = lax.ppermute(total.astype(BF16), "chan", [(a, a ^ 4) for a in range(chans)])

    applied = pl.pallas_call(
        filter_kernel,
        name="filter",
        out_shape=shape(bins, parts, group, CORES * voxels),
        in_specs=[VMEM] * 4,
        out_specs=VMEM,
        scratch_shapes=[pltpu.VMEM((2, frames, frames), BF16)],
        compiler_params=WIDE,
    )(total, far, y, peer)

    got = lax.all_to_all(applied, "bin", split_axis=0, concat_axis=0, tiled=True)
    return pl.pallas_call(
        place_kernel,
        name="place",
        out_shape=shape(group, parts, bins, CORES * voxels),
        in_specs=[VMEM],
        out_specs=HBM,
        scratch_shapes=[
            pltpu.VMEM((parts, group, bins, CORES * voxels), BF16),
            pltpu.SemaphoreType.DMA((parts,)),
        ],
        compiler_params=WIDE,
    )(got)


def solution(mesh):
    chans = mesh.shape["chan"]
    fine = Mesh(mesh.devices.reshape(chans, BINS, CORES), ("chan", "bin", "core"))
    return jax.shard_map(
        shards,
        mesh=fine,
        in_specs=(P(None, None, ("bin", "core"), "chan"), P(), P(None, "chan"), P()),
        out_specs=P(("bin", "core"), None, None, "chan"),
        check_vma=False,
    )
```

```python
import functools
import math

import jax
import jax.numpy as jnp
from jax import lax
from jax.experimental import pallas as pl
from jax.experimental.pallas import tpu as pltpu
from jax.sharding import Mesh, PartitionSpec as P

EPSILON = 1e-06
BINS = 8
CORES = 2
F32 = jnp.float32
BF16 = jnp.bfloat16
ROOT = math.sqrt(2.0)
SIN = tuple(
    ROOT * c
    for c in (3.1415925800446924, -5.167706878924515, 2.5500313772531213, -0.5980451739748806, 0.0772201286897368)
)
COS = tuple(
    ROOT * c
    for c in (0.9999999534666272, -4.934792858670076, 4.058411914063177, -1.331880160583308, 0.21969679727234584)
)
ROUNDER = 12582912.0
ROWS = 512
LANES = 256
WIDE = pltpu.CompilerParams(vmem_limit_bytes=16 * 1024 * 1024)
VMEM = pl.BlockSpec(memory_space=pltpu.VMEM)
HBM = pl.BlockSpec(memory_space=pltpu.HBM)


def horner(coefficients, z):
    total = coefficients[-1] * z + coefficients[-2]
    for value in coefficients[-3::-1]:
        total = total * z + value
    return total


def digits(value, unit):
    high = jnp.floor(value * (1.0 / unit))
    return high, value - unit * high


def spread_kernel(
    rf_ref, elem_ref, vox_ref, bins_ref, out_ref, lhs_ref, rhs_ref, wave_ref, held, elem, vox, numbers, sems
):
    parts, bins = held.shape[:2]
    chans = out_ref.shape[0] // bins
    reads = [
        pltpu.make_async_copy(source, target, sems.at[n])
        for n, (source, target) in enumerate(
            ((rf_ref, held), (elem_ref, elem), (vox_ref, vox), (bins_ref, numbers))
        )
    ]
    for copy in reads:
        copy.start()
    reads[0].wait()
    copies = [
        pltpu.make_async_copy(
            held.at[part], out_ref.at[k * bins : (k + 1) * bins, part], sems.at[4 + k * parts + part]
        )
        for k in range(chans)
        for part in range(parts)
    ]
    for copy in copies:
        copy.start()
    for copy in reads[1:]:
        copy.wait()

    channels = elem.shape[1]
    place = elem[...].astype(F32)
    high, low = digits(jnp.sum(place * place, axis=0, keepdims=True), 16.0)
    one = jnp.ones((1, channels), F32)
    lhs_ref[...] = jnp.transpose(jnp.concatenate([place, high, low, one, one, 0.0 * one], axis=0)).astype(BF16)
    voxels = wave_ref.shape[1]
    voxel = vox[:, pl.ds(pl.multiple_of(lax.axis_index("core") * voxels, voxels), voxels)].astype(F32)
    high, low = digits(jnp.sum(voxel * voxel, axis=0, keepdims=True), 64.0)
    one = jnp.ones((1, voxels), F32)
    zero = 0.0 * one
    wave_ref[0:1] = voxel[2:3]
    wave_ref[1:2] = one * ((32.0 + numbers[lax.axis_index("bin")].astype(F32)) / 64.0)
    rhs_ref[0] = jnp.concatenate([-2.0 * voxel, 16.0 * one, one, 64.0 * high, low, zero], axis=0).astype(BF16)
    scale = 1.0 / math.sqrt(channels)
    rhs_ref[1] = jnp.concatenate(
        [zero, zero, -scale * one, zero, zero, scale * voxel[2:3], zero, zero], axis=0
    ).astype(BF16)
    for copy in copies:
        copy.wait()


def operator_kernel(lhs_ref, rhs_ref, wave_ref, upper, lower_ref, lower, sem):
    channels = lhs_ref.shape[0]
    share = upper.shape[2]
    voxels = share + lower.shape[2]

    def tile(index, carry, out_ref, lanes):
        rows = pl.ds(pl.multiple_of(index * ROWS, ROWS), ROWS)
        left = lhs_ref[rows]
        squared = jnp.dot(left, rhs_ref[0, :, lanes], preferred_element_type=F32)
        depth = jnp.dot(left, rhs_ref[1, :, lanes], preferred_element_type=F32)
        inverse = lax.rsqrt(squared)
        turns = (wave_ref[0:1, lanes] + squared * inverse) * wave_ref[1:2, lanes]
        part = turns - ((turns + ROUNDER) - ROUNDER)
        z = part * part
        sine = part * horner(SIN, z)
        cosine = horner(COS, z)
        weight = depth * inverse
        lean = weight * sine
        out_ref[0, rows] = (weight - lean * sine).astype(BF16)
        out_ref[1, rows] = (lean * cosine).astype(BF16)
        return carry

    lax.fori_loop(0, channels // ROWS, functools.partial(tile, out_ref=lower, lanes=slice(share, voxels)), 0)
    copy = pltpu.make_async_copy(lower, lower_ref, sem)
    copy.start()
    lax.fori_loop(0, channels // ROWS, functools.partial(tile, out_ref=upper, lanes=slice(0, share)), 0)
    copy.wait()


def arrange(samples, data):
    blocks, bins, _, group, width = samples.shape
    half = bins * group
    for k in range(blocks):
        for part in range(2):
            data[part * half : (part + 1) * half, k * width : (k + 1) * width] = samples[k, :, part].reshape(half, width)


def beamform(data, operator, start):
    half = data.shape[0] // 2
    for n in range(0, operator.shape[2], LANES):
        first, second = (
            jnp.dot(data[...], operator[which, :, n : n + LANES], preferred_element_type=F32) for which in range(2)
        )
        real = (first[:half] + second[half:]).astype(BF16)
        imag = (first[half:] - second[:half]).astype(BF16)
        yield slice(start + n, start + n + LANES), real, imag


def own_kernel(upper, lower_ref, samples, out_ref, lower, data, sem):
    copy = pltpu.make_async_copy(lower_ref, lower, sem)
    copy.start()
    arrange(samples, data)
    half = out_ref.shape[0] // 2
    for lanes, real, imag in beamform(data, upper, 0):
        out_ref[:half, lanes], out_ref[half:, lanes] = real, imag
    copy.wait()
    for lanes, real, imag in beamform(data, lower, upper.shape[2]):
        out_ref[:half, lanes], out_ref[half:, lanes] = real, imag


def other_kernel(upper, lower, samples, own, y_ref, keep_ref, send_ref, data, gram):
    core = lax.axis_index("core")
    frames = y_ref.shape[0] // 2
    half = frames // CORES
    here = pl.multiple_of(core * half, half)
    there = pl.multiple_of((1 - core) * half, half)
    y_ref[pl.ds(here, half)] = own[:half]
    y_ref[pl.ds(frames + here, half)] = own[half:]
    arrange(samples, data)
    for operator, start in ((upper, 0), (lower, upper.shape[2])):
        for lanes, real, imag in beamform(data, operator, start):
            y_ref[pl.ds(there, half), lanes], y_ref[pl.ds(frames + there, half), lanes] = real, imag
    y = y_ref[...]
    products = lax.dot_general(y, y, (((1,), (1,)), ((), ())), preferred_element_type=F32)
    gram[...] = (products[:frames, :frames] + products[frames:, frames:]) + (
        products[:frames, frames:] - products[frames:, :frames]
    )
    keep_ref[...] = gram[pl.ds(here, half), :]
    send_ref[...] = gram[pl.ds(there, half), :]


def halves(x):
    high = x.astype(BF16)
    return high, (x - high.astype(F32)).astype(BF16)


def product(left, right):
    left_high, left_low = halves(left)
    right_high, right_low = halves(right)
    return jnp.dot(
        jnp.concatenate([left_high, left_high, left_low], axis=1),
        jnp.concatenate([right_high, right_low, right_high], axis=0),
        preferred_element_type=F32,
    )


def unpack(packed):
    flipped = jnp.transpose(packed)
    return 0.5 * (packed + flipped), 0.5 * (packed - flipped), flipped


def filter_kernel(mine, twin, y_ref, peer_ref, out_ref, gram, kept):
    core = lax.axis_index("core")
    half, frames = mine.shape
    gram[pl.ds(pl.multiple_of(core * half, half), half), :] = mine[...]
    gram[pl.ds(pl.multiple_of((1 - core) * half, half), half), :] = twin[...]
    packed = gram[...]
    squares = jnp.sum(packed * packed)
    factor = 4.0 / jnp.sqrt(jnp.full((1, 1), squares + EPSILON, F32))
    real, imag, flipped = unpack(packed)
    left = jnp.concatenate([real, imag], axis=1)
    second = product(left, jnp.concatenate([packed, flipped], axis=0)) * (factor * factor)
    third = product(left, jnp.concatenate([second, jnp.transpose(second)], axis=0)) * factor
    rows = lax.broadcasted_iota(jnp.int32, (frames, frames), 0)
    cols = lax.broadcasted_iota(jnp.int32, (frames, frames), 1)
    identity = jnp.where(rows == cols, 1.0, 0.0).astype(F32)
    real, imag, _ = unpack(identity - factor * packed + 0.3 * second - 0.03 * third)
    kept[0] = real.astype(BF16)
    kept[1] = imag.astype(BF16)
    real, imag = (kept[part, pl.ds(pl.multiple_of(core * half, half), half)] for part in range(2))
    matrix = jnp.concatenate(
        [jnp.concatenate([real, imag], axis=1), jnp.concatenate([-imag, real], axis=1)], axis=0
    )
    bins, parts, group, _ = out_ref.shape
    voxels = y_ref.shape[1]
    for source, place in ((y_ref, core), (peer_ref, 1 - core)):
        lanes = pl.ds(pl.multiple_of(place * voxels, voxels), voxels)
        applied = jnp.dot(matrix, source[...], preferred_element_type=F32).astype(BF16)
        for part in range(parts):
            for j in range(bins):
                row = part * half + j * group
                out_ref[j, part, :, lanes] = applied[row : row + group]


def place_kernel(got, out_ref, held, sems):
    bins, parts, group, voxels = got.shape
    size = group * bins
    rows = lax.broadcasted_iota(jnp.int32, (size, size), 0)
    cols = lax.broadcasted_iota(jnp.int32, (size, size), 1)
    turn = jnp.where(cols == (rows % bins) * group + rows // bins, 1.0, 0.0).astype(BF16)
    copies = [
        pltpu.make_async_copy(held.at[part], out_ref.at[:, part], sems.at[part]) for part in range(parts)
    ]
    for part in range(parts):
        moved = jnp.dot(turn, got[:, part].reshape(size, voxels), preferred_element_type=F32).astype(BF16)
        held[part] = moved.reshape(group, bins, voxels)
        copies[part].start()
    for copy in copies:
        copy.wait()


def shards(rf_data, elem_pos, vox_pos, subbands):
    parts, bins, group, width = rf_data.shape
    channels = elem_pos.shape[1]
    chans = channels // width
    voxels = vox_pos.shape[1] // CORES
    frames = group * bins * CORES
    half = frames // CORES

    def shape(*dims, dtype=BF16):
        return jax.ShapeDtypeStruct(dims, dtype)

    def swap(x):
        return lax.ppermute(x, "core", [(0, 1), (1, 0)])

    def across(x, bits):
        return lax.ppermute(x, "chan", [(a, a ^ bits) for a in range(chans)])

    def in_hbm(x):
        return pltpu.with_memory_space_constraint(x, pltpu.HBM)

    by_bin, lhs, rhs, wave = pl.pallas_call(
        spread_kernel,
        name="spread",
        out_shape=(
            shape(chans * bins, parts, group, width),
            shape(channels, 8),
            shape(2, 8, voxels),
            shape(2, voxels, dtype=F32),
        ),
        in_specs=[HBM] * 4,
        out_specs=(HBM, VMEM, VMEM, VMEM),
        scratch_shapes=[
            pltpu.VMEM(rf_data.shape, BF16),
            pltpu.VMEM(elem_pos.shape, jnp.int32),
            pltpu.VMEM(vox_pos.shape, jnp.int32),
            pltpu.SMEM(subbands.shape, jnp.int32),
            pltpu.SemaphoreType.DMA((chans * parts + 4,)),
        ],
        compiler_params=WIDE,
    )(in_hbm(rf_data), in_hbm(elem_pos), in_hbm(vox_pos), in_hbm(subbands))
    own = lax.all_to_all(by_bin, ("chan", "bin"), split_axis=0, concat_axis=0, tiled=True)

    share = voxels // 2
    upper, lower = pl.pallas_call(
        operator_kernel,
        name="operator",
        out_shape=(shape(2, channels, share), pltpu.HBM((2, channels, voxels - share), BF16)),
        in_specs=[VMEM, VMEM, VMEM],
        out_specs=(VMEM, HBM),
        scratch_shapes=[
            pltpu.VMEM((2, channels, voxels - share), BF16),
            pltpu.SemaphoreType.DMA,
        ],
        compiler_params=WIDE,
        cost_estimate=pl.CostEstimate(
            flops=60 * channels * voxels,
            transcendentals=channels * voxels,
            bytes_accessed=4 * channels * voxels,
        ),
    )(lhs, rhs, wave)

    own, upper, lower = lax.optimization_barrier((own, upper, lower))
    other = swap(own)
    own = own.reshape(chans, bins, parts, group, width)
    other = other.reshape(chans, bins, parts, group, width)

    beam_cost = pl.CostEstimate(
        flops=8 * half * channels * voxels * 2, transcendentals=0, bytes_accessed=4 * channels * voxels
    )
    mine, lower = pl.pallas_call(
        own_kernel,
        name="beam_own",
        out_shape=(shape(frames, voxels), shape(2, channels, voxels - share)),
        in_specs=[VMEM, HBM, VMEM],
        out_specs=(VMEM, VMEM),
        scratch_shapes=[
            pltpu.VMEM((frames, channels), BF16),
            pltpu.SemaphoreType.DMA,
        ],
        compiler_params=WIDE,
        cost_estimate=beam_cost,
    )(upper, in_hbm(lower), own)
    y, keep, send = pl.pallas_call(
        other_kernel,
        name="beam_other",
        out_shape=(shape(2 * frames, voxels), shape(half, frames, dtype=F32), shape(half, frames, dtype=F32)),
        in_specs=[VMEM, VMEM, VMEM, VMEM],
        out_specs=(VMEM, VMEM, VMEM),
        scratch_shapes=[pltpu.VMEM((frames, channels), BF16), pltpu.VMEM((frames, frames), F32)],
        compiler_params=WIDE,
        cost_estimate=beam_cost,
    )(upper, lower, other, mine)

    total = keep + swap(send)
    total, y = lax.optimization_barrier((total, y))
    peer = swap(y)
    narrow = total.astype(BF16)
    total = total + sum(across(narrow, bits).astype(F32) for bits in (1, 3, 2))
    total = total + across(total.astype(BF16), 4).astype(F32)
    rest = swap(total)

    applied = pl.pallas_call(
        filter_kernel,
        name="filter",
        out_shape=shape(bins, parts, group, CORES * voxels),
        in_specs=[VMEM] * 4,
        out_specs=VMEM,
        scratch_shapes=[pltpu.VMEM((frames, frames), F32), pltpu.VMEM((2, frames, frames), BF16)],
        compiler_params=WIDE,
    )(total, rest, y, peer)

    got = lax.all_to_all(applied, "bin", split_axis=0, concat_axis=0, tiled=True)
    return pl.pallas_call(
        place_kernel,
        name="place",
        out_shape=shape(group, parts, bins, CORES * voxels),
        in_specs=[VMEM],
        out_specs=HBM,
        scratch_shapes=[
            pltpu.VMEM((parts, group, bins, CORES * voxels), BF16),
            pltpu.SemaphoreType.DMA((parts,)),
        ],
        compiler_params=WIDE,
    )(got)


def solution(mesh):
    chans = mesh.shape["chan"]
    fine = Mesh(mesh.devices.reshape(chans, BINS, CORES), ("chan", "bin", "core"))
    return jax.shard_map(
        shards,
        mesh=fine,
        in_specs=(P(None, None, ("bin", "core"), "chan"), P(), P(None, "chan"), P()),
        out_specs=P(("bin", "core"), None, None, "chan"),
        check_vma=False,
    )
```

```python
import functools
import math

import jax
import jax.numpy as jnp
from jax import lax
from jax.experimental import pallas as pl
from jax.experimental.pallas import tpu as pltpu
from jax.sharding import Mesh, PartitionSpec as P

EPSILON = 1e-06
BINS = 8
CORES = 2
F32 = jnp.float32
BF16 = jnp.bfloat16
ROOT = math.sqrt(2.0)
SIN = tuple(
    ROOT * c
    for c in (3.1415925800446924, -5.167706878924515, 2.5500313772531213, -0.5980451739748806, 0.0772201286897368)
)
COS = tuple(
    ROOT * c
    for c in (0.9999999534666272, -4.934792858670076, 4.058411914063177, -1.331880160583308, 0.21969679727234584)
)
ROUNDER = 12582912.0
ROWS = 512
LANES = 256
WIDE = pltpu.CompilerParams(vmem_limit_bytes=16 * 1024 * 1024)
VMEM = pl.BlockSpec(memory_space=pltpu.VMEM)
HBM = pl.BlockSpec(memory_space=pltpu.HBM)


def horner(coefficients, z):
    total = coefficients[-1] * z + coefficients[-2]
    for value in coefficients[-3::-1]:
        total = total * z + value
    return total


def digits(value, unit):
    high = jnp.floor(value * (1.0 / unit))
    return high, value - unit * high


def spread_kernel(
    rf_ref, elem_ref, vox_ref, bins_ref, out_ref, lhs_ref, rhs_ref, wave_ref, held, elem, vox, numbers, sems
):
    parts, bins = held.shape[:2]
    chans = out_ref.shape[0] // bins
    reads = [
        pltpu.make_async_copy(source, target, sems.at[n])
        for n, (source, target) in enumerate(
            ((rf_ref, held), (elem_ref, elem), (vox_ref, vox), (bins_ref, numbers))
        )
    ]
    for copy in reads:
        copy.start()
    reads[0].wait()
    copies = [
        pltpu.make_async_copy(
            held.at[part], out_ref.at[k * bins : (k + 1) * bins, part], sems.at[4 + k * parts + part]
        )
        for k in range(chans)
        for part in range(parts)
    ]
    for copy in copies:
        copy.start()
    for copy in reads[1:]:
        copy.wait()

    channels = elem.shape[1]
    place = elem[...].astype(F32)
    high, low = digits(jnp.sum(place * place, axis=0, keepdims=True), 16.0)
    one = jnp.ones((1, channels), F32)
    lhs_ref[...] = jnp.transpose(jnp.concatenate([place, high, low, one, one, 0.0 * one], axis=0)).astype(BF16)
    voxels = wave_ref.shape[1]
    voxel = vox[:, pl.ds(pl.multiple_of(lax.axis_index("core") * voxels, voxels), voxels)].astype(F32)
    high, low = digits(jnp.sum(voxel * voxel, axis=0, keepdims=True), 64.0)
    one = jnp.ones((1, voxels), F32)
    zero = 0.0 * one
    wave_ref[0:1] = voxel[2:3]
    wave_ref[1:2] = one * ((32.0 + numbers[lax.axis_index("bin")].astype(F32)) / 64.0)
    rhs_ref[0] = jnp.concatenate([-2.0 * voxel, 16.0 * one, one, 64.0 * high, low, zero], axis=0).astype(BF16)
    scale = 1.0 / math.sqrt(channels)
    rhs_ref[1] = jnp.concatenate(
        [zero, zero, -scale * one, zero, zero, scale * voxel[2:3], zero, zero], axis=0
    ).astype(BF16)
    for copy in copies:
        copy.wait()


def operator_kernel(lhs_ref, rhs_ref, wave_ref, upper, lower_ref, lower, sem):
    channels = lhs_ref.shape[0]
    share = upper.shape[2]
    voxels = share + lower.shape[2]

    def tile(index, carry, out_ref, lanes):
        rows = pl.ds(pl.multiple_of(index * ROWS, ROWS), ROWS)
        left = lhs_ref[rows]
        squared = jnp.dot(left, rhs_ref[0, :, lanes], preferred_element_type=F32)
        depth = jnp.dot(left, rhs_ref[1, :, lanes], preferred_element_type=F32)
        inverse = lax.rsqrt(squared)
        turns = (wave_ref[0:1, lanes] + squared * inverse) * wave_ref[1:2, lanes]
        part = turns - ((turns + ROUNDER) - ROUNDER)
        z = part * part
        sine = part * horner(SIN, z)
        cosine = horner(COS, z)
        weight = depth * inverse
        lean = weight * sine
        out_ref[0, rows] = (weight - lean * sine).astype(BF16)
        out_ref[1, rows] = (lean * cosine).astype(BF16)
        return carry

    lax.fori_loop(0, channels // ROWS, functools.partial(tile, out_ref=lower, lanes=slice(share, voxels)), 0)
    copy = pltpu.make_async_copy(lower, lower_ref, sem)
    copy.start()
    lax.fori_loop(0, channels // ROWS, functools.partial(tile, out_ref=upper, lanes=slice(0, share)), 0)
    copy.wait()


def arrange(samples, data):
    blocks, bins, _, group, width = samples.shape
    half = bins * group
    for k in range(blocks):
        for part in range(2):
            data[part * half : (part + 1) * half, k * width : (k + 1) * width] = samples[k, :, part].reshape(half, width)


def beamform(data, operator, start):
    half = data.shape[0] // 2
    for n in range(0, operator.shape[2], LANES):
        first, second = (
            jnp.dot(data[...], operator[which, :, n : n + LANES], preferred_element_type=F32) for which in range(2)
        )
        real = (first[:half] + second[half:]).astype(BF16)
        imag = (first[half:] - second[:half]).astype(BF16)
        yield slice(start + n, start + n + LANES), real, imag


def own_kernel(upper, lower_ref, samples, out_ref, lower, data, sem):
    copy = pltpu.make_async_copy(lower_ref, lower, sem)
    copy.start()
    arrange(samples, data)
    half = out_ref.shape[0] // 2
    for lanes, real, imag in beamform(data, upper, 0):
        out_ref[:half, lanes], out_ref[half:, lanes] = real, imag
    copy.wait()
    for lanes, real, imag in beamform(data, lower, upper.shape[2]):
        out_ref[:half, lanes], out_ref[half:, lanes] = real, imag


def other_kernel(upper, lower, samples, own, y_ref, keep_ref, send_ref, data, gram):
    core = lax.axis_index("core")
    frames = y_ref.shape[0] // 2
    half = frames // CORES
    here = pl.multiple_of(core * half, half)
    there = pl.multiple_of((1 - core) * half, half)
    y_ref[pl.ds(here, half)] = own[:half]
    y_ref[pl.ds(frames + here, half)] = own[half:]
    arrange(samples, data)
    for operator, start in ((upper, 0), (lower, upper.shape[2])):
        for lanes, real, imag in beamform(data, operator, start):
            y_ref[pl.ds(there, half), lanes], y_ref[pl.ds(frames + there, half), lanes] = real, imag
    y = y_ref[...]
    products = lax.dot_general(y, y, (((1,), (1,)), ((), ())), preferred_element_type=F32)
    gram[...] = (products[:frames, :frames] + products[frames:, frames:]) + (
        products[:frames, frames:] - products[frames:, :frames]
    )
    keep_ref[...] = gram[pl.ds(here, half), :]
    send_ref[...] = gram[pl.ds(there, half), :]


def halves(x):
    high = x.astype(BF16)
    return high, (x - high.astype(F32)).astype(BF16)


def product(left, right):
    left_high, left_low = halves(left)
    right_high, right_low = halves(right)
    return jnp.dot(
        jnp.concatenate([left_high, left_high, left_low], axis=1),
        jnp.concatenate([right_high, right_low, right_high], axis=0),
        preferred_element_type=F32,
    )


def unpack(packed):
    flipped = jnp.transpose(packed)
    return 0.5 * (packed + flipped), 0.5 * (packed - flipped), flipped


def filter_kernel(mine, far, twin, far_twin, y_ref, peer_ref, out_ref, gram, kept):
    core = lax.axis_index("core")
    half, frames = mine.shape
    gram[pl.ds(pl.multiple_of(core * half, half), half), :] = mine[...] + far[...].astype(F32)
    gram[pl.ds(pl.multiple_of((1 - core) * half, half), half), :] = twin[...] + far_twin[...].astype(F32)
    packed = gram[...]
    squares = jnp.sum(packed * packed)
    factor = 4.0 / jnp.sqrt(jnp.full((1, 1), squares + EPSILON, F32))
    real, imag, flipped = unpack(packed)
    left = jnp.concatenate([real, imag], axis=1)
    second = product(left, jnp.concatenate([packed, flipped], axis=0)) * (factor * factor)
    third = product(left, jnp.concatenate([second, jnp.transpose(second)], axis=0)) * factor
    rows = lax.broadcasted_iota(jnp.int32, (frames, frames), 0)
    cols = lax.broadcasted_iota(jnp.int32, (frames, frames), 1)
    identity = jnp.where(rows == cols, 1.0, 0.0).astype(F32)
    real, imag, _ = unpack(identity - factor * packed + 0.3 * second - 0.03 * third)
    kept[0] = real.astype(BF16)
    kept[1] = imag.astype(BF16)
    real, imag = (kept[part, pl.ds(pl.multiple_of(core * half, half), half)] for part in range(2))
    matrix = jnp.concatenate(
        [jnp.concatenate([real, imag], axis=1), jnp.concatenate([-imag, real], axis=1)], axis=0
    )
    bins, parts, group, _ = out_ref.shape
    voxels = y_ref.shape[1]
    for source, place in ((y_ref, core), (peer_ref, 1 - core)):
        lanes = pl.ds(pl.multiple_of(place * voxels, voxels), voxels)
        applied = jnp.dot(matrix, source[...], preferred_element_type=F32).astype(BF16)
        for part in range(parts):
            for j in range(bins):
                row = part * half + j * group
                out_ref[j, part, :, lanes] = applied[row : row + group]


def place_kernel(got, out_ref, held, sems):
    bins, parts, group, voxels = got.shape
    size = group * bins
    rows = lax.broadcasted_iota(jnp.int32, (size, size), 0)
    cols = lax.broadcasted_iota(jnp.int32, (size, size), 1)
    turn = jnp.where(cols == (rows % bins) * group + rows // bins, 1.0, 0.0).astype(BF16)
    copies = [
        pltpu.make_async_copy(held.at[part], out_ref.at[:, part], sems.at[part]) for part in range(parts)
    ]
    for part in range(parts):
        moved = jnp.dot(turn, got[:, part].reshape(size, voxels), preferred_element_type=F32).astype(BF16)
        held[part] = moved.reshape(group, bins, voxels)
        copies[part].start()
    for copy in copies:
        copy.wait()


def shards(rf_data, elem_pos, vox_pos, subbands):
    parts, bins, group, width = rf_data.shape
    channels = elem_pos.shape[1]
    chans = channels // width
    voxels = vox_pos.shape[1] // CORES
    frames = group * bins * CORES
    half = frames // CORES

    def shape(*dims, dtype=BF16):
        return jax.ShapeDtypeStruct(dims, dtype)

    def swap(x):
        return lax.ppermute(x, "core", [(0, 1), (1, 0)])

    def across(x, bits):
        return lax.ppermute(x, "chan", [(a, a ^ bits) for a in range(chans)])

    def in_hbm(x):
        return pltpu.with_memory_space_constraint(x, pltpu.HBM)

    by_bin, lhs, rhs, wave = pl.pallas_call(
        spread_kernel,
        name="spread",
        out_shape=(
            shape(chans * bins, parts, group, width),
            shape(channels, 8),
            shape(2, 8, voxels),
            shape(2, voxels, dtype=F32),
        ),
        in_specs=[HBM] * 4,
        out_specs=(HBM, VMEM, VMEM, VMEM),
        scratch_shapes=[
            pltpu.VMEM(rf_data.shape, BF16),
            pltpu.VMEM(elem_pos.shape, jnp.int32),
            pltpu.VMEM(vox_pos.shape, jnp.int32),
            pltpu.SMEM(subbands.shape, jnp.int32),
            pltpu.SemaphoreType.DMA((chans * parts + 4,)),
        ],
        compiler_params=WIDE,
    )(in_hbm(rf_data), in_hbm(elem_pos), in_hbm(vox_pos), in_hbm(subbands))
    own = lax.all_to_all(by_bin, ("chan", "bin"), split_axis=0, concat_axis=0, tiled=True)

    share = voxels // 2
    upper, lower = pl.pallas_call(
        operator_kernel,
        name="operator",
        out_shape=(shape(2, channels, share), pltpu.HBM((2, channels, voxels - share), BF16)),
        in_specs=[VMEM, VMEM, VMEM],
        out_specs=(VMEM, HBM),
        scratch_shapes=[
            pltpu.VMEM((2, channels, voxels - share), BF16),
            pltpu.SemaphoreType.DMA,
        ],
        compiler_params=WIDE,
        cost_estimate=pl.CostEstimate(
            flops=60 * channels * voxels,
            transcendentals=channels * voxels,
            bytes_accessed=4 * channels * voxels,
        ),
    )(lhs, rhs, wave)

    own, upper, lower = lax.optimization_barrier((own, upper, lower))
    other = swap(own)
    own = own.reshape(chans, bins, parts, group, width)
    other = other.reshape(chans, bins, parts, group, width)

    beam_cost = pl.CostEstimate(
        flops=8 * half * channels * voxels * 2, transcendentals=0, bytes_accessed=4 * channels * voxels
    )
    mine, lower = pl.pallas_call(
        own_kernel,
        name="beam_own",
        out_shape=(shape(frames, voxels), shape(2, channels, voxels - share)),
        in_specs=[VMEM, HBM, VMEM],
        out_specs=(VMEM, VMEM),
        scratch_shapes=[
            pltpu.VMEM((frames, channels), BF16),
            pltpu.SemaphoreType.DMA,
        ],
        compiler_params=WIDE,
        cost_estimate=beam_cost,
    )(upper, in_hbm(lower), own)
    y, keep, send = pl.pallas_call(
        other_kernel,
        name="beam_other",
        out_shape=(shape(2 * frames, voxels), shape(half, frames, dtype=F32), shape(half, frames, dtype=F32)),
        in_specs=[VMEM, VMEM, VMEM, VMEM],
        out_specs=(VMEM, VMEM, VMEM),
        scratch_shapes=[pltpu.VMEM((frames, channels), BF16), pltpu.VMEM((frames, frames), F32)],
        compiler_params=WIDE,
        cost_estimate=beam_cost,
    )(upper, lower, other, mine)

    total = keep + swap(send)
    total, y = lax.optimization_barrier((total, y))
    peer = swap(y)
    narrow = total.astype(BF16)
    total = total + sum(across(narrow, bits).astype(F32) for bits in (1, 3, 2))
    narrow = total.astype(BF16)
    far = across(narrow, 4)
    far_twin = lax.ppermute(
        narrow, ("chan", "core"), [(2 * a + c, 2 * (a ^ 4) + 1 - c) for a in range(chans) for c in range(CORES)]
    )
    twin = swap(total)

    applied = pl.pallas_call(
        filter_kernel,
        name="filter",
        out_shape=shape(bins, parts, group, CORES * voxels),
        in_specs=[VMEM] * 6,
        out_specs=VMEM,
        scratch_shapes=[pltpu.VMEM((frames, frames), F32), pltpu.VMEM((2, frames, frames), BF16)],
        compiler_params=WIDE,
    )(total, far, twin, far_twin, y, peer)

    got = lax.all_to_all(applied, "bin", split_axis=0, concat_axis=0, tiled=True)
    return pl.pallas_call(
        place_kernel,
        name="place",
        out_shape=shape(group, parts, bins, CORES * voxels),
        in_specs=[VMEM],
        out_specs=HBM,
        scratch_shapes=[
            pltpu.VMEM((parts, group, bins, CORES * voxels), BF16),
            pltpu.SemaphoreType.DMA((parts,)),
        ],
        compiler_params=WIDE,
    )(got)


def solution(mesh):
    chans = mesh.shape["chan"]
    fine = Mesh(mesh.devices.reshape(chans, BINS, CORES), ("chan", "bin", "core"))
    return jax.shard_map(
        shards,
        mesh=fine,
        in_specs=(P(None, None, ("bin", "core"), "chan"), P(), P(None, "chan"), P()),
        out_specs=P(("bin", "core"), None, None, "chan"),
        check_vma=False,
    )
```

```python
import functools
import math

import jax
import jax.numpy as jnp
from jax import lax
from jax.experimental import pallas as pl
from jax.experimental.pallas import tpu as pltpu
from jax.sharding import Mesh, PartitionSpec as P

EPSILON = 1e-06
BINS = 8
CORES = 2
F32 = jnp.float32
BF16 = jnp.bfloat16
ROOT = math.sqrt(2.0)
SIN = tuple(
    ROOT * c
    for c in (3.1415925800446924, -5.167706878924515, 2.5500313772531213, -0.5980451739748806, 0.0772201286897368)
)
COS = tuple(
    ROOT * c
    for c in (0.9999999534666272, -4.934792858670076, 4.058411914063177, -1.331880160583308, 0.21969679727234584)
)
ROUNDER = 12582912.0
ROWS = 512
LANES = 256
WIDE = pltpu.CompilerParams(vmem_limit_bytes=16 * 1024 * 1024)
VMEM = pl.BlockSpec(memory_space=pltpu.VMEM)
HBM = pl.BlockSpec(memory_space=pltpu.HBM)


def horner(coefficients, z):
    total = coefficients[-1] * z + coefficients[-2]
    for value in coefficients[-3::-1]:
        total = total * z + value
    return total


def digits(value, unit):
    high = jnp.floor(value * (1.0 / unit))
    return high, value - unit * high


def spread_kernel(
    rf_ref, elem_ref, vox_ref, bins_ref, out_ref, lhs_ref, rhs_ref, wave_ref, held, elem, vox, numbers, sems
):
    parts, bins = held.shape[:2]
    chans = out_ref.shape[0] // bins
    reads = [
        pltpu.make_async_copy(source, target, sems.at[n])
        for n, (source, target) in enumerate(
            ((rf_ref, held), (elem_ref, elem), (vox_ref, vox), (bins_ref, numbers))
        )
    ]
    for copy in reads:
        copy.start()
    reads[0].wait()
    copies = [
        pltpu.make_async_copy(
            held.at[part], out_ref.at[k * bins : (k + 1) * bins, part], sems.at[4 + k * parts + part]
        )
        for k in range(chans)
        for part in range(parts)
    ]
    for copy in copies:
        copy.start()
    for copy in reads[1:]:
        copy.wait()

    channels = elem.shape[1]
    place = elem[...].astype(F32)
    high, low = digits(jnp.sum(place * place, axis=0, keepdims=True), 16.0)
    one = jnp.ones((1, channels), F32)
    lhs_ref[...] = jnp.transpose(jnp.concatenate([place, high, low, one, one, 0.0 * one], axis=0)).astype(BF16)
    voxels = wave_ref.shape[1]
    voxel = vox[:, pl.ds(pl.multiple_of(lax.axis_index("core") * voxels, voxels), voxels)].astype(F32)
    high, low = digits(jnp.sum(voxel * voxel, axis=0, keepdims=True), 64.0)
    one = jnp.ones((1, voxels), F32)
    zero = 0.0 * one
    wave_ref[0:1] = voxel[2:3]
    wave_ref[1:2] = one * ((32.0 + numbers[lax.axis_index("bin")].astype(F32)) / 64.0)
    rhs_ref[0] = jnp.concatenate([-2.0 * voxel, 16.0 * one, one, 64.0 * high, low, zero], axis=0).astype(BF16)
    scale = 1.0 / math.sqrt(channels)
    rhs_ref[1] = jnp.concatenate(
        [zero, zero, -scale * one, zero, zero, scale * voxel[2:3], zero, zero], axis=0
    ).astype(BF16)
    for copy in copies:
        copy.wait()


def operator_kernel(lhs_ref, rhs_ref, wave_ref, upper, lower_ref, lower, sem):
    channels = lhs_ref.shape[0]
    share = upper.shape[2]
    voxels = share + lower.shape[2]

    def tile(index, carry, out_ref, lanes):
        rows = pl.ds(pl.multiple_of(index * ROWS, ROWS), ROWS)
        left = lhs_ref[rows]
        squared = jnp.dot(left, rhs_ref[0, :, lanes], preferred_element_type=F32)
        depth = jnp.dot(left, rhs_ref[1, :, lanes], preferred_element_type=F32)
        inverse = lax.rsqrt(squared)
        turns = (wave_ref[0:1, lanes] + squared * inverse) * wave_ref[1:2, lanes]
        part = turns - ((turns + ROUNDER) - ROUNDER)
        z = part * part
        sine = part * horner(SIN, z)
        cosine = horner(COS, z)
        weight = depth * inverse
        lean = weight * sine
        out_ref[0, rows] = (weight - lean * sine).astype(BF16)
        out_ref[1, rows] = (lean * cosine).astype(BF16)
        return carry

    lax.fori_loop(0, channels // ROWS, functools.partial(tile, out_ref=lower, lanes=slice(share, voxels)), 0)
    copy = pltpu.make_async_copy(lower, lower_ref, sem)
    copy.start()
    lax.fori_loop(0, channels // ROWS, functools.partial(tile, out_ref=upper, lanes=slice(0, share)), 0)
    copy.wait()


def arrange(samples, data):
    blocks, bins, _, group, width = samples.shape
    half = bins * group
    for k in range(blocks):
        for part in range(2):
            data[part * half : (part + 1) * half, k * width : (k + 1) * width] = samples[k, :, part].reshape(half, width)


def beamform(data, operator, start):
    half = data.shape[0] // 2
    for n in range(0, operator.shape[2], LANES):
        first, second = (
            jnp.dot(data[...], operator[which, :, n : n + LANES], preferred_element_type=F32) for which in range(2)
        )
        real = (first[:half] + second[half:]).astype(BF16)
        imag = (first[half:] - second[:half]).astype(BF16)
        yield slice(start + n, start + n + LANES), real, imag


def own_kernel(upper, lower_ref, samples, out_ref, lower, data, sem):
    copy = pltpu.make_async_copy(lower_ref, lower, sem)
    copy.start()
    arrange(samples, data)
    half = out_ref.shape[0] // 2
    for lanes, real, imag in beamform(data, upper, 0):
        out_ref[:half, lanes], out_ref[half:, lanes] = real, imag
    copy.wait()
    for lanes, real, imag in beamform(data, lower, upper.shape[2]):
        out_ref[:half, lanes], out_ref[half:, lanes] = real, imag


def gram_rows(y_ref, start):
    frames = y_ref.shape[0] // 2
    half = frames // CORES
    left = jnp.concatenate([y_ref[pl.ds(start, half)], y_ref[pl.ds(frames + start, half)]], axis=0)
    products = lax.dot_general(left, y_ref[...], (((1,), (1,)), ((), ())), preferred_element_type=F32)
    return (products[:half, :frames] + products[half:, frames:]) + (
        products[:half, frames:] - products[half:, :frames]
    )


def keep_kernel(y_ref, out_ref):
    half = out_ref.shape[0]
    out_ref[...] = gram_rows(y_ref, pl.multiple_of(lax.axis_index("core") * half, half))


def other_kernel(upper, lower, samples, own, y_ref, send_ref, data):
    core = lax.axis_index("core")
    frames = y_ref.shape[0] // 2
    half = frames // CORES
    here = pl.multiple_of(core * half, half)
    there = pl.multiple_of((1 - core) * half, half)
    y_ref[pl.ds(here, half)] = own[:half]
    y_ref[pl.ds(frames + here, half)] = own[half:]
    arrange(samples, data)
    for operator, start in ((upper, 0), (lower, upper.shape[2])):
        for lanes, real, imag in beamform(data, operator, start):
            y_ref[pl.ds(there, half), lanes], y_ref[pl.ds(frames + there, half), lanes] = real, imag
    send_ref[...] = gram_rows(y_ref, there)


def halves(x):
    high = x.astype(BF16)
    return high, (x - high.astype(F32)).astype(BF16)


def product(left, right):
    left = left.astype(BF16)
    return jnp.dot(
        jnp.concatenate([left, left], axis=1), jnp.concatenate(halves(right), axis=0), preferred_element_type=F32
    )


def unpack(packed):
    flipped = jnp.transpose(packed)
    return 0.5 * (packed + flipped), 0.5 * (packed - flipped), flipped


def filter_kernel(mine, far, twin, far_twin, y_ref, peer_ref, out_ref, gram, kept):
    core = lax.axis_index("core")
    half, frames = mine.shape
    gram[pl.ds(pl.multiple_of(core * half, half), half), :] = mine[...] + far[...].astype(F32)
    gram[pl.ds(pl.multiple_of((1 - core) * half, half), half), :] = twin[...] + far_twin[...].astype(F32)
    packed = gram[...]
    squares = jnp.sum(packed * packed)
    factor = 4.0 / jnp.sqrt(jnp.full((1, 1), squares + EPSILON, F32))
    real, imag, flipped = unpack(packed)
    left = jnp.concatenate([real, imag], axis=1)
    second = product(left, jnp.concatenate([packed, flipped], axis=0)) * (factor * factor)
    right = jnp.concatenate([second, jnp.transpose(second)], axis=0).astype(BF16)
    third = jnp.dot(left.astype(BF16), right, preferred_element_type=F32) * factor
    rows = lax.broadcasted_iota(jnp.int32, (frames, frames), 0)
    cols = lax.broadcasted_iota(jnp.int32, (frames, frames), 1)
    identity = jnp.where(rows == cols, 1.0, 0.0).astype(F32)
    real, imag, _ = unpack(identity - factor * packed + 0.3 * second - 0.03 * third)
    kept[0] = real.astype(BF16)
    kept[1] = imag.astype(BF16)
    real, imag = (kept[part, pl.ds(pl.multiple_of(core * half, half), half)] for part in range(2))
    matrix = jnp.concatenate(
        [jnp.concatenate([real, imag], axis=1), jnp.concatenate([-imag, real], axis=1)], axis=0
    )
    bins, parts, group, _ = out_ref.shape
    voxels = y_ref.shape[1]
    for source, place in ((y_ref, core), (peer_ref, 1 - core)):
        lanes = pl.ds(pl.multiple_of(place * voxels, voxels), voxels)
        applied = jnp.dot(matrix, source[...], preferred_element_type=F32).astype(BF16)
        for part in range(parts):
            for j in range(bins):
                row = part * half + j * group
                out_ref[j, part, :, lanes] = applied[row : row + group]


def place_kernel(got, out_ref, held, sems):
    bins, parts, group, voxels = got.shape
    size = group * bins
    rows = lax.broadcasted_iota(jnp.int32, (size, size), 0)
    cols = lax.broadcasted_iota(jnp.int32, (size, size), 1)
    turn = jnp.where(cols == (rows % bins) * group + rows // bins, 1.0, 0.0).astype(BF16)
    copies = [
        pltpu.make_async_copy(held.at[part], out_ref.at[:, part], sems.at[part]) for part in range(parts)
    ]
    for part in range(parts):
        moved = jnp.dot(turn, got[:, part].reshape(size, voxels), preferred_element_type=F32).astype(BF16)
        held[part] = moved.reshape(group, bins, voxels)
        copies[part].start()
    for copy in copies:
        copy.wait()


def shards(rf_data, elem_pos, vox_pos, subbands):
    parts, bins, group, width = rf_data.shape
    channels = elem_pos.shape[1]
    chans = channels // width
    voxels = vox_pos.shape[1] // CORES
    frames = group * bins * CORES
    half = frames // CORES

    def shape(*dims, dtype=BF16):
        return jax.ShapeDtypeStruct(dims, dtype)

    def swap(x):
        return lax.ppermute(x, "core", [(0, 1), (1, 0)])

    def across(x, bits):
        return lax.ppermute(x, "chan", [(a, a ^ bits) for a in range(chans)])

    def in_hbm(x):
        return pltpu.with_memory_space_constraint(x, pltpu.HBM)

    by_bin, lhs, rhs, wave = pl.pallas_call(
        spread_kernel,
        name="spread",
        out_shape=(
            shape(chans * bins, parts, group, width),
            shape(channels, 8),
            shape(2, 8, voxels),
            shape(2, voxels, dtype=F32),
        ),
        in_specs=[HBM] * 4,
        out_specs=(HBM, VMEM, VMEM, VMEM),
        scratch_shapes=[
            pltpu.VMEM(rf_data.shape, BF16),
            pltpu.VMEM(elem_pos.shape, jnp.int32),
            pltpu.VMEM(vox_pos.shape, jnp.int32),
            pltpu.SMEM(subbands.shape, jnp.int32),
            pltpu.SemaphoreType.DMA((chans * parts + 4,)),
        ],
        compiler_params=WIDE,
    )(in_hbm(rf_data), in_hbm(elem_pos), in_hbm(vox_pos), in_hbm(subbands))
    own = lax.all_to_all(by_bin, ("chan", "bin"), split_axis=0, concat_axis=0, tiled=True)

    share = voxels // 2
    upper, lower = pl.pallas_call(
        operator_kernel,
        name="operator",
        out_shape=(shape(2, channels, share), pltpu.HBM((2, channels, voxels - share), BF16)),
        in_specs=[VMEM, VMEM, VMEM],
        out_specs=(VMEM, HBM),
        scratch_shapes=[
            pltpu.VMEM((2, channels, voxels - share), BF16),
            pltpu.SemaphoreType.DMA,
        ],
        compiler_params=WIDE,
        cost_estimate=pl.CostEstimate(
            flops=60 * channels * voxels,
            transcendentals=channels * voxels,
            bytes_accessed=4 * channels * voxels,
        ),
    )(lhs, rhs, wave)

    own, upper, lower = lax.optimization_barrier((own, upper, lower))
    other = swap(own)
    own = own.reshape(chans, bins, parts, group, width)
    other = other.reshape(chans, bins, parts, group, width)

    beam_cost = pl.CostEstimate(
        flops=8 * half * channels * voxels * 2, transcendentals=0, bytes_accessed=4 * channels * voxels
    )
    mine, lower = pl.pallas_call(
        own_kernel,
        name="beam_own",
        out_shape=(shape(frames, voxels), shape(2, channels, voxels - share)),
        in_specs=[VMEM, HBM, VMEM],
        out_specs=(VMEM, VMEM),
        scratch_shapes=[
            pltpu.VMEM((frames, channels), BF16),
            pltpu.SemaphoreType.DMA,
        ],
        compiler_params=WIDE,
        cost_estimate=beam_cost,
    )(upper, in_hbm(lower), own)
    y, send = pl.pallas_call(
        other_kernel,
        name="beam_other",
        out_shape=(shape(2 * frames, voxels), shape(half, frames, dtype=F32)),
        in_specs=[VMEM, VMEM, VMEM, VMEM],
        out_specs=(VMEM, VMEM),
        scratch_shapes=[pltpu.VMEM((frames, channels), BF16)],
        compiler_params=WIDE,
        cost_estimate=beam_cost,
    )(upper, lower, other, mine)

    sent = swap(send)
    keep = pl.pallas_call(
        keep_kernel,
        name="gram_keep",
        out_shape=shape(half, frames, dtype=F32),
        in_specs=[VMEM],
        out_specs=VMEM,
        compiler_params=WIDE,
        cost_estimate=pl.CostEstimate(
            flops=8 * half * frames * voxels, transcendentals=0, bytes_accessed=4 * frames * voxels
        ),
    )(y)
    total = keep + sent
    total, y = lax.optimization_barrier((total, y))
    peer = swap(y)
    narrow = total.astype(BF16)
    total = total + sum(across(narrow, bits).astype(F32) for bits in (1, 3, 2))
    narrow = total.astype(BF16)
    far = across(narrow, 4)
    far_twin = lax.ppermute(
        narrow, ("chan", "core"), [(2 * a + c, 2 * (a ^ 4) + 1 - c) for a in range(chans) for c in range(CORES)]
    )
    twin = swap(total)

    applied = pl.pallas_call(
        filter_kernel,
        name="filter",
        out_shape=shape(bins, parts, group, CORES * voxels),
        in_specs=[VMEM] * 6,
        out_specs=VMEM,
        scratch_shapes=[pltpu.VMEM((frames, frames), F32), pltpu.VMEM((2, frames, frames), BF16)],
        compiler_params=WIDE,
    )(total, far, twin, far_twin, y, peer)

    got = lax.all_to_all(applied, "bin", split_axis=0, concat_axis=0, tiled=True)
    return pl.pallas_call(
        place_kernel,
        name="place",
        out_shape=shape(group, parts, bins, CORES * voxels),
        in_specs=[VMEM],
        out_specs=HBM,
        scratch_shapes=[
            pltpu.VMEM((parts, group, bins, CORES * voxels), BF16),
            pltpu.SemaphoreType.DMA((parts,)),
        ],
        compiler_params=WIDE,
    )(got)


def solution(mesh):
    chans = mesh.shape["chan"]
    fine = Mesh(mesh.devices.reshape(chans, BINS, CORES), ("chan", "bin", "core"))
    return jax.shard_map(
        shards,
        mesh=fine,
        in_specs=(P(None, None, ("bin", "core"), "chan"), P(), P(None, "chan"), P()),
        out_specs=P(("bin", "core"), None, None, "chan"),
        check_vma=False,
    )
```

```python
import functools
import math

import jax
import jax.numpy as jnp
from jax import lax
from jax.experimental import pallas as pl
from jax.experimental.pallas import tpu as pltpu
from jax.sharding import Mesh, PartitionSpec as P

EPSILON = 1e-06
BINS = 8
CORES = 2
F32 = jnp.float32
BF16 = jnp.bfloat16
ROOT = math.sqrt(2.0)
SIN = tuple(
    ROOT * c
    for c in (3.1415925800446924, -5.167706878924515, 2.5500313772531213, -0.5980451739748806, 0.0772201286897368)
)
COS = tuple(
    ROOT * c
    for c in (0.9999999534666272, -4.934792858670076, 4.058411914063177, -1.331880160583308, 0.21969679727234584)
)
ROUNDER = 12582912.0
ROWS = 512
LANES = 256
WIDE = pltpu.CompilerParams(vmem_limit_bytes=16 * 1024 * 1024)
VMEM = pl.BlockSpec(memory_space=pltpu.VMEM)
HBM = pl.BlockSpec(memory_space=pltpu.HBM)


def horner(coefficients, z):
    total = coefficients[-1] * z + coefficients[-2]
    for value in coefficients[-3::-1]:
        total = total * z + value
    return total


def digits(value, unit):
    high = jnp.floor(value * (1.0 / unit))
    return high, value - unit * high


def spread_kernel(
    rf_ref, elem_ref, vox_ref, bins_ref, out_ref, lhs_ref, rhs_ref, wave_ref, held, elem, vox, numbers, sems
):
    parts, bins = held.shape[:2]
    chans = out_ref.shape[0] // bins
    reads = [
        pltpu.make_async_copy(source, target, sems.at[n])
        for n, (source, target) in enumerate(
            ((rf_ref, held), (elem_ref, elem), (vox_ref, vox), (bins_ref, numbers))
        )
    ]
    for copy in reads:
        copy.start()
    reads[0].wait()
    copies = [
        pltpu.make_async_copy(
            held.at[part], out_ref.at[k * bins : (k + 1) * bins, part], sems.at[4 + k * parts + part]
        )
        for k in range(chans)
        for part in range(parts)
    ]
    for copy in copies:
        copy.start()
    for copy in reads[1:]:
        copy.wait()

    channels = elem.shape[1]
    place = elem[...].astype(F32)
    high, low = digits(jnp.sum(place * place, axis=0, keepdims=True), 16.0)
    one = jnp.ones((1, channels), F32)
    lhs_ref[...] = jnp.transpose(jnp.concatenate([place, high, low, one, one, 0.0 * one], axis=0)).astype(BF16)
    voxels = wave_ref.shape[1]
    voxel = vox[:, pl.ds(pl.multiple_of(lax.axis_index("core") * voxels, voxels), voxels)].astype(F32)
    high, low = digits(jnp.sum(voxel * voxel, axis=0, keepdims=True), 64.0)
    one = jnp.ones((1, voxels), F32)
    zero = 0.0 * one
    wave_ref[0:1] = voxel[2:3]
    wave_ref[1:2] = one * ((32.0 + numbers[lax.axis_index("bin")].astype(F32)) / 64.0)
    rhs_ref[0] = jnp.concatenate([-2.0 * voxel, 16.0 * one, one, 64.0 * high, low, zero], axis=0).astype(BF16)
    scale = 1.0 / math.sqrt(channels)
    rhs_ref[1] = jnp.concatenate(
        [zero, zero, -scale * one, zero, zero, scale * voxel[2:3], zero, zero], axis=0
    ).astype(BF16)
    for copy in copies:
        copy.wait()


def operator_kernel(lhs_ref, rhs_ref, wave_ref, upper, lower_ref, lower, sem):
    channels = lhs_ref.shape[0]
    share = upper.shape[2]
    voxels = share + lower.shape[2]

    def tile(index, carry, out_ref, lanes):
        rows = pl.ds(pl.multiple_of(index * ROWS, ROWS), ROWS)
        left = lhs_ref[rows]
        squared = jnp.dot(left, rhs_ref[0, :, lanes], preferred_element_type=F32)
        depth = jnp.dot(left, rhs_ref[1, :, lanes], preferred_element_type=F32)
        inverse = lax.rsqrt(squared)
        turns = (wave_ref[0:1, lanes] + squared * inverse) * wave_ref[1:2, lanes]
        part = turns - ((turns + ROUNDER) - ROUNDER)
        z = part * part
        sine = part * horner(SIN, z)
        cosine = horner(COS, z)
        weight = depth * inverse
        lean = weight * sine
        out_ref[0, rows] = (weight - lean * sine).astype(BF16)
        out_ref[1, rows] = (lean * cosine).astype(BF16)
        return carry

    lax.fori_loop(0, channels // ROWS, functools.partial(tile, out_ref=lower, lanes=slice(share, voxels)), 0)
    copy = pltpu.make_async_copy(lower, lower_ref, sem)
    copy.start()
    lax.fori_loop(0, channels // ROWS, functools.partial(tile, out_ref=upper, lanes=slice(0, share)), 0)
    copy.wait()


def arrange(samples, data):
    blocks, bins, _, group, width = samples.shape
    half = bins * group
    for k in range(blocks):
        for part in range(2):
            data[part * half : (part + 1) * half, k * width : (k + 1) * width] = samples[k, :, part].reshape(half, width)


def beamform(data, operator, start):
    half = data.shape[0] // 2
    for n in range(0, operator.shape[2], LANES):
        first, second = (
            jnp.dot(data[...], operator[which, :, n : n + LANES], preferred_element_type=F32) for which in range(2)
        )
        real = (first[:half] + second[half:]).astype(BF16)
        imag = (first[half:] - second[:half]).astype(BF16)
        yield slice(start + n, start + n + LANES), real, imag


def own_kernel(upper, lower_ref, samples, out_ref, lower, data, sem):
    copy = pltpu.make_async_copy(lower_ref, lower, sem)
    copy.start()
    arrange(samples, data)
    half = out_ref.shape[0] // 2
    for lanes, real, imag in beamform(data, upper, 0):
        out_ref[:half, lanes], out_ref[half:, lanes] = real, imag
    copy.wait()
    for lanes, real, imag in beamform(data, lower, upper.shape[2]):
        out_ref[:half, lanes], out_ref[half:, lanes] = real, imag


def other_kernel(upper, lower, samples, own, y_ref, keep_ref, send_ref, data, gram):
    core = lax.axis_index("core")
    frames = y_ref.shape[0] // 2
    half = frames // CORES
    here = pl.multiple_of(core * half, half)
    there = pl.multiple_of((1 - core) * half, half)
    y_ref[pl.ds(here, half)] = own[:half]
    y_ref[pl.ds(frames + here, half)] = own[half:]
    arrange(samples, data)
    for operator, start in ((upper, 0), (lower, upper.shape[2])):
        for lanes, real, imag in beamform(data, operator, start):
            y_ref[pl.ds(there, half), lanes], y_ref[pl.ds(frames + there, half), lanes] = real, imag
    y = y_ref[...]
    products = lax.dot_general(y, y, (((1,), (1,)), ((), ())), preferred_element_type=F32)
    gram[...] = (products[:frames, :frames] + products[frames:, frames:]) + (
        products[:frames, frames:] - products[frames:, :frames]
    )
    keep_ref[...] = gram[pl.ds(here, half), :]
    send_ref[...] = gram[pl.ds(there, half), :]


def halves(x):
    high = x.astype(BF16)
    return high, (x - high.astype(F32)).astype(BF16)


def product(left, right):
    left = left.astype(BF16)
    return jnp.dot(
        jnp.concatenate([left, left], axis=1), jnp.concatenate(halves(right), axis=0), preferred_element_type=F32
    )


def unpack(packed):
    flipped = jnp.transpose(packed)
    return 0.5 * (packed + flipped), 0.5 * (packed - flipped), flipped


def filter_kernel(mine, far, twin, far_twin, y_ref, peer_ref, out_ref, gram, kept):
    core = lax.axis_index("core")
    half, frames = mine.shape
    gram[pl.ds(pl.multiple_of(core * half, half), half), :] = mine[...] + far[...].astype(F32)
    gram[pl.ds(pl.multiple_of((1 - core) * half, half), half), :] = twin[...] + far_twin[...].astype(F32)
    packed = gram[...]
    squares = jnp.sum(packed * packed)
    factor = 4.0 / jnp.sqrt(jnp.full((1, 1), squares + EPSILON, F32))
    real, imag, flipped = unpack(packed)
    left = jnp.concatenate([real, imag], axis=1)
    second = product(left, jnp.concatenate([packed, flipped], axis=0)) * (factor * factor)
    right = jnp.concatenate([second, jnp.transpose(second)], axis=0).astype(BF16)
    third = jnp.dot(left.astype(BF16), right, preferred_element_type=F32) * factor
    rows = lax.broadcasted_iota(jnp.int32, (frames, frames), 0)
    cols = lax.broadcasted_iota(jnp.int32, (frames, frames), 1)
    identity = jnp.where(rows == cols, 1.0, 0.0).astype(F32)
    real, imag, _ = unpack(identity - factor * packed + 0.3 * second - 0.03 * third)
    kept[0] = real.astype(BF16)
    kept[1] = imag.astype(BF16)
    real, imag = (kept[part, pl.ds(pl.multiple_of(core * half, half), half)] for part in range(2))
    matrix = jnp.concatenate(
        [jnp.concatenate([real, imag], axis=1), jnp.concatenate([-imag, real], axis=1)], axis=0
    )
    bins, parts, group, _ = out_ref.shape
    voxels = y_ref.shape[1]
    for source, place in ((y_ref, core), (peer_ref, 1 - core)):
        lanes = pl.ds(pl.multiple_of(place * voxels, voxels), voxels)
        applied = jnp.dot(matrix, source[...], preferred_element_type=F32).astype(BF16)
        for part in range(parts):
            for j in range(bins):
                row = part * half + j * group
                out_ref[j, part, :, lanes] = applied[row : row + group]


def place_kernel(got, out_ref, held, sems):
    bins, parts, group, voxels = got.shape
    size = group * bins
    rows = lax.broadcasted_iota(jnp.int32, (size, size), 0)
    cols = lax.broadcasted_iota(jnp.int32, (size, size), 1)
    turn = jnp.where(cols == (rows % bins) * group + rows // bins, 1.0, 0.0).astype(BF16)
    copies = [
        pltpu.make_async_copy(held.at[part], out_ref.at[:, part], sems.at[part]) for part in range(parts)
    ]
    for part in range(parts):
        moved = jnp.dot(turn, got[:, part].reshape(size, voxels), preferred_element_type=F32).astype(BF16)
        held[part] = moved.reshape(group, bins, voxels)
        copies[part].start()
    for copy in copies:
        copy.wait()


def shards(rf_data, elem_pos, vox_pos, subbands):
    parts, bins, group, width = rf_data.shape
    channels = elem_pos.shape[1]
    chans = channels // width
    voxels = vox_pos.shape[1] // CORES
    frames = group * bins * CORES
    half = frames // CORES

    def shape(*dims, dtype=BF16):
        return jax.ShapeDtypeStruct(dims, dtype)

    def swap(x):
        return lax.ppermute(x, "core", [(0, 1), (1, 0)])

    def across(x, bits):
        return lax.ppermute(x, "chan", [(a, a ^ bits) for a in range(chans)])

    def in_hbm(x):
        return pltpu.with_memory_space_constraint(x, pltpu.HBM)

    by_bin, lhs, rhs, wave = pl.pallas_call(
        spread_kernel,
        name="spread",
        out_shape=(
            shape(chans * bins, parts, group, width),
            shape(channels, 8),
            shape(2, 8, voxels),
            shape(2, voxels, dtype=F32),
        ),
        in_specs=[HBM] * 4,
        out_specs=(HBM, VMEM, VMEM, VMEM),
        scratch_shapes=[
            pltpu.VMEM(rf_data.shape, BF16),
            pltpu.VMEM(elem_pos.shape, jnp.int32),
            pltpu.VMEM(vox_pos.shape, jnp.int32),
            pltpu.SMEM(subbands.shape, jnp.int32),
            pltpu.SemaphoreType.DMA((chans * parts + 4,)),
        ],
        compiler_params=WIDE,
    )(in_hbm(rf_data), in_hbm(elem_pos), in_hbm(vox_pos), in_hbm(subbands))
    own = lax.all_to_all(by_bin, ("chan", "bin"), split_axis=0, concat_axis=0, tiled=True)

    share = voxels // 2
    upper, lower = pl.pallas_call(
        operator_kernel,
        name="operator",
        out_shape=(shape(2, channels, share), pltpu.HBM((2, channels, voxels - share), BF16)),
        in_specs=[VMEM, VMEM, VMEM],
        out_specs=(VMEM, HBM),
        scratch_shapes=[
            pltpu.VMEM((2, channels, voxels - share), BF16),
            pltpu.SemaphoreType.DMA,
        ],
        compiler_params=WIDE,
        cost_estimate=pl.CostEstimate(
            flops=60 * channels * voxels,
            transcendentals=channels * voxels,
            bytes_accessed=4 * channels * voxels,
        ),
    )(lhs, rhs, wave)

    own, upper, lower = lax.optimization_barrier((own, upper, lower))
    other = swap(own)
    own = own.reshape(chans, bins, parts, group, width)
    other = other.reshape(chans, bins, parts, group, width)

    beam_cost = pl.CostEstimate(
        flops=8 * half * channels * voxels * 2, transcendentals=0, bytes_accessed=4 * channels * voxels
    )
    mine, lower = pl.pallas_call(
        own_kernel,
        name="beam_own",
        out_shape=(shape(frames, voxels), shape(2, channels, voxels - share)),
        in_specs=[VMEM, HBM, VMEM],
        out_specs=(VMEM, VMEM),
        scratch_shapes=[
            pltpu.VMEM((frames, channels), BF16),
            pltpu.SemaphoreType.DMA,
        ],
        compiler_params=WIDE,
        cost_estimate=beam_cost,
    )(upper, in_hbm(lower), own)
    y, keep, send = pl.pallas_call(
        other_kernel,
        name="beam_other",
        out_shape=(shape(2 * frames, voxels), shape(half, frames, dtype=F32), shape(half, frames, dtype=F32)),
        in_specs=[VMEM, VMEM, VMEM, VMEM],
        out_specs=(VMEM, VMEM, VMEM),
        scratch_shapes=[pltpu.VMEM((frames, channels), BF16), pltpu.VMEM((frames, frames), F32)],
        compiler_params=WIDE,
        cost_estimate=beam_cost,
    )(upper, lower, other, mine)

    total = keep + swap(send)
    total, y = lax.optimization_barrier((total, y))
    peer = swap(y)
    narrow = total.astype(BF16)
    total = total + sum(across(narrow, bits).astype(F32) for bits in (1, 3, 2))
    narrow = total.astype(BF16)
    far = across(narrow, 4)
    far_twin = lax.ppermute(
        narrow, ("chan", "core"), [(2 * a + c, 2 * (a ^ 4) + 1 - c) for a in range(chans) for c in range(CORES)]
    )
    twin = swap(total)

    applied = pl.pallas_call(
        filter_kernel,
        name="filter",
        out_shape=shape(bins, parts, group, CORES * voxels),
        in_specs=[VMEM] * 6,
        out_specs=VMEM,
        scratch_shapes=[pltpu.VMEM((frames, frames), F32), pltpu.VMEM((2, frames, frames), BF16)],
        compiler_params=WIDE,
    )(total, far, twin, far_twin, y, peer)

    got = lax.all_to_all(applied, "bin", split_axis=0, concat_axis=0, tiled=True)
    return pl.pallas_call(
        place_kernel,
        name="place",
        out_shape=shape(group, parts, bins, CORES * voxels),
        in_specs=[VMEM],
        out_specs=HBM,
        scratch_shapes=[
            pltpu.VMEM((parts, group, bins, CORES * voxels), BF16),
            pltpu.SemaphoreType.DMA((parts,)),
        ],
        compiler_params=WIDE,
    )(got)


def solution(mesh):
    chans = mesh.shape["chan"]
    fine = Mesh(mesh.devices.reshape(chans, BINS, CORES), ("chan", "bin", "core"))
    return jax.shard_map(
        shards,
        mesh=fine,
        in_specs=(P(None, None, ("bin", "core"), "chan"), P(), P(None, "chan"), P()),
        out_specs=P(("bin", "core"), None, None, "chan"),
        check_vma=False,
    )
```

```python
import functools
import math

import jax
import jax.numpy as jnp
from jax import lax
from jax.experimental import pallas as pl
from jax.experimental.pallas import tpu as pltpu
from jax.sharding import Mesh, PartitionSpec as P

EPSILON = 1e-06
BINS = 8
CORES = 2
F32 = jnp.float32
BF16 = jnp.bfloat16
ROOT = math.sqrt(2.0)
SIN = tuple(
    ROOT * c
    for c in (3.1415925800446924, -5.167706878924515, 2.5500313772531213, -0.5980451739748806, 0.0772201286897368)
)
COS = tuple(
    ROOT * c
    for c in (0.9999999534666272, -4.934792858670076, 4.058411914063177, -1.331880160583308, 0.21969679727234584)
)
ROUNDER = 12582912.0
ROWS = 512
LANES = 512
WIDE = pltpu.CompilerParams(vmem_limit_bytes=16 * 1024 * 1024)
VMEM = pl.BlockSpec(memory_space=pltpu.VMEM)
HBM = pl.BlockSpec(memory_space=pltpu.HBM)


def horner(coefficients, z):
    total = coefficients[-1] * z + coefficients[-2]
    for value in coefficients[-3::-1]:
        total = total * z + value
    return total


def digits(value, unit):
    high = jnp.floor(value * (1.0 / unit))
    return high, value - unit * high


def spread_kernel(
    rf_ref, elem_ref, vox_ref, bins_ref, out_ref, lhs_ref, rhs_ref, wave_ref, held, elem, vox, numbers, sems
):
    parts, bins = held.shape[:2]
    chans = out_ref.shape[0] // bins
    reads = [
        pltpu.make_async_copy(source, target, sems.at[n])
        for n, (source, target) in enumerate(
            ((rf_ref, held), (elem_ref, elem), (vox_ref, vox), (bins_ref, numbers))
        )
    ]
    for copy in reads:
        copy.start()
    reads[0].wait()
    copies = [
        pltpu.make_async_copy(
            held.at[part], out_ref.at[k * bins : (k + 1) * bins, part], sems.at[4 + k * parts + part]
        )
        for k in range(chans)
        for part in range(parts)
    ]
    for copy in copies:
        copy.start()
    for copy in reads[1:]:
        copy.wait()

    channels = elem.shape[1]
    place = elem[...].astype(F32)
    high, low = digits(jnp.sum(place * place, axis=0, keepdims=True), 16.0)
    one = jnp.ones((1, channels), F32)
    lhs_ref[...] = jnp.transpose(jnp.concatenate([place, high, low, one, one, 0.0 * one], axis=0)).astype(BF16)
    voxels = wave_ref.shape[1]
    voxel = vox[:, pl.ds(pl.multiple_of(lax.axis_index("core") * voxels, voxels), voxels)].astype(F32)
    high, low = digits(jnp.sum(voxel * voxel, axis=0, keepdims=True), 64.0)
    one = jnp.ones((1, voxels), F32)
    zero = 0.0 * one
    wave_ref[0:1] = voxel[2:3]
    wave_ref[1:2] = one * ((32.0 + numbers[lax.axis_index("bin")].astype(F32)) / 64.0)
    rhs_ref[0] = jnp.concatenate([-2.0 * voxel, 16.0 * one, one, 64.0 * high, low, zero], axis=0).astype(BF16)
    scale = 1.0 / math.sqrt(channels)
    rhs_ref[1] = jnp.concatenate(
        [zero, zero, -scale * one, zero, zero, scale * voxel[2:3], zero, zero], axis=0
    ).astype(BF16)
    for copy in copies:
        copy.wait()


def operator_kernel(lhs_ref, rhs_ref, wave_ref, upper, lower_ref, lower, sem):
    channels = lhs_ref.shape[0]
    share = upper.shape[2]
    voxels = share + lower.shape[2]

    def tile(index, carry, out_ref, lanes):
        rows = pl.ds(pl.multiple_of(index * ROWS, ROWS), ROWS)
        left = lhs_ref[rows]
        squared = jnp.dot(left, rhs_ref[0, :, lanes], preferred_element_type=F32)
        depth = jnp.dot(left, rhs_ref[1, :, lanes], preferred_element_type=F32)
        inverse = lax.rsqrt(squared)
        turns = (wave_ref[0:1, lanes] + squared * inverse) * wave_ref[1:2, lanes]
        part = turns - ((turns + ROUNDER) - ROUNDER)
        z = part * part
        sine = part * horner(SIN, z)
        cosine = horner(COS, z)
        weight = depth * inverse
        lean = weight * sine
        out_ref[0, rows] = (weight - lean * sine).astype(BF16)
        out_ref[1, rows] = (lean * cosine).astype(BF16)
        return carry

    lax.fori_loop(0, channels // ROWS, functools.partial(tile, out_ref=lower, lanes=slice(share, voxels)), 0)
    copy = pltpu.make_async_copy(lower, lower_ref, sem)
    copy.start()
    lax.fori_loop(0, channels // ROWS, functools.partial(tile, out_ref=upper, lanes=slice(0, share)), 0)
    copy.wait()


def arrange(samples, data):
    blocks, bins, _, group, width = samples.shape
    half = bins * group
    for k in range(blocks):
        for part in range(2):
            data[part * half : (part + 1) * half, k * width : (k + 1) * width] = samples[k, :, part].reshape(half, width)


def beamform(data, operator, start):
    half = data.shape[0] // 2
    for n in range(0, operator.shape[2], LANES):
        first, second = (
            jnp.dot(data[...], operator[which, :, n : n + LANES], preferred_element_type=F32) for which in range(2)
        )
        real = (first[:half] + second[half:]).astype(BF16)
        imag = (first[half:] - second[:half]).astype(BF16)
        yield slice(start + n, start + n + LANES), real, imag


def own_kernel(upper, lower_ref, samples, out_ref, lower, data, sem):
    copy = pltpu.make_async_copy(lower_ref, lower, sem)
    copy.start()
    arrange(samples, data)
    half = out_ref.shape[0] // 2
    for lanes, real, imag in beamform(data, upper, 0):
        out_ref[:half, lanes], out_ref[half:, lanes] = real, imag
    copy.wait()
    for lanes, real, imag in beamform(data, lower, upper.shape[2]):
        out_ref[:half, lanes], out_ref[half:, lanes] = real, imag


def other_kernel(upper, lower, samples, own, y_ref, keep_ref, send_ref, data, gram):
    core = lax.axis_index("core")
    frames = y_ref.shape[0] // 2
    half = frames // CORES
    here = pl.multiple_of(core * half, half)
    there = pl.multiple_of((1 - core) * half, half)
    y_ref[pl.ds(here, half)] = own[:half]
    y_ref[pl.ds(frames + here, half)] = own[half:]
    arrange(samples, data)
    for operator, start in ((upper, 0), (lower, upper.shape[2])):
        for lanes, real, imag in beamform(data, operator, start):
            y_ref[pl.ds(there, half), lanes], y_ref[pl.ds(frames + there, half), lanes] = real, imag
    y = y_ref[...]
    products = lax.dot_general(y, y, (((1,), (1,)), ((), ())), preferred_element_type=F32)
    gram[...] = (products[:frames, :frames] + products[frames:, frames:]) + (
        products[:frames, frames:] - products[frames:, :frames]
    )
    keep_ref[...] = gram[pl.ds(here, half), :]
    send_ref[...] = gram[pl.ds(there, half), :]


def halves(x):
    high = x.astype(BF16)
    return high, (x - high.astype(F32)).astype(BF16)


def product(left, right):
    left = left.astype(BF16)
    return jnp.dot(
        jnp.concatenate([left, left], axis=1), jnp.concatenate(halves(right), axis=0), preferred_element_type=F32
    )


def unpack(packed):
    flipped = jnp.transpose(packed)
    return 0.5 * (packed + flipped), 0.5 * (packed - flipped), flipped


def filter_kernel(mine, far, twin, far_twin, y_ref, peer_ref, out_ref, gram, kept):
    core = lax.axis_index("core")
    half, frames = mine.shape
    gram[pl.ds(pl.multiple_of(core * half, half), half), :] = mine[...] + far[...].astype(F32)
    gram[pl.ds(pl.multiple_of((1 - core) * half, half), half), :] = twin[...] + far_twin[...].astype(F32)
    packed = gram[...]
    squares = jnp.sum(packed * packed)
    factor = 4.0 / jnp.sqrt(jnp.full((1, 1), squares + EPSILON, F32))
    real, imag, flipped = unpack(packed)
    left = jnp.concatenate([real, imag], axis=1)
    second = product(left, jnp.concatenate([packed, flipped], axis=0)) * (factor * factor)
    right = jnp.concatenate([second, jnp.transpose(second)], axis=0).astype(BF16)
    third = jnp.dot(left.astype(BF16), right, preferred_element_type=F32) * factor
    rows = lax.broadcasted_iota(jnp.int32, (frames, frames), 0)
    cols = lax.broadcasted_iota(jnp.int32, (frames, frames), 1)
    identity = jnp.where(rows == cols, 1.0, 0.0).astype(F32)
    real, imag, _ = unpack(identity - factor * packed + 0.3 * second - 0.03 * third)
    kept[0] = real.astype(BF16)
    kept[1] = imag.astype(BF16)
    real, imag = (kept[part, pl.ds(pl.multiple_of(core * half, half), half)] for part in range(2))
    matrix = jnp.concatenate(
        [jnp.concatenate([real, imag], axis=1), jnp.concatenate([-imag, real], axis=1)], axis=0
    )
    bins, parts, group, _ = out_ref.shape
    voxels = y_ref.shape[1]
    for source, place in ((y_ref, core), (peer_ref, 1 - core)):
        lanes = pl.ds(pl.multiple_of(place * voxels, voxels), voxels)
        applied = jnp.dot(matrix, source[...], preferred_element_type=F32).astype(BF16)
        for part in range(parts):
            for j in range(bins):
                row = part * half + j * group
                out_ref[j, part, :, lanes] = applied[row : row + group]


def place_kernel(got, out_ref, held, sems):
    bins, parts, group, voxels = got.shape
    size = group * bins
    rows = lax.broadcasted_iota(jnp.int32, (size, size), 0)
    cols = lax.broadcasted_iota(jnp.int32, (size, size), 1)
    turn = jnp.where(cols == (rows % bins) * group + rows // bins, 1.0, 0.0).astype(BF16)
    copies = [
        pltpu.make_async_copy(held.at[part], out_ref.at[:, part], sems.at[part]) for part in range(parts)
    ]
    for part in range(parts):
        moved = jnp.dot(turn, got[:, part].reshape(size, voxels), preferred_element_type=F32).astype(BF16)
        held[part] = moved.reshape(group, bins, voxels)
        copies[part].start()
    for copy in copies:
        copy.wait()


def shards(rf_data, elem_pos, vox_pos, subbands):
    parts, bins, group, width = rf_data.shape
    channels = elem_pos.shape[1]
    chans = channels // width
    voxels = vox_pos.shape[1] // CORES
    frames = group * bins * CORES
    half = frames // CORES

    def shape(*dims, dtype=BF16):
        return jax.ShapeDtypeStruct(dims, dtype)

    def swap(x):
        return lax.ppermute(x, "core", [(0, 1), (1, 0)])

    def across(x, bits):
        return lax.ppermute(x, "chan", [(a, a ^ bits) for a in range(chans)])

    def in_hbm(x):
        return pltpu.with_memory_space_constraint(x, pltpu.HBM)

    by_bin, lhs, rhs, wave = pl.pallas_call(
        spread_kernel,
        name="spread",
        out_shape=(
            shape(chans * bins, parts, group, width),
            shape(channels, 8),
            shape(2, 8, voxels),
            shape(2, voxels, dtype=F32),
        ),
        in_specs=[HBM] * 4,
        out_specs=(HBM, VMEM, VMEM, VMEM),
        scratch_shapes=[
            pltpu.VMEM(rf_data.shape, BF16),
            pltpu.VMEM(elem_pos.shape, jnp.int32),
            pltpu.VMEM(vox_pos.shape, jnp.int32),
            pltpu.SMEM(subbands.shape, jnp.int32),
            pltpu.SemaphoreType.DMA((chans * parts + 4,)),
        ],
        compiler_params=WIDE,
    )(in_hbm(rf_data), in_hbm(elem_pos), in_hbm(vox_pos), in_hbm(subbands))
    own = lax.all_to_all(by_bin, ("chan", "bin"), split_axis=0, concat_axis=0, tiled=True)

    share = voxels // 2
    upper, lower = pl.pallas_call(
        operator_kernel,
        name="operator",
        out_shape=(shape(2, channels, share), pltpu.HBM((2, channels, voxels - share), BF16)),
        in_specs=[VMEM, VMEM, VMEM],
        out_specs=(VMEM, HBM),
        scratch_shapes=[
            pltpu.VMEM((2, channels, voxels - share), BF16),
            pltpu.SemaphoreType.DMA,
        ],
        compiler_params=WIDE,
        cost_estimate=pl.CostEstimate(
            flops=60 * channels * voxels,
            transcendentals=channels * voxels,
            bytes_accessed=4 * channels * voxels,
        ),
    )(lhs, rhs, wave)

    own, upper, lower = lax.optimization_barrier((own, upper, lower))
    other = swap(own)
    own = own.reshape(chans, bins, parts, group, width)
    other = other.reshape(chans, bins, parts, group, width)

    beam_cost = pl.CostEstimate(
        flops=8 * half * channels * voxels * 2, transcendentals=0, bytes_accessed=4 * channels * voxels
    )
    mine, lower = pl.pallas_call(
        own_kernel,
        name="beam_own",
        out_shape=(shape(frames, voxels), shape(2, channels, voxels - share)),
        in_specs=[VMEM, HBM, VMEM],
        out_specs=(VMEM, VMEM),
        scratch_shapes=[
            pltpu.VMEM((frames, channels), BF16),
            pltpu.SemaphoreType.DMA,
        ],
        compiler_params=WIDE,
        cost_estimate=beam_cost,
    )(upper, in_hbm(lower), own)
    y, keep, send = pl.pallas_call(
        other_kernel,
        name="beam_other",
        out_shape=(shape(2 * frames, voxels), shape(half, frames, dtype=F32), shape(half, frames, dtype=F32)),
        in_specs=[VMEM, VMEM, VMEM, VMEM],
        out_specs=(VMEM, VMEM, VMEM),
        scratch_shapes=[pltpu.VMEM((frames, channels), BF16), pltpu.VMEM((frames, frames), F32)],
        compiler_params=WIDE,
        cost_estimate=beam_cost,
    )(upper, lower, other, mine)

    total = keep + swap(send)
    total, y = lax.optimization_barrier((total, y))
    peer = swap(y)
    narrow = total.astype(BF16)
    total = total + sum(across(narrow, bits).astype(F32) for bits in (1, 3, 2))
    narrow = total.astype(BF16)
    far = across(narrow, 4)
    far_twin = lax.ppermute(
        narrow, ("chan", "core"), [(2 * a + c, 2 * (a ^ 4) + 1 - c) for a in range(chans) for c in range(CORES)]
    )
    twin = swap(total)

    applied = pl.pallas_call(
        filter_kernel,
        name="filter",
        out_shape=shape(bins, parts, group, CORES * voxels),
        in_specs=[VMEM] * 6,
        out_specs=VMEM,
        scratch_shapes=[pltpu.VMEM((frames, frames), F32), pltpu.VMEM((2, frames, frames), BF16)],
        compiler_params=WIDE,
    )(total, far, twin, far_twin, y, peer)

    got = lax.all_to_all(applied, "bin", split_axis=0, concat_axis=0, tiled=True)
    return pl.pallas_call(
        place_kernel,
        name="place",
        out_shape=shape(group, parts, bins, CORES * voxels),
        in_specs=[VMEM],
        out_specs=HBM,
        scratch_shapes=[
            pltpu.VMEM((parts, group, bins, CORES * voxels), BF16),
            pltpu.SemaphoreType.DMA((parts,)),
        ],
        compiler_params=WIDE,
    )(got)


def solution(mesh):
    chans = mesh.shape["chan"]
    fine = Mesh(mesh.devices.reshape(chans, BINS, CORES), ("chan", "bin", "core"))
    return jax.shard_map(
        shards,
        mesh=fine,
        in_specs=(P(None, None, ("bin", "core"), "chan"), P(), P(None, "chan"), P()),
        out_specs=P(("bin", "core"), None, None, "chan"),
        check_vma=False,
    )
```

```python
import functools
import math

import jax
import jax.numpy as jnp
from jax import lax
from jax.experimental import pallas as pl
from jax.experimental.pallas import tpu as pltpu
from jax.sharding import Mesh, PartitionSpec as P

EPSILON = 1e-06
BINS = 8
CORES = 2
F32 = jnp.float32
BF16 = jnp.bfloat16
ROOT = math.sqrt(2.0)
SIN = tuple(
    ROOT * c
    for c in (3.1415925800446924, -5.167706878924515, 2.5500313772531213, -0.5980451739748806, 0.0772201286897368)
)
COS = tuple(
    ROOT * c
    for c in (0.9999999534666272, -4.934792858670076, 4.058411914063177, -1.331880160583308, 0.21969679727234584)
)
ROUNDER = 12582912.0
ROWS = 512
LANES = 256
WIDE = pltpu.CompilerParams(vmem_limit_bytes=16 * 1024 * 1024)
VMEM = pl.BlockSpec(memory_space=pltpu.VMEM)
HBM = pl.BlockSpec(memory_space=pltpu.HBM)


def horner(coefficients, z):
    total = coefficients[-1] * z + coefficients[-2]
    for value in coefficients[-3::-1]:
        total = total * z + value
    return total


def digits(value, unit):
    high = jnp.floor(value * (1.0 / unit))
    return high, value - unit * high


def spread_kernel(
    rf_ref, elem_ref, vox_ref, bins_ref, out_ref, lhs_ref, rhs_ref, wave_ref, held, elem, vox, numbers, sems
):
    parts, bins = held.shape[:2]
    chans = out_ref.shape[0] // bins
    reads = [
        pltpu.make_async_copy(source, target, sems.at[n])
        for n, (source, target) in enumerate(
            ((rf_ref, held), (elem_ref, elem), (vox_ref, vox), (bins_ref, numbers))
        )
    ]
    for copy in reads:
        copy.start()
    reads[0].wait()
    copies = [
        pltpu.make_async_copy(
            held.at[part], out_ref.at[k * bins : (k + 1) * bins, part], sems.at[4 + k * parts + part]
        )
        for k in range(chans)
        for part in range(parts)
    ]
    for copy in copies:
        copy.start()
    for copy in reads[1:]:
        copy.wait()

    channels = elem.shape[1]
    place = elem[...].astype(F32)
    high, low = digits(jnp.sum(place * place, axis=0, keepdims=True), 16.0)
    one = jnp.ones((1, channels), F32)
    lhs_ref[...] = jnp.transpose(jnp.concatenate([place, high, low, one, one, 0.0 * one], axis=0)).astype(BF16)
    voxels = wave_ref.shape[1]
    voxel = vox[:, pl.ds(pl.multiple_of(lax.axis_index("core") * voxels, voxels), voxels)].astype(F32)
    high, low = digits(jnp.sum(voxel * voxel, axis=0, keepdims=True), 64.0)
    one = jnp.ones((1, voxels), F32)
    zero = 0.0 * one
    wave_ref[0:1] = voxel[2:3]
    wave_ref[1:2] = one * ((32.0 + numbers[lax.axis_index("bin")].astype(F32)) / 64.0)
    rhs_ref[0] = jnp.concatenate([-2.0 * voxel, 16.0 * one, one, 64.0 * high, low, zero], axis=0).astype(BF16)
    scale = 1.0 / math.sqrt(channels)
    rhs_ref[1] = jnp.concatenate(
        [zero, zero, -scale * one, zero, zero, scale * voxel[2:3], zero, zero], axis=0
    ).astype(BF16)
    for copy in copies:
        copy.wait()


def operator_kernel(lhs_ref, rhs_ref, wave_ref, upper, lower_ref, lower, sem):
    channels = lhs_ref.shape[0]
    share = upper.shape[2]
    voxels = share + lower.shape[2]

    def tile(index, carry, out_ref, lanes):
        rows = pl.ds(pl.multiple_of(index * ROWS, ROWS), ROWS)
        left = lhs_ref[rows]
        squared = jnp.dot(left, rhs_ref[0, :, lanes], preferred_element_type=F32)
        depth = jnp.dot(left, rhs_ref[1, :, lanes], preferred_element_type=F32)
        inverse = lax.rsqrt(squared)
        turns = (wave_ref[0:1, lanes] + squared * inverse) * wave_ref[1:2, lanes]
        part = turns - ((turns + ROUNDER) - ROUNDER)
        z = part * part
        sine = part * horner(SIN, z)
        cosine = horner(COS, z)
        weight = depth * inverse
        lean = weight * sine
        out_ref[0, rows] = (weight - lean * sine).astype(BF16)
        out_ref[1, rows] = (lean * cosine).astype(BF16)
        return carry

    lax.fori_loop(0, channels // ROWS, functools.partial(tile, out_ref=lower, lanes=slice(share, voxels)), 0)
    copy = pltpu.make_async_copy(lower, lower_ref, sem)
    copy.start()
    lax.fori_loop(0, channels // ROWS, functools.partial(tile, out_ref=upper, lanes=slice(0, share)), 0)
    copy.wait()


def arrange(samples, data):
    blocks, bins, _, group, width = samples.shape
    half = bins * group
    for k in range(blocks):
        for part in range(2):
            data[part * half : (part + 1) * half, k * width : (k + 1) * width] = samples[k, :, part].reshape(half, width)


def beamform(data, operator, start):
    half = data.shape[0] // 2
    for n in range(0, operator.shape[2], LANES):
        first, second = (
            jnp.dot(data[...], operator[which, :, n : n + LANES], preferred_element_type=F32) for which in range(2)
        )
        real = (first[:half] + second[half:]).astype(BF16)
        imag = (first[half:] - second[:half]).astype(BF16)
        yield slice(start + n, start + n + LANES), real, imag


def own_kernel(upper, lower_ref, samples, out_ref, lower, data, sem):
    copy = pltpu.make_async_copy(lower_ref, lower, sem)
    copy.start()
    arrange(samples, data)
    half = out_ref.shape[0] // 2
    for lanes, real, imag in beamform(data, upper, 0):
        out_ref[:half, lanes], out_ref[half:, lanes] = real, imag
    copy.wait()
    for lanes, real, imag in beamform(data, lower, upper.shape[2]):
        out_ref[:half, lanes], out_ref[half:, lanes] = real, imag


def other_kernel(upper, lower, samples, own, y_ref, keep_ref, send_ref, data, gram):
    core = lax.axis_index("core")
    frames = y_ref.shape[0] // 2
    half = frames // CORES
    here = pl.multiple_of(core * half, half)
    there = pl.multiple_of((1 - core) * half, half)
    y_ref[pl.ds(here, half)] = own[:half]
    y_ref[pl.ds(frames + here, half)] = own[half:]
    arrange(samples, data)
    for operator, start in ((upper, 0), (lower, upper.shape[2])):
        for lanes, real, imag in beamform(data, operator, start):
            y_ref[pl.ds(there, half), lanes], y_ref[pl.ds(frames + there, half), lanes] = real, imag
    y = y_ref[...]
    products = lax.dot_general(y, y, (((1,), (1,)), ((), ())), preferred_element_type=F32)
    gram[...] = (products[:frames, :frames] + products[frames:, frames:]) + (
        products[:frames, frames:] - products[frames:, :frames]
    )
    keep_ref[...] = gram[pl.ds(here, half), :]
    send_ref[...] = gram[pl.ds(there, half), :].astype(BF16)


def halves(x):
    high = x.astype(BF16)
    return high, (x - high.astype(F32)).astype(BF16)


def product(left, right):
    left = left.astype(BF16)
    return jnp.dot(
        jnp.concatenate([left, left], axis=1), jnp.concatenate(halves(right), axis=0), preferred_element_type=F32
    )


def unpack(packed):
    flipped = jnp.transpose(packed)
    return 0.5 * (packed + flipped), 0.5 * (packed - flipped), flipped


def filter_kernel(mine, far, twin, far_twin, y_ref, peer_ref, out_ref, gram, kept):
    core = lax.axis_index("core")
    half, frames = mine.shape
    gram[pl.ds(pl.multiple_of(core * half, half), half), :] = mine[...] + far[...].astype(F32)
    gram[pl.ds(pl.multiple_of((1 - core) * half, half), half), :] = twin[...] + far_twin[...].astype(F32)
    packed = gram[...]
    squares = jnp.sum(packed * packed)
    factor = 4.0 / jnp.sqrt(jnp.full((1, 1), squares + EPSILON, F32))
    real, imag, flipped = unpack(packed)
    left = jnp.concatenate([real, imag], axis=1)
    second = product(left, jnp.concatenate([packed, flipped], axis=0)) * (factor * factor)
    right = jnp.concatenate([second, jnp.transpose(second)], axis=0).astype(BF16)
    third = jnp.dot(left.astype(BF16), right, preferred_element_type=F32) * factor
    rows = lax.broadcasted_iota(jnp.int32, (frames, frames), 0)
    cols = lax.broadcasted_iota(jnp.int32, (frames, frames), 1)
    identity = jnp.where(rows == cols, 1.0, 0.0).astype(F32)
    real, imag, _ = unpack(identity - factor * packed + 0.3 * second - 0.03 * third)
    kept[0] = real.astype(BF16)
    kept[1] = imag.astype(BF16)
    real, imag = (kept[part, pl.ds(pl.multiple_of(core * half, half), half)] for part in range(2))
    matrix = jnp.concatenate(
        [jnp.concatenate([real, imag], axis=1), jnp.concatenate([-imag, real], axis=1)], axis=0
    )
    bins, parts, group, _ = out_ref.shape
    voxels = y_ref.shape[1]
    for source, place in ((y_ref, core), (peer_ref, 1 - core)):
        lanes = pl.ds(pl.multiple_of(place * voxels, voxels), voxels)
        applied = jnp.dot(matrix, source[...], preferred_element_type=F32).astype(BF16)
        for part in range(parts):
            for j in range(bins):
                row = part * half + j * group
                out_ref[j, part, :, lanes] = applied[row : row + group]


def place_kernel(got, out_ref, held, sems):
    bins, parts, group, voxels = got.shape
    size = group * bins
    rows = lax.broadcasted_iota(jnp.int32, (size, size), 0)
    cols = lax.broadcasted_iota(jnp.int32, (size, size), 1)
    turn = jnp.where(cols == (rows % bins) * group + rows // bins, 1.0, 0.0).astype(BF16)
    copies = [
        pltpu.make_async_copy(held.at[part], out_ref.at[:, part], sems.at[part]) for part in range(parts)
    ]
    for part in range(parts):
        moved = jnp.dot(turn, got[:, part].reshape(size, voxels), preferred_element_type=F32).astype(BF16)
        held[part] = moved.reshape(group, bins, voxels)
        copies[part].start()
    for copy in copies:
        copy.wait()


def shards(rf_data, elem_pos, vox_pos, subbands):
    parts, bins, group, width = rf_data.shape
    channels = elem_pos.shape[1]
    chans = channels // width
    voxels = vox_pos.shape[1] // CORES
    frames = group * bins * CORES
    half = frames // CORES

    def shape(*dims, dtype=BF16):
        return jax.ShapeDtypeStruct(dims, dtype)

    def swap(x):
        return lax.ppermute(x, "core", [(0, 1), (1, 0)])

    def across(x, bits):
        return lax.ppermute(x, "chan", [(a, a ^ bits) for a in range(chans)])

    def in_hbm(x):
        return pltpu.with_memory_space_constraint(x, pltpu.HBM)

    by_bin, lhs, rhs, wave = pl.pallas_call(
        spread_kernel,
        name="spread",
        out_shape=(
            shape(chans * bins, parts, group, width),
            shape(channels, 8),
            shape(2, 8, voxels),
            shape(2, voxels, dtype=F32),
        ),
        in_specs=[HBM] * 4,
        out_specs=(HBM, VMEM, VMEM, VMEM),
        scratch_shapes=[
            pltpu.VMEM(rf_data.shape, BF16),
            pltpu.VMEM(elem_pos.shape, jnp.int32),
            pltpu.VMEM(vox_pos.shape, jnp.int32),
            pltpu.SMEM(subbands.shape, jnp.int32),
            pltpu.SemaphoreType.DMA((chans * parts + 4,)),
        ],
        compiler_params=WIDE,
    )(in_hbm(rf_data), in_hbm(elem_pos), in_hbm(vox_pos), in_hbm(subbands))
    own = lax.all_to_all(by_bin, ("chan", "bin"), split_axis=0, concat_axis=0, tiled=True)

    share = voxels // 2
    upper, lower = pl.pallas_call(
        operator_kernel,
        name="operator",
        out_shape=(shape(2, channels, share), pltpu.HBM((2, channels, voxels - share), BF16)),
        in_specs=[VMEM, VMEM, VMEM],
        out_specs=(VMEM, HBM),
        scratch_shapes=[
            pltpu.VMEM((2, channels, voxels - share), BF16),
            pltpu.SemaphoreType.DMA,
        ],
        compiler_params=WIDE,
        cost_estimate=pl.CostEstimate(
            flops=60 * channels * voxels,
            transcendentals=channels * voxels,
            bytes_accessed=4 * channels * voxels,
        ),
    )(lhs, rhs, wave)

    own, upper, lower = lax.optimization_barrier((own, upper, lower))
    other = swap(own)
    own = own.reshape(chans, bins, parts, group, width)
    other = other.reshape(chans, bins, parts, group, width)

    beam_cost = pl.CostEstimate(
        flops=8 * half * channels * voxels * 2, transcendentals=0, bytes_accessed=4 * channels * voxels
    )
    mine, lower = pl.pallas_call(
        own_kernel,
        name="beam_own",
        out_shape=(shape(frames, voxels), shape(2, channels, voxels - share)),
        in_specs=[VMEM, HBM, VMEM],
        out_specs=(VMEM, VMEM),
        scratch_shapes=[
            pltpu.VMEM((frames, channels), BF16),
            pltpu.SemaphoreType.DMA,
        ],
        compiler_params=WIDE,
        cost_estimate=beam_cost,
    )(upper, in_hbm(lower), own)
    y, keep, send = pl.pallas_call(
        other_kernel,
        name="beam_other",
        out_shape=(shape(2 * frames, voxels), shape(half, frames, dtype=F32), shape(half, frames)),
        in_specs=[VMEM, VMEM, VMEM, VMEM],
        out_specs=(VMEM, VMEM, VMEM),
        scratch_shapes=[pltpu.VMEM((frames, channels), BF16), pltpu.VMEM((frames, frames), F32)],
        compiler_params=WIDE,
        cost_estimate=beam_cost,
    )(upper, lower, other, mine)

    total = keep + swap(send).astype(F32)
    total, y = lax.optimization_barrier((total, y))
    peer = swap(y)
    narrow = total.astype(BF16)
    total = total + sum(across(narrow, bits).astype(F32) for bits in (1, 3, 2))
    narrow = total.astype(BF16)
    far = across(narrow, 4)
    far_twin = lax.ppermute(
        narrow, ("chan", "core"), [(2 * a + c, 2 * (a ^ 4) + 1 - c) for a in range(chans) for c in range(CORES)]
    )
    twin = swap(total)

    applied = pl.pallas_call(
        filter_kernel,
        name="filter",
        out_shape=shape(bins, parts, group, CORES * voxels),
        in_specs=[VMEM] * 6,
        out_specs=VMEM,
        scratch_shapes=[pltpu.VMEM((frames, frames), F32), pltpu.VMEM((2, frames, frames), BF16)],
        compiler_params=WIDE,
    )(total, far, twin, far_twin, y, peer)

    got = lax.all_to_all(applied, "bin", split_axis=0, concat_axis=0, tiled=True)
    return pl.pallas_call(
        place_kernel,
        name="place",
        out_shape=shape(group, parts, bins, CORES * voxels),
        in_specs=[VMEM],
        out_specs=HBM,
        scratch_shapes=[
            pltpu.VMEM((parts, group, bins, CORES * voxels), BF16),
            pltpu.SemaphoreType.DMA((parts,)),
        ],
        compiler_params=WIDE,
    )(got)


def solution(mesh):
    chans = mesh.shape["chan"]
    fine = Mesh(mesh.devices.reshape(chans, BINS, CORES), ("chan", "bin", "core"))
    return jax.shard_map(
        shards,
        mesh=fine,
        in_specs=(P(None, None, ("bin", "core"), "chan"), P(), P(None, "chan"), P()),
        out_specs=P(("bin", "core"), None, None, "chan"),
        check_vma=False,
    )
```

```python
import functools
import math

import jax
import jax.numpy as jnp
from jax import lax
from jax.experimental import pallas as pl
from jax.experimental.pallas import tpu as pltpu
from jax.sharding import Mesh, PartitionSpec as P

EPSILON = 1e-06
BINS = 8
CORES = 2
F32 = jnp.float32
BF16 = jnp.bfloat16
ROOT = math.sqrt(2.0)
SIN = tuple(
    ROOT * c
    for c in (3.1415925800446924, -5.167706878924515, 2.5500313772531213, -0.5980451739748806, 0.0772201286897368)
)
COS = tuple(
    ROOT * c
    for c in (0.9999999534666272, -4.934792858670076, 4.058411914063177, -1.331880160583308, 0.21969679727234584)
)
ROUNDER = 12582912.0
ROWS = 512
LANES = 256
WIDE = pltpu.CompilerParams(vmem_limit_bytes=16 * 1024 * 1024)
VMEM = pl.BlockSpec(memory_space=pltpu.VMEM)
HBM = pl.BlockSpec(memory_space=pltpu.HBM)


def horner(coefficients, z):
    total = coefficients[-1] * z + coefficients[-2]
    for value in coefficients[-3::-1]:
        total = total * z + value
    return total


def digits(value, unit):
    high = jnp.floor(value * (1.0 / unit))
    return high, value - unit * high


def spread_kernel(
    rf_ref, elem_ref, vox_ref, bins_ref, out_ref, lhs_ref, rhs_ref, wave_ref, held, block, elem, vox, numbers, sems
):
    parts, bins = held.shape[:2]
    chans = out_ref.shape[0] // bins
    reads = [
        pltpu.make_async_copy(source, target, sems.at[n])
        for n, (source, target) in enumerate(
            ((rf_ref, held), (elem_ref, elem), (vox_ref, vox), (bins_ref, numbers))
        )
    ]
    for copy in reads:
        copy.start()
    reads[0].wait()
    for part in range(parts):
        block[:, part] = held[part]
    copies = [
        pltpu.make_async_copy(block, out_ref.at[k * bins : (k + 1) * bins], sems.at[4 + k]) for k in range(chans)
    ]
    for copy in copies:
        copy.start()
    for copy in reads[1:]:
        copy.wait()

    channels = elem.shape[1]
    place = elem[...].astype(F32)
    high, low = digits(jnp.sum(place * place, axis=0, keepdims=True), 16.0)
    one = jnp.ones((1, channels), F32)
    lhs_ref[...] = jnp.transpose(jnp.concatenate([place, high, low, one, one, 0.0 * one], axis=0)).astype(BF16)
    voxels = wave_ref.shape[1]
    voxel = vox[:, pl.ds(pl.multiple_of(lax.axis_index("core") * voxels, voxels), voxels)].astype(F32)
    high, low = digits(jnp.sum(voxel * voxel, axis=0, keepdims=True), 64.0)
    one = jnp.ones((1, voxels), F32)
    zero = 0.0 * one
    wave_ref[0:1] = voxel[2:3]
    wave_ref[1:2] = one * ((32.0 + numbers[lax.axis_index("bin")].astype(F32)) / 64.0)
    rhs_ref[0] = jnp.concatenate([-2.0 * voxel, 16.0 * one, one, 64.0 * high, low, zero], axis=0).astype(BF16)
    scale = 1.0 / math.sqrt(channels)
    rhs_ref[1] = jnp.concatenate(
        [zero, zero, -scale * one, zero, zero, scale * voxel[2:3], zero, zero], axis=0
    ).astype(BF16)
    for copy in copies:
        copy.wait()


def operator_kernel(lhs_ref, rhs_ref, wave_ref, upper, lower_ref, lower, sem):
    channels = lhs_ref.shape[0]
    share = upper.shape[2]
    voxels = share + lower.shape[2]

    def tile(index, carry, out_ref, lanes):
        rows = pl.ds(pl.multiple_of(index * ROWS, ROWS), ROWS)
        left = lhs_ref[rows]
        squared = jnp.dot(left, rhs_ref[0, :, lanes], preferred_element_type=F32)
        depth = jnp.dot(left, rhs_ref[1, :, lanes], preferred_element_type=F32)
        inverse = lax.rsqrt(squared)
        turns = (wave_ref[0:1, lanes] + squared * inverse) * wave_ref[1:2, lanes]
        part = turns - ((turns + ROUNDER) - ROUNDER)
        z = part * part
        sine = part * horner(SIN, z)
        cosine = horner(COS, z)
        weight = depth * inverse
        lean = weight * sine
        out_ref[0, rows] = (weight - lean * sine).astype(BF16)
        out_ref[1, rows] = (lean * cosine).astype(BF16)
        return carry

    lax.fori_loop(0, channels // ROWS, functools.partial(tile, out_ref=lower, lanes=slice(share, voxels)), 0)
    copy = pltpu.make_async_copy(lower, lower_ref, sem)
    copy.start()
    lax.fori_loop(0, channels // ROWS, functools.partial(tile, out_ref=upper, lanes=slice(0, share)), 0)
    copy.wait()


def arrange(samples, data):
    blocks, bins, _, group, width = samples.shape
    half = bins * group
    for k in range(blocks):
        for part in range(2):
            data[part * half : (part + 1) * half, k * width : (k + 1) * width] = samples[k, :, part].reshape(half, width)


def beamform(data, operator, start):
    half = data.shape[0] // 2
    for n in range(0, operator.shape[2], LANES):
        first, second = (
            jnp.dot(data[...], operator[which, :, n : n + LANES], preferred_element_type=F32) for which in range(2)
        )
        real = (first[:half] + second[half:]).astype(BF16)
        imag = (first[half:] - second[:half]).astype(BF16)
        yield slice(start + n, start + n + LANES), real, imag


def own_kernel(upper, lower_ref, samples, out_ref, lower, data, sem):
    copy = pltpu.make_async_copy(lower_ref, lower, sem)
    copy.start()
    arrange(samples, data)
    half = out_ref.shape[0] // 2
    for lanes, real, imag in beamform(data, upper, 0):
        out_ref[:half, lanes], out_ref[half:, lanes] = real, imag
    copy.wait()
    for lanes, real, imag in beamform(data, lower, upper.shape[2]):
        out_ref[:half, lanes], out_ref[half:, lanes] = real, imag


def other_kernel(upper, lower, samples, own, y_ref, keep_ref, send_ref, data, gram):
    core = lax.axis_index("core")
    frames = y_ref.shape[0] // 2
    half = frames // CORES
    here = pl.multiple_of(core * half, half)
    there = pl.multiple_of((1 - core) * half, half)
    y_ref[pl.ds(here, half)] = own[:half]
    y_ref[pl.ds(frames + here, half)] = own[half:]
    arrange(samples, data)
    for operator, start in ((upper, 0), (lower, upper.shape[2])):
        for lanes, real, imag in beamform(data, operator, start):
            y_ref[pl.ds(there, half), lanes], y_ref[pl.ds(frames + there, half), lanes] = real, imag
    y = y_ref[...]
    products = lax.dot_general(y, y, (((1,), (1,)), ((), ())), preferred_element_type=F32)
    gram[...] = (products[:frames, :frames] + products[frames:, frames:]) + (
        products[:frames, frames:] - products[frames:, :frames]
    )
    keep_ref[...] = gram[pl.ds(here, half), :]
    send_ref[...] = gram[pl.ds(there, half), :]


def halves(x):
    high = x.astype(BF16)
    return high, (x - high.astype(F32)).astype(BF16)


def product(left, right):
    left = left.astype(BF16)
    return jnp.dot(
        jnp.concatenate([left, left], axis=1), jnp.concatenate(halves(right), axis=0), preferred_element_type=F32
    )


def unpack(packed):
    flipped = jnp.transpose(packed)
    return 0.5 * (packed + flipped), 0.5 * (packed - flipped), flipped


def filter_kernel(mine, far, twin, far_twin, y_ref, peer_ref, out_ref, gram, kept):
    core = lax.axis_index("core")
    half, frames = mine.shape
    gram[pl.ds(pl.multiple_of(core * half, half), half), :] = mine[...] + far[...].astype(F32)
    gram[pl.ds(pl.multiple_of((1 - core) * half, half), half), :] = twin[...] + far_twin[...].astype(F32)
    packed = gram[...]
    squares = jnp.sum(packed * packed)
    factor = 4.0 / jnp.sqrt(jnp.full((1, 1), squares + EPSILON, F32))
    real, imag, flipped = unpack(packed)
    left = jnp.concatenate([real, imag], axis=1)
    second = product(left, jnp.concatenate([packed, flipped], axis=0)) * (factor * factor)
    right = jnp.concatenate([second, jnp.transpose(second)], axis=0).astype(BF16)
    third = jnp.dot(left.astype(BF16), right, preferred_element_type=F32) * factor
    rows = lax.broadcasted_iota(jnp.int32, (frames, frames), 0)
    cols = lax.broadcasted_iota(jnp.int32, (frames, frames), 1)
    identity = jnp.where(rows == cols, 1.0, 0.0).astype(F32)
    real, imag, _ = unpack(identity - factor * packed + 0.3 * second - 0.03 * third)
    kept[0] = real.astype(BF16)
    kept[1] = imag.astype(BF16)
    real, imag = (kept[part, pl.ds(pl.multiple_of(core * half, half), half)] for part in range(2))
    matrix = jnp.concatenate(
        [jnp.concatenate([real, imag], axis=1), jnp.concatenate([-imag, real], axis=1)], axis=0
    )
    bins, parts, group, _ = out_ref.shape
    voxels = y_ref.shape[1]
    for source, place in ((y_ref, core), (peer_ref, 1 - core)):
        lanes = pl.ds(pl.multiple_of(place * voxels, voxels), voxels)
        applied = jnp.dot(matrix, source[...], preferred_element_type=F32).astype(BF16)
        for part in range(parts):
            for j in range(bins):
                row = part * half + j * group
                out_ref[j, part, :, lanes] = applied[row : row + group]


def place_kernel(got, out_ref, held, sems):
    bins, parts, group, voxels = got.shape
    size = group * bins
    rows = lax.broadcasted_iota(jnp.int32, (size, size), 0)
    cols = lax.broadcasted_iota(jnp.int32, (size, size), 1)
    turn = jnp.where(cols == (rows % bins) * group + rows // bins, 1.0, 0.0).astype(BF16)
    copies = [
        pltpu.make_async_copy(held.at[part], out_ref.at[:, part], sems.at[part]) for part in range(parts)
    ]
    for part in range(parts):
        moved = jnp.dot(turn, got[:, part].reshape(size, voxels), preferred_element_type=F32).astype(BF16)
        held[part] = moved.reshape(group, bins, voxels)
        copies[part].start()
    for copy in copies:
        copy.wait()


def shards(rf_data, elem_pos, vox_pos, subbands):
    parts, bins, group, width = rf_data.shape
    channels = elem_pos.shape[1]
    chans = channels // width
    voxels = vox_pos.shape[1] // CORES
    frames = group * bins * CORES
    half = frames // CORES

    def shape(*dims, dtype=BF16):
        return jax.ShapeDtypeStruct(dims, dtype)

    def swap(x):
        return lax.ppermute(x, "core", [(0, 1), (1, 0)])

    def across(x, bits):
        return lax.ppermute(x, "chan", [(a, a ^ bits) for a in range(chans)])

    def in_hbm(x):
        return pltpu.with_memory_space_constraint(x, pltpu.HBM)

    by_bin, lhs, rhs, wave = pl.pallas_call(
        spread_kernel,
        name="spread",
        out_shape=(
            shape(chans * bins, parts, group, width),
            shape(channels, 8),
            shape(2, 8, voxels),
            shape(2, voxels, dtype=F32),
        ),
        in_specs=[HBM] * 4,
        out_specs=(HBM, VMEM, VMEM, VMEM),
        scratch_shapes=[
            pltpu.VMEM(rf_data.shape, BF16),
            pltpu.VMEM((bins, parts, group, width), BF16),
            pltpu.VMEM(elem_pos.shape, jnp.int32),
            pltpu.VMEM(vox_pos.shape, jnp.int32),
            pltpu.SMEM(subbands.shape, jnp.int32),
            pltpu.SemaphoreType.DMA((chans + 4,)),
        ],
        compiler_params=WIDE,
    )(in_hbm(rf_data), in_hbm(elem_pos), in_hbm(vox_pos), in_hbm(subbands))
    own = lax.all_to_all(by_bin, ("chan", "bin"), split_axis=0, concat_axis=0, tiled=True)

    share = voxels // 2
    upper, lower = pl.pallas_call(
        operator_kernel,
        name="operator",
        out_shape=(shape(2, channels, share), pltpu.HBM((2, channels, voxels - share), BF16)),
        in_specs=[VMEM, VMEM, VMEM],
        out_specs=(VMEM, HBM),
        scratch_shapes=[
            pltpu.VMEM((2, channels, voxels - share), BF16),
            pltpu.SemaphoreType.DMA,
        ],
        compiler_params=WIDE,
        cost_estimate=pl.CostEstimate(
            flops=60 * channels * voxels,
            transcendentals=channels * voxels,
            bytes_accessed=4 * channels * voxels,
        ),
    )(lhs, rhs, wave)

    own, upper, lower = lax.optimization_barrier((own, upper, lower))
    other = swap(own)
    own = own.reshape(chans, bins, parts, group, width)
    other = other.reshape(chans, bins, parts, group, width)

    beam_cost = pl.CostEstimate(
        flops=8 * half * channels * voxels * 2, transcendentals=0, bytes_accessed=4 * channels * voxels
    )
    mine, lower = pl.pallas_call(
        own_kernel,
        name="beam_own",
        out_shape=(shape(frames, voxels), shape(2, channels, voxels - share)),
        in_specs=[VMEM, HBM, VMEM],
        out_specs=(VMEM, VMEM),
        scratch_shapes=[
            pltpu.VMEM((frames, channels), BF16),
            pltpu.SemaphoreType.DMA,
        ],
        compiler_params=WIDE,
        cost_estimate=beam_cost,
    )(upper, in_hbm(lower), own)
    y, keep, send = pl.pallas_call(
        other_kernel,
        name="beam_other",
        out_shape=(shape(2 * frames, voxels), shape(half, frames, dtype=F32), shape(half, frames, dtype=F32)),
        in_specs=[VMEM, VMEM, VMEM, VMEM],
        out_specs=(VMEM, VMEM, VMEM),
        scratch_shapes=[pltpu.VMEM((frames, channels), BF16), pltpu.VMEM((frames, frames), F32)],
        compiler_params=WIDE,
        cost_estimate=beam_cost,
    )(upper, lower, other, mine)

    total = keep + swap(send)
    total, y = lax.optimization_barrier((total, y))
    peer = swap(y)
    narrow = total.astype(BF16)
    total = total + sum(across(narrow, bits).astype(F32) for bits in (1, 3, 2))
    narrow = total.astype(BF16)
    far = across(narrow, 4)
    far_twin = lax.ppermute(
        narrow, ("chan", "core"), [(2 * a + c, 2 * (a ^ 4) + 1 - c) for a in range(chans) for c in range(CORES)]
    )
    twin = swap(total)

    applied = pl.pallas_call(
        filter_kernel,
        name="filter",
        out_shape=shape(bins, parts, group, CORES * voxels),
        in_specs=[VMEM] * 6,
        out_specs=VMEM,
        scratch_shapes=[pltpu.VMEM((frames, frames), F32), pltpu.VMEM((2, frames, frames), BF16)],
        compiler_params=WIDE,
    )(total, far, twin, far_twin, y, peer)

    got = lax.all_to_all(applied, "bin", split_axis=0, concat_axis=0, tiled=True)
    return pl.pallas_call(
        place_kernel,
        name="place",
        out_shape=shape(group, parts, bins, CORES * voxels),
        in_specs=[VMEM],
        out_specs=HBM,
        scratch_shapes=[
            pltpu.VMEM((parts, group, bins, CORES * voxels), BF16),
            pltpu.SemaphoreType.DMA((parts,)),
        ],
        compiler_params=WIDE,
    )(got)


def solution(mesh):
    chans = mesh.shape["chan"]
    fine = Mesh(mesh.devices.reshape(chans, BINS, CORES), ("chan", "bin", "core"))
    return jax.shard_map(
        shards,
        mesh=fine,
        in_specs=(P(None, None, ("bin", "core"), "chan"), P(), P(None, "chan"), P()),
        out_specs=P(("bin", "core"), None, None, "chan"),
        check_vma=False,
    )
```
